32 devices in a mesh: segment: 2 (over y), frame: 16 (over z, x, core).
Axes of the slice: x: 2, y: 2, z: 4, core: 2. Of those that a mesh axis runs over, the one named last changes fastest.
Arguments:
- noisy_clips: bfloat16 [4, 16, 16, 16, 512], P(None, 'frame'), may hold values from -6 to 6
- conv_first: bfloat16 [2, 9, 512, 512], P('segment', None, 'frame'), may hold values from -0.09375 to 0.09375
- conv_second: bfloat16 [2, 9, 512, 512], P('segment', None, 'frame'), may hold values from -0.09375 to 0.09375
- temporal: bfloat16 [2, 3, 512, 512], P('segment', None, 'frame'), may hold values from -0.15625 to 0.15625
Outputs:
- denoised: bfloat16 [4, 16, 16, 16, 512], P(None, 'frame', 'segment')
The draws below stay inside these ranges and needn't reach their ends.
All inputs are finite; a program needn't handle non-finite values.
Results may differ from the reference program's by a relative error of at most 0.013.
Values may be sent and summed in bfloat16 or wider, within the bound.
A program may use at most 64 MiB of HBM per device.

```python
import jax
import jax.numpy as jnp

C = 512
MAP = 16
CLIPS = 4
SECTIONS = 2
FRAMES = 16


def shard_levels(stream_key, shape, split, low, high):
    factor_of = 1.0
    for position, blocks in split:
        steps = jax.random.uniform(jax.random.fold_in(jax.random.fold_in(stream_key, 6), position), (blocks,), jnp.float32, low / len(split), high / len(split))
        factor_of = factor_of * jnp.repeat(jnp.exp(steps), shape[position] // blocks).reshape((-1,) + (1,) * (len(shape) - 1 - position))
    return factor_of


def gaussian(own_key, shape, scale, reach, shards=(), kind=jnp.bfloat16):
    array = scale * jax.random.normal(own_key, shape, jnp.float32)
    if shards:
        array = array * shard_levels(own_key, shape, shards, -0.22, 0.18)
    return jnp.clip(array, -reach, reach).astype(kind)


def setup_inputs(seed: int = 0) -> dict:
    key_list = jax.random.split(jax.random.key(seed), 5)
    return {
        "noisy_clips": gaussian(key_list[0], (CLIPS, FRAMES, MAP, MAP, C), 1.0, 6.0, ((1, 16),)),
        "conv_first": gaussian(key_list[1], (SECTIONS, 9, C, C), (9 * C) ** -0.5, 0.09375, ((0, 2), (2, 16))),
        "conv_second": gaussian(key_list[2], (SECTIONS, 9, C, C), (9 * C) ** -0.5, 0.09375, ((0, 2), (2, 16))),
        "temporal": gaussian(key_list[3], (SECTIONS, 3, C, C), (3 * C) ** -0.5, 0.15625, ((0, 2), (2, 16))),
    }


skip_scale = 0.7071067811865476


def spatial(field_in, kernel):
    extent = field_in.shape[1]
    channels = field_in.shape[3]
    padded = jnp.pad(field_in, ((0, 0), (1, 1), (1, 1), (0, 0)))
    accumulated = jnp.zeros((field_in.shape[0] * extent * extent, channels), jnp.float32)
    for row_shift in range(3):
        for col_shift in range(3):
            window = padded[:, row_shift:row_shift + extent, col_shift:col_shift + extent, :].reshape(-1, channels)
            accumulated = accumulated + jnp.dot(window, kernel[3 * row_shift + col_shift], preferred_element_type=jnp.float32)
    return accumulated.reshape(field_in.shape)


def section(entering, first_kernel, second_kernel, time_kernel):
    full_shape = entering.shape
    channels = full_shape[4]
    frame_total = full_shape[1]
    flat = entering.reshape((-1,) + full_shape[2:])
    activated = jax.nn.silu(spatial(flat, first_kernel)).astype(jnp.bfloat16)
    spatial_term = spatial(activated, second_kernel).reshape(full_shape)
    activated = activated.reshape(full_shape)
    extended = jnp.pad(activated, ((0, 0), (1, 1), (0, 0), (0, 0), (0, 0)))
    time_term = jnp.zeros(full_shape, jnp.float32)
    for offset in range(3):
        window = extended[:, offset:offset + frame_total].reshape(-1, channels)
        time_term = time_term + jnp.dot(window, time_kernel[offset], preferred_element_type=jnp.float32).reshape(full_shape)
    return (entering.astype(jnp.float32) + jax.nn.silu(spatial_term + time_term)).astype(jnp.bfloat16)


def reference(noisy_clips, conv_first, conv_second, temporal):
    sections = conv_first.shape[0]
    half_sections = sections // 2
    current = noisy_clips
    inputs_down = []
    for section_index in range(sections):
        if section_index < half_sections:
            entering = current
            inputs_down.append(current)
        else:
            partner = inputs_down[sections - 1 - section_index]
            entering = ((current.astype(jnp.float32) + partner.astype(jnp.float32)) * skip_scale).astype(jnp.bfloat16)
        current = section(entering, conv_first[section_index], conv_second[section_index], temporal[section_index])
    return current
```

```python
import functools

import jax
import jax.numpy as jnp
from jax import lax
from jax.experimental import pallas as pl
from jax.experimental.pallas import tpu as pltpu
from jax.sharding import PartitionSpec as P

skip_scale = 0.7071067811865476
MESH = pl.DeviceIdType.MESH


def passed_along(shard, axis, by):
    length = lax.axis_size(axis)
    pairs = [(i, i + by) for i in range(length) if 0 <= i + by < length]
    return lax.ppermute(shard, axis, pairs)


def extended_2(cells, sides, width):
    for axis, dim in sides:
        count = lax.axis_size(axis)
        ends = count - 1
        head = lax.slice_in_dim(cells, 0, width, axis=dim)
        tail = lax.slice_in_dim(cells, cells.shape[dim] - width, cells.shape[dim], axis=dim)
        cells = jnp.concatenate(
            [
                lax.ppermute(tail, axis, [(i, (i + 1) % count) for i in range(ends)]),
                cells,
                lax.ppermute(head, axis, [((i + 1) % count, i) for i in range(ends)]),
            ],
            axis=dim,
        )
    return cells


def broadcast(shard, axis, root):
    mine = lax.axis_index(axis) == root
    return lax.psum(jnp.where(mine, shard, jnp.zeros_like(shard)), axis)


def spatial(field_in, kernel):
    extent = field_in.shape[1]
    channels = field_in.shape[3]
    padded = jnp.pad(field_in, ((0, 0), (1, 1), (1, 1), (0, 0)))
    accumulated = jnp.zeros((field_in.shape[0] * extent * extent, channels), jnp.float32)
    for row_shift in range(3):
        for col_shift in range(3):
            window = padded[
                :, row_shift : row_shift + extent, col_shift : col_shift + extent, :
            ].reshape(-1, channels)
            accumulated = accumulated + jnp.dot(
                window, kernel[3 * row_shift + col_shift], preferred_element_type=jnp.float32
            )
    return accumulated.reshape(field_in.shape)


def temporal_mix(extended, kernel, frame_local):
    channels = extended.shape[3]
    out_shape = (frame_local,) + extended.shape[1:]
    accumulated = jnp.zeros(out_shape, jnp.float32)
    for offset in range(3):
        window = extended[offset : offset + frame_local].reshape(-1, channels)
        accumulated = accumulated + jnp.dot(
            window, kernel[offset], preferred_element_type=jnp.float32
        ).reshape(out_shape)
    return accumulated


def pipelined(noisy_clips, conv_first, conv_second, temporal):
    sections = lax.axis_size("segment")
    segment_id = lax.axis_index("segment")
    first_full, second_full, time_full = (
        lax.all_gather(conv_first, "frame", axis=2, tiled=True),
        lax.all_gather(conv_second, "frame", axis=2, tiled=True),
        lax.all_gather(temporal, "frame", axis=2, tiled=True),
    )
    first_kernel = first_full[0]
    second_kernel = second_full[0]
    time_kernel = time_full[0]
    clip_count = noisy_clips.shape[0]
    frame_local = noisy_clips.shape[1]
    side_len = noisy_clips.shape[2]
    block_shape = noisy_clips.shape[1:]
    tick_count = clip_count + sections - 1
    half_sections = sections // 2
    is_up = segment_id >= half_sections
    store_depth = max(half_sections - 1, 1)
    side_store = jnp.zeros((store_depth,) + block_shape, jnp.bfloat16)
    out_store = jnp.zeros(noisy_clips.shape, jnp.bfloat16)
    prev_out = jnp.zeros(block_shape, jnp.bfloat16)

    def tick_step(carry, tick_index):
        prev_out, side_store, out_store = carry
        clip_now = tick_index - segment_id
        active = (clip_now >= 0) & (clip_now < clip_count)
        clip_slot = jnp.clip(clip_now, 0, clip_count - 1)
        own_input = lax.dynamic_index_in_dim(noisy_clips, clip_slot, 0, keepdims=False)
        received, side_store = passed_along((prev_out, side_store), "segment", 1)
        entering = jnp.where(segment_id == 0, own_input, received)
        written = (jnp.arange(store_depth) == segment_id - 1) & (segment_id < half_sections)
        side_store = jnp.where(written[:, None, None, None, None], entering[None], side_store)
        stack_slot = jnp.clip(sections - 2 - segment_id, 0, store_depth - 1)
        stored = lax.dynamic_index_in_dim(side_store, stack_slot, 0, keepdims=False)
        skip_feature = jnp.where(segment_id == sections - 1, own_input, stored)
        joined = (
            (entering.astype(jnp.float32) + skip_feature.astype(jnp.float32)) * skip_scale
        ).astype(jnp.bfloat16)
        section_in = jnp.where(is_up, joined, entering)
        activated = lax.cond(
            active,
            lambda: jax.nn.silu(spatial(section_in, first_kernel)).astype(jnp.bfloat16),
            lambda: jnp.zeros(block_shape, jnp.bfloat16),
        )
        extended = extended_2(activated, (("frame", 0),), 1)

        def second_pass():
            branch_sum = spatial(activated, second_kernel) + temporal_mix(
                extended, time_kernel, frame_local
            )
            return (section_in.astype(jnp.float32) + jax.nn.silu(branch_sum)).astype(jnp.bfloat16)

        section_out = lax.cond(active, second_pass, lambda: jnp.zeros(block_shape, jnp.bfloat16))
        finished = (jnp.arange(clip_count) == clip_slot) & active & (segment_id == sections - 1)
        out_store = jnp.where(finished[:, None, None, None, None], section_out[None], out_store)
        return ((section_out, side_store, out_store), None)

    final_carry, unused = lax.scan(
        tick_step, (prev_out, side_store, out_store), jnp.arange(tick_count, dtype=jnp.int32)
    )
    delivered = broadcast(final_carry[2], "segment", sections - 1)
    slab_rows = side_len // sections
    return lax.dynamic_slice_in_dim(delivered, segment_id * slab_rows, slab_rows, 2)


def fused_kernel(
    frames,
    noisy_ref,
    first_ref,
    second_ref,
    time_ref,
    out_ref,
    w_ref,
    xe,
    xa,
    a_send,
    a_recv,
    t_send,
    t_recv,
    e_mine,
    e_recv,
    acc_ref,
    o_full,
    local_sem,
    y_sem,
    got_sem,
    sent_sem,
    a_sem,
    t_sem,
    e_sem,
    o_sem,
):
    clips, side, lanes = noisy_ref.shape[0], noisy_ref.shape[2], noisy_ref.shape[4]
    half = lanes // 2
    cells = side * side
    depth = first_ref.shape[2]
    width = time_ref.shape[1]
    rows_per_conv = first_ref.shape[1] // width
    per_section = 2 * rows_per_conv + 1
    taps = per_section * width
    groups = 2 * per_section
    line = frames // 4
    seg = lax.axis_index("segment")
    me = lax.axis_index("frame")
    core, x_at, z_at = lax.rem(me, 2), lax.rem(me // 2, 2), me // 4
    peer = 1 - seg
    other = me + 1 - 2 * core
    slab_rows = side // 2

    def frame_of(x_place, z_place):
        return (z_place * 2 + x_place) * 2 + core

    x_peer = frame_of(1 - x_at, z_at)
    z_pair = z_at + 1 - 2 * lax.rem(z_at, 2)
    z_half = z_at // 2
    far = []
    for k in range(1, line // 2):
        part = lax.rem(z_half + k, line // 2)
        far += [2 * part, 2 * part + 1]
    after, before = lax.rem(me + 1, frames), lax.rem(me + frames - 1, frames)

    barrier = pltpu.get_barrier_semaphore()
    pl.semaphore_signal(barrier, inc=1, device_id=(peer, me), device_id_type=MESH)
    near = [other, x_peer, after, before] + [frame_of(x_at, z) for z in far + [z_pair]]
    for target in near:
        pl.semaphore_signal(barrier, inc=1, device_id=(seg, target), device_id_type=MESH)

    def columns(which):
        return pl.ds(pl.multiple_of(which * half, half), half)

    def rows_of(owner):
        return pl.ds(pl.multiple_of(owner * depth, depth), depth)

    def part(j):
        if j < rows_per_conv:
            return first_ref, j * width
        if j == rows_per_conv:
            return time_ref, 0
        return second_ref, (j - rows_per_conv - 1) * width

    def local_copy(j):
        ref, start = part(j)
        return pltpu.make_async_copy(
            ref.at[0, pl.ds(start, width), :, columns(seg)],
            w_ref.at[pl.ds(seg * taps + j * width, width), rows_of(me)],
            local_sem.at[j],
        )

    def remote(src, dst, send, recv, device):
        return pltpu.make_async_remote_copy(
            src_ref=src,
            dst_ref=dst,
            send_sem=send,
            recv_sem=recv,
            device_id=device,
            device_id_type=MESH,
        )

    def take(ref, sem):
        pltpu.make_async_copy(ref, ref, sem).wait()

    def y_copy(j):
        ref, start = part(j)
        return remote(
            ref.at[0, pl.ds(start, width), :, columns(peer)],
            w_ref.at[pl.ds(seg * taps + j * width, width), rows_of(me)],
            y_sem.at[per_section],
            y_sem.at[j],
            (peer, me),
        )

    def slab(g, owner):
        return w_ref.at[pl.ds(g * width, width), rows_of(owner)]

    def some(g, count):
        return w_ref.at[pl.ds(g * width, width), pl.ds(0, count * depth)]

    own, crossed, lined, rest = 0, 1, 2, 3

    def give(g, owner, kind, link, target):
        ref = slab(g, owner)
        remote(ref, ref, sent_sem.at[link], got_sem.at[kind, g], (seg, target)).start()

    def give_core(g, owner):
        give(g, owner, own, 2, other)

    def round_own(g):
        section, j = g // per_section, lax.rem(g, per_section)

        @pl.when(seg == section)
        def _():
            take(slab(g, me), local_sem.at[j])

        @pl.when(seg != section)
        def _():
            take(slab(g, me), y_sem.at[j])

        give(g, me, crossed, 0, x_peer)
        for z in far:
            give(g, me, lined, 1, frame_of(x_at, z))
        give(g, me, rest, 1, frame_of(x_at, z_pair))
        give_core(g, me)

    def round_cross(g):
        take(some(g, 1), got_sem.at[crossed, g])
        give(g, x_peer, rest, 1, frame_of(x_at, z_pair))
        give_core(g, x_peer)

    def round_line(g):
        take(some(g, len(far)), got_sem.at[lined, g])
        for z in far:
            give(g, frame_of(x_at, z), rest, 0, x_peer)
        for z in far:
            give_core(g, frame_of(x_at, z))

    def round_rest(g):
        take(some(g, len(far) + 2), got_sem.at[rest, g])
        give_core(g, frame_of(x_at, z_pair))
        give_core(g, frame_of(1 - x_at, z_pair))
        for z in far:
            give_core(g, frame_of(1 - x_at, z))

    def round_done(g):
        take(some(g, 2 * line), got_sem.at[own, g])

    def build(x, clip, value, where):
        width_of = value.shape[1]
        wide = value.astype(jnp.float32)
        place = lax.broadcasted_iota(jnp.int32, (cells, width_of), 0) % side
        shifted = (
            jnp.where(place == 0, 0.0, pltpu.roll(wide, 1, 0)).astype(jnp.bfloat16),
            value,
            jnp.where(place == side - 1, 0.0, pltpu.roll(wide, cells - 1, 0)).astype(jnp.bfloat16),
        )
        for dx in range(3):
            x[dx, clip, 1 : side + 1, :, where] = shifted[dx].reshape(side, side, width_of)

    def row_sum(x, clip, dy, base):
        total = None
        for dx in range(3):
            view = x[dx, clip, dy : dy + side].reshape(cells, lanes)
            term = jnp.dot(view, w_ref[base + dx], preferred_element_type=jnp.float32)
            total = term if total is None else total + term
        return total

    def silu(u):
        return u / (1.0 + jnp.exp(-u))

    def a_copy(s, clip):
        return remote(
            a_send.at[s, clip], a_recv.at[s, clip], a_sem.at[2, 0], a_sem.at[s, clip], (peer, me)
        )

    def e_copy(clip):
        return remote(e_mine.at[clip], e_recv.at[clip], e_sem.at[1, 0], e_sem.at[0, clip], (peer, me))

    def t_copy(s, way, clip):
        target = after if way == 0 else before
        return remote(
            t_send.at[way, s, clip],
            t_recv.at[way, s, clip],
            t_sem.at[way, 2, 0],
            t_sem.at[way, s, clip],
            (seg, target),
        )

    def o_copy(clip):
        return remote(
            o_full.at[clip, pl.ds(peer * slab_rows, slab_rows)],
            out_ref.at[clip, 0, :, :, columns(seg)],
            o_sem.at[1, 0],
            o_sem.at[0, clip],
            (peer, me),
        )

    def first_row(s, dy):
        def work(clip):
            term = row_sum(xe, clip, dy, s * taps + dy * width)
            acc_ref[clip] = term if dy == 0 else acc_ref[clip] + term

        return work

    def send_active(s):
        def work(clip):
            a_send[s, clip] = silu(acc_ref[clip]).astype(jnp.bfloat16)
            a_copy(s, clip).start()

        return work

    def take_active(s):
        def work(clip):
            a_copy(s, clip).wait_recv()
            build(xa, clip, a_send[s, clip], columns(seg))
            build(xa, clip, a_recv[s, clip], columns(peer))

        return work

    sends_on = (me < frames - 1, me > 0)
    takes_on = (me > 0, me < frames - 1)

    def terms(s):
        def work(clip):
            base = s * taps + rows_per_conv * width
            view = xa[1, clip, 1 : side + 1].reshape(cells, lanes)

            def mixed(k):
                return jnp.dot(view, w_ref[base + k], preferred_element_type=jnp.float32)

            for way, k in ((0, 0), (1, 2)):
                t_send[way, s, clip] = mixed(k).astype(jnp.bfloat16)

                @pl.when(sends_on[way])
                def _():
                    t_copy(s, way, clip).start()

            acc_ref[clip] = mixed(1)

        return work

    def second_row(s, dy):
        def work(clip):
            base = s * taps + (rows_per_conv + 1 + dy) * width
            acc_ref[clip] = acc_ref[clip] + row_sum(xa, clip, dy, base)

        return work

    def finished(s, clip):
        for way in range(2):

            @pl.when(takes_on[way])
            def _():
                t_copy(s, way, clip).wait_recv()
                acc_ref[clip] = acc_ref[clip] + t_recv[way, s, clip].astype(jnp.float32)

        return silu(acc_ref[clip])

    def end_first(clip):
        mine = noisy_ref[clip, 0, :, :, columns(seg)].reshape(cells, half).astype(jnp.float32)
        out = (mine + finished(0, clip)).astype(jnp.bfloat16)
        e_mine[clip] = ((out.astype(jnp.float32) + mine) * skip_scale).astype(jnp.bfloat16)
        e_copy(clip).start()

    def take_entering(clip):
        e_copy(clip).wait_recv()
        build(xe, clip, e_mine[clip], columns(seg))
        build(xe, clip, e_recv[clip], columns(peer))

    def end_second(clip):
        out = (e_mine[clip].astype(jnp.float32) + finished(1, clip)).astype(jnp.bfloat16)
        o_full[clip] = out.reshape(side, side, half)
        o_copy(clip).start()
        out_ref[clip, 0, :, :, columns(seg)] = o_full[clip, pl.ds(seg * slab_rows, slab_rows)]

    for j in range(per_section):
        local_copy(j).start()

    edge = jnp.zeros((side, lanes), jnp.bfloat16)
    for x in (xe, xa):
        for dx in range(3):

            @pl.loop(0, clips)
            def _(clip):
                x[dx, clip, 0] = edge
                x[dx, clip, side + 1] = edge

    @pl.loop(0, clips)
    def _(clip):
        build(xe, clip, noisy_ref[clip, 0].reshape(cells, lanes), slice(None))

    pl.semaphore_wait(barrier, len(near) + 1)

    for j in range(per_section):
        y_copy(j).start()

    beat = clips
    rounds = (
        (0, round_own),
        (3, round_cross),
        (5, round_line),
        (9, round_rest),
        (11, round_done),
    )

    def ready(g):
        return beat * g + rounds[-1][0]

    steps = (
        ((0, 1, ((0, 1), (0, 1), (0, 1))), (25, 3), (((27, 3), (31, 2), (36, 1)), (38, 1))),
        ((43, 3, ((43, 3), (44, 3), (47, 2))), (52, 3), (((56, 2), (60, 1), (63, 1)), (64, 1))),
    )
    plan = []
    for s in range(2):
        first, mixed_at, second = steps[s]
        base = per_section * s
        if s == 1:
            plan.append((first[0], first[1], take_entering))
        for dy, (offset, stride) in enumerate(first[2]):
            plan.append((max(offset, ready(base + dy)), stride, first_row(s, dy)))
        plan.append((plan[-1][0], plan[-1][1], send_active(s)))
        plan.append((mixed_at[0], mixed_at[1], take_active(s)))
        plan.append((max(mixed_at[0], ready(base + 3)), mixed_at[1], terms(s)))
        for dy, (offset, stride) in enumerate(second[0]):
            plan.append((max(offset, ready(base + 4 + dy)), stride, second_row(s, dy)))
        plan.append((second[1][0], second[1][1], end_first if s == 0 else end_second))
    last = max(offset + stride * (clips - 1) + 1 for offset, stride, _ in plan)

    @pl.loop(0, last)
    def _(step):
        for lag, work in reversed(rounds):
            at = step - lag

            @pl.when((at >= 0) & (lax.rem(at, beat) == 0) & (at < beat * groups))
            def _():
                work(at // beat)

        for offset, stride, work in plan:
            at = step - offset

            @pl.when((at >= 0) & (lax.rem(at, stride) == 0) & (at < stride * clips))
            def _():
                work(at // stride)

    @pl.loop(0, clips)
    def _(clip):
        o_copy(clip).wait_recv()

    take(o_full.at[:, pl.ds(0, slab_rows)], o_sem.at[1, 0])
    take(e_mine, e_sem.at[1, 0])
    take(a_send, a_sem.at[2, 0])
    for way in range(2):

        @pl.when(sends_on[way])
        def _():
            take(t_send.at[way], t_sem.at[way, 2, 0])

    take(w_ref.at[pl.ds(0, taps), pl.ds(0, depth)], y_sem.at[per_section])
    for link, count in enumerate((line - 1, line, 2 * line)):
        take(w_ref.at[:, pl.ds(0, count * depth)], sent_sem.at[link])


def on_device(noisy_clips, conv_first, conv_second, temporal):
    sections = lax.axis_size("segment")
    frames = lax.axis_size("frame")
    clips, frame_local, side, _, lanes = noisy_clips.shape
    half = lanes // 2
    cells = side * side
    if sections != 2 or half % 128 or frames % 8 or frames < 16 or frame_local != 1 or side % 16:
        return pipelined(noisy_clips, conv_first, conv_second, temporal)
    taps = conv_first.shape[1] + temporal.shape[1] + conv_second.shape[1]
    per_section = taps // temporal.shape[1]
    dma = pltpu.SemaphoreType.DMA
    vmem = pl.BlockSpec(memory_space=pltpu.VMEM)
    kind = jnp.bfloat16
    return pl.pallas_call(
        functools.partial(fused_kernel, frames),
        out_shape=jax.ShapeDtypeStruct((clips, 1, side // 2, side, lanes), kind),
        in_specs=[vmem] + [pl.BlockSpec(memory_space=pl.ANY)] * 3,
        out_specs=vmem,
        scratch_shapes=[
            pltpu.VMEM((2 * taps, lanes, half), kind),
            pltpu.VMEM((3, clips, side + 2, side, lanes), kind),
            pltpu.VMEM((3, clips, side + 2, side, lanes), kind),
            pltpu.VMEM((2, clips, cells, half), kind),
            pltpu.VMEM((2, clips, cells, half), kind),
            pltpu.VMEM((2, 2, clips, cells, half), kind),
            pltpu.VMEM((2, 2, clips, cells, half), kind),
            pltpu.VMEM((clips, cells, half), kind),
            pltpu.VMEM((clips, cells, half), kind),
            pltpu.VMEM((clips, cells, half), jnp.float32),
            pltpu.VMEM((clips, side, side, half), kind),
            dma((per_section,)),
            dma((per_section + 1,)),
            dma((4, 2 * per_section)),
            dma((3,)),
            dma((3, clips)),
            dma((2, 3, clips)),
            dma((2, clips)),
            dma((2, clips)),
        ],
        compiler_params=pltpu.CompilerParams(
            collective_id=0, has_side_effects=True, vmem_limit_bytes=58 * 1024 * 1024
        ),
    )(noisy_clips, conv_first, conv_second, temporal)


def solution(mesh):
    in_specs = (
        P(None, "frame", None, None, None),
        P("segment", None, "frame", None),
        P("segment", None, "frame", None),
        P("segment", None, "frame", None),
    )
    out_specs = P(None, "frame", "segment", None, None)
    return jax.shard_map(
        on_device, mesh=mesh, in_specs=in_specs, out_specs=out_specs, check_vma=False
    )
```

```python
import functools

import jax
import jax.numpy as jnp
from jax import lax
from jax.experimental import pallas as pl
from jax.experimental.pallas import tpu as pltpu
from jax.sharding import PartitionSpec as P

skip_scale = 0.7071067811865476
MESH = pl.DeviceIdType.MESH


def passed_along(shard, axis, by):
    length = lax.axis_size(axis)
    pairs = [(i, i + by) for i in range(length) if 0 <= i + by < length]
    return lax.ppermute(shard, axis, pairs)


def extended_2(cells, sides, width):
    for axis, dim in sides:
        count = lax.axis_size(axis)
        ends = count - 1
        head = lax.slice_in_dim(cells, 0, width, axis=dim)
        tail = lax.slice_in_dim(cells, cells.shape[dim] - width, cells.shape[dim], axis=dim)
        cells = jnp.concatenate(
            [
                lax.ppermute(tail, axis, [(i, (i + 1) % count) for i in range(ends)]),
                cells,
                lax.ppermute(head, axis, [((i + 1) % count, i) for i in range(ends)]),
            ],
            axis=dim,
        )
    return cells


def broadcast(shard, axis, root):
    mine = lax.axis_index(axis) == root
    return lax.psum(jnp.where(mine, shard, jnp.zeros_like(shard)), axis)


def spatial(field_in, kernel):
    extent = field_in.shape[1]
    channels = field_in.shape[3]
    padded = jnp.pad(field_in, ((0, 0), (1, 1), (1, 1), (0, 0)))
    accumulated = jnp.zeros((field_in.shape[0] * extent * extent, channels), jnp.float32)
    for row_shift in range(3):
        for col_shift in range(3):
            window = padded[
                :, row_shift : row_shift + extent, col_shift : col_shift + extent, :
            ].reshape(-1, channels)
            accumulated = accumulated + jnp.dot(
                window, kernel[3 * row_shift + col_shift], preferred_element_type=jnp.float32
            )
    return accumulated.reshape(field_in.shape)


def temporal_mix(extended, kernel, frame_local):
    channels = extended.shape[3]
    out_shape = (frame_local,) + extended.shape[1:]
    accumulated = jnp.zeros(out_shape, jnp.float32)
    for offset in range(3):
        window = extended[offset : offset + frame_local].reshape(-1, channels)
        accumulated = accumulated + jnp.dot(
            window, kernel[offset], preferred_element_type=jnp.float32
        ).reshape(out_shape)
    return accumulated


def pipelined(noisy_clips, conv_first, conv_second, temporal):
    sections = lax.axis_size("segment")
    segment_id = lax.axis_index("segment")
    first_full, second_full, time_full = (
        lax.all_gather(conv_first, "frame", axis=2, tiled=True),
        lax.all_gather(conv_second, "frame", axis=2, tiled=True),
        lax.all_gather(temporal, "frame", axis=2, tiled=True),
    )
    first_kernel = first_full[0]
    second_kernel = second_full[0]
    time_kernel = time_full[0]
    clip_count = noisy_clips.shape[0]
    frame_local = noisy_clips.shape[1]
    side_len = noisy_clips.shape[2]
    block_shape = noisy_clips.shape[1:]
    tick_count = clip_count + sections - 1
    half_sections = sections // 2
    is_up = segment_id >= half_sections
    store_depth = max(half_sections - 1, 1)
    side_store = jnp.zeros((store_depth,) + block_shape, jnp.bfloat16)
    out_store = jnp.zeros(noisy_clips.shape, jnp.bfloat16)
    prev_out = jnp.zeros(block_shape, jnp.bfloat16)

    def tick_step(carry, tick_index):
        prev_out, side_store, out_store = carry
        clip_now = tick_index - segment_id
        active = (clip_now >= 0) & (clip_now < clip_count)
        clip_slot = jnp.clip(clip_now, 0, clip_count - 1)
        own_input = lax.dynamic_index_in_dim(noisy_clips, clip_slot, 0, keepdims=False)
        received, side_store = passed_along((prev_out, side_store), "segment", 1)
        entering = jnp.where(segment_id == 0, own_input, received)
        written = (jnp.arange(store_depth) == segment_id - 1) & (segment_id < half_sections)
        side_store = jnp.where(written[:, None, None, None, None], entering[None], side_store)
        stack_slot = jnp.clip(sections - 2 - segment_id, 0, store_depth - 1)
        stored = lax.dynamic_index_in_dim(side_store, stack_slot, 0, keepdims=False)
        skip_feature = jnp.where(segment_id == sections - 1, own_input, stored)
        joined = (
            (entering.astype(jnp.float32) + skip_feature.astype(jnp.float32)) * skip_scale
        ).astype(jnp.bfloat16)
        section_in = jnp.where(is_up, joined, entering)
        activated = lax.cond(
            active,
            lambda: jax.nn.silu(spatial(section_in, first_kernel)).astype(jnp.bfloat16),
            lambda: jnp.zeros(block_shape, jnp.bfloat16),
        )
        extended = extended_2(activated, (("frame", 0),), 1)

        def second_pass():
            branch_sum = spatial(activated, second_kernel) + temporal_mix(
                extended, time_kernel, frame_local
            )
            return (section_in.astype(jnp.float32) + jax.nn.silu(branch_sum)).astype(jnp.bfloat16)

        section_out = lax.cond(active, second_pass, lambda: jnp.zeros(block_shape, jnp.bfloat16))
        finished = (jnp.arange(clip_count) == clip_slot) & active & (segment_id == sections - 1)
        out_store = jnp.where(finished[:, None, None, None, None], section_out[None], out_store)
        return ((section_out, side_store, out_store), None)

    final_carry, unused = lax.scan(
        tick_step, (prev_out, side_store, out_store), jnp.arange(tick_count, dtype=jnp.int32)
    )
    delivered = broadcast(final_carry[2], "segment", sections - 1)
    slab_rows = side_len // sections
    return lax.dynamic_slice_in_dim(delivered, segment_id * slab_rows, slab_rows, 2)


def fused_kernel(
    frames,
    noisy_ref,
    first_ref,
    second_ref,
    time_ref,
    out_ref,
    w_ref,
    n_ref,
    xe,
    xa,
    a_send,
    a_recv,
    t_send,
    t_recv,
    e_mine,
    e_recv,
    acc_ref,
    o_full,
    local_sem,
    n_sem,
    y_sem,
    got_sem,
    sent_sem,
    a_sem,
    t_sem,
    e_sem,
    o_sem,
):
    clips, side, lanes = noisy_ref.shape[0], noisy_ref.shape[2], noisy_ref.shape[4]
    half = lanes // 2
    cells = side * side
    depth = first_ref.shape[2]
    width = time_ref.shape[1]
    rows_per_conv = first_ref.shape[1] // width
    per_section = 2 * rows_per_conv + 1
    taps = per_section * width
    groups = 2 * per_section
    line = frames // 4
    seg = lax.axis_index("segment")
    me = lax.axis_index("frame")
    slots = frames // line
    core, x_at, z_at, place = lax.rem(me, 2), lax.rem(me // 2, 2), me // slots, lax.rem(me, slots)
    peer = 1 - seg
    other = me + 1 - 2 * core
    slab_rows = side // 2

    def frame_of(x_place, z_place):
        return (z_place * 2 + x_place) * 2 + core

    x_peer = frame_of(1 - x_at, z_at)
    z_pair = z_at + 1 - 2 * lax.rem(z_at, 2)
    z_half = z_at // 2
    far = []
    for k in range(1, line // 2):
        part = lax.rem(z_half + k, line // 2)
        far += [2 * part, 2 * part + 1]
    across = (x_peer, x_peer + 1 - 2 * core)

    barrier = pltpu.get_barrier_semaphore()
    near = [(seg, other)] + [(seg, f) for f in across]
    near += [(seg, frame_of(x_at, z)) for z in far + [z_pair]]
    near += [(peer, f) for f in (me, other) + across]
    for target in near:
        pl.semaphore_signal(barrier, inc=1, device_id=target, device_id_type=MESH)

    def columns(which):
        return pl.ds(pl.multiple_of(which * half, half), half)

    def rows_of(owner):
        return pl.ds(pl.multiple_of(owner * depth, depth), depth)

    def part(j):
        if j < rows_per_conv:
            return first_ref, j * width
        if j == rows_per_conv:
            return time_ref, 0
        return second_ref, (j - rows_per_conv - 1) * width

    def local_copy(j):
        ref, start = part(j)
        return pltpu.make_async_copy(
            ref.at[0, pl.ds(start, width), :, columns(seg)],
            w_ref.at[pl.ds(seg * taps + j * width, width), rows_of(me)],
            local_sem.at[j],
        )

    def remote(src, dst, send, recv, device):
        return pltpu.make_async_remote_copy(
            src_ref=src,
            dst_ref=dst,
            send_sem=send,
            recv_sem=recv,
            device_id=device,
            device_id_type=MESH,
        )

    def take(ref, sem):
        pltpu.make_async_copy(ref, ref, sem).wait()

    def y_copy(j):
        ref, start = part(j)
        return remote(
            ref.at[0, pl.ds(start, width), :, columns(peer)],
            w_ref.at[pl.ds(seg * taps + j * width, width), rows_of(me)],
            y_sem.at[per_section],
            y_sem.at[j],
            (peer, me),
        )

    def slab(g, owner):
        return w_ref.at[pl.ds(g * width, width), rows_of(owner)]

    def some(g, count):
        return w_ref.at[pl.ds(g * width, width), pl.ds(0, count * depth)]

    own, crossed, lined, rest = 0, 1, 2, 3

    def give(g, owner, kind, link, target):
        ref = slab(g, owner)
        remote(ref, ref, sent_sem.at[link], got_sem.at[kind, g], (seg, target)).start()

    def give_core(g, owner):
        give(g, owner, own, 2, other)

    def round_own(g):
        section, j = g // per_section, lax.rem(g, per_section)

        @pl.when(seg == section)
        def _():
            take(slab(g, me), local_sem.at[j])

        @pl.when(seg != section)
        def _():
            take(slab(g, me), y_sem.at[j])

        give(g, me, crossed, 0, x_peer)
        for z in far:
            give(g, me, lined, 1, frame_of(x_at, z))
        give(g, me, rest, 1, frame_of(x_at, z_pair))
        give_core(g, me)

    def round_cross(g):
        take(some(g, 1), got_sem.at[crossed, g])
        give(g, x_peer, rest, 1, frame_of(x_at, z_pair))
        give_core(g, x_peer)

    def round_line(g):
        take(some(g, len(far)), got_sem.at[lined, g])
        for z in far:
            give(g, frame_of(x_at, z), rest, 0, x_peer)
        for z in far:
            give_core(g, frame_of(x_at, z))

    def round_rest(g):
        take(some(g, len(far) + 2), got_sem.at[rest, g])
        give_core(g, frame_of(x_at, z_pair))
        give_core(g, frame_of(1 - x_at, z_pair))
        for z in far:
            give_core(g, frame_of(1 - x_at, z))

    def round_done(g):
        take(some(g, 2 * line), got_sem.at[own, g])

    def build(x, clip, value, where):
        width_of = value.shape[1]
        wide = value.astype(jnp.float32)
        place = lax.broadcasted_iota(jnp.int32, (cells, width_of), 0) % side
        shifted = (
            jnp.where(place == 0, 0.0, pltpu.roll(wide, 1, 0)).astype(jnp.bfloat16),
            value,
            jnp.where(place == side - 1, 0.0, pltpu.roll(wide, cells - 1, 0)).astype(jnp.bfloat16),
        )
        for dx in range(3):
            x[dx, clip, 1 : side + 1, :, where] = shifted[dx].reshape(side, side, width_of)

    def row_sum(x, clip, rows, base, total=None):
        for dy in rows:
            for dx in range(3):
                view = x[dx, clip, dy : dy + side].reshape(cells, lanes)
                term = jnp.dot(
                    view, w_ref[base + width * dy + dx], preferred_element_type=jnp.float32
                )
                total = term if total is None else total + term
        return total

    def silu(u):
        return u / (1.0 + jnp.exp(-u))

    def arrival(j):
        return jnp.where(j == 0, 0, jnp.where(j == 1, slots - 1, j - 1))

    def departure(j):
        there = lax.rem(place + slots // 2 * (1 - j // 2), slots)
        return jnp.where(lax.rem(j, 2) == 0, there + 1 - 2 * lax.rem(there, 2), there)

    def noisy_local():
        return pltpu.make_async_copy(noisy_ref.at[place, 0], n_ref.at[place], n_sem.at[0])

    def send_noisy(unused):
        remote(
            noisy_ref.at[lax.rem(other, slots), 0],
            n_ref.at[place],
            n_sem.at[4],
            n_sem.at[1],
            (seg, other),
        ).start()
        for target in across:
            remote(
                noisy_ref.at[lax.rem(target, slots), 0, :, :, columns(seg)],
                n_ref.at[place, :, :, columns(seg)],
                n_sem.at[4],
                n_sem.at[2],
                (seg, target),
            ).start()

    def relay_noisy(unused):
        take(n_ref.at[0], n_sem.at[2])
        for target in across:
            ref = n_ref.at[lax.rem(target, slots), :, :, columns(seg)]
            remote(ref, ref, n_sem.at[4], n_sem.at[3], (peer, me)).start()

    def take_noisy(unused):
        for i in (0, 1, 3):
            take(n_ref.at[0], n_sem.at[i])

    def build_noisy(j):
        slot = arrival(j)
        build(xe, slot, n_ref[slot].reshape(cells, lanes), slice(None))

    def a_copy(s, slot):
        return remote(
            a_send.at[s, slot], a_recv.at[s, slot], a_sem.at[2, 0], a_sem.at[s, slot], (peer, me)
        )

    def e_copy(slot):
        return remote(e_mine.at[slot], e_recv.at[slot], e_sem.at[1, 0], e_sem.at[0, slot], (peer, me))

    sends_on = (z_at < line - 1, z_at > 0)
    takes_on = (z_at > 0, z_at < line - 1)

    def t_copy(s, way):
        target = me + slots if way == 0 else me - slots
        return remote(
            t_send.at[way, s],
            t_recv.at[way, s],
            t_sem.at[way, 2],
            t_sem.at[way, s],
            (seg, lax.rem(target + frames, frames)),
        )

    def o_copy(slot, rows):
        return remote(
            o_full.at[2 * slot + rows],
            out_ref.at[place, 0, :, :, columns(seg)],
            o_sem.at[1],
            o_sem.at[0],
            (rows, z_at * slots + slot),
        )

    def first_rows(s):
        def work(j):
            slot = arrival(j)
            total = row_sum(xe, slot, range(rows_per_conv), s * taps)
            a_send[s, slot] = silu(total).astype(jnp.bfloat16)
            a_copy(s, slot).start()

        return work

    def take_active(s):
        def work(j):
            slot = arrival(j)
            a_copy(s, slot).wait_recv()
            build(xa, slot + 1, a_send[s, slot], columns(seg))
            build(xa, slot + 1, a_recv[s, slot], columns(peer))

        return work

    def mixed(s, slot, k):
        view = xa[1, slot + k, 1 : side + 1].reshape(cells, lanes)
        return jnp.dot(
            view, w_ref[s * taps + rows_per_conv * width + k], preferred_element_type=jnp.float32
        )

    def terms(s):
        def work(j):
            for way, slot in ((1, 0), (0, slots - 1)):

                @pl.when((j == 1 - way) & sends_on[way])
                def _():
                    view = xa[1, slot + 1, 1 : side + 1].reshape(cells, lanes)
                    base = s * taps + rows_per_conv * width
                    t_send[way, s] = jnp.dot(
                        view, w_ref[base + 2 * way], preferred_element_type=jnp.float32
                    ).astype(jnp.bfloat16)
                    t_copy(s, way).start()

        return work

    def second_sum(s, slot, rows, with_time, total=None):
        base = s * taps + (rows_per_conv + 1) * width
        total = row_sum(xa, slot + 1, rows, base, total)
        if with_time:
            for k in range(width):
                total = total + mixed(s, slot, k)
        return total

    def early_rows(s, rows, with_time):
        def work(j):
            slot = arrival(j)
            acc_ref[slot] = second_sum(s, slot, rows, with_time)

        return work

    def finished(s, slot):
        for way, edge_slot in ((0, 0), (1, slots - 1)):

            @pl.when(takes_on[way] & (slot == edge_slot))
            def _():
                t_copy(s, way).wait_recv()
                acc_ref[slot] = acc_ref[slot] + t_recv[way, s].astype(jnp.float32)

        return silu(acc_ref[slot])

    def end_first(j):
        slot = arrival(j)
        acc_ref[slot] = second_sum(0, slot, range(rows_per_conv), True)
        mine = n_ref[slot, :, :, columns(seg)].reshape(cells, half).astype(jnp.float32)
        out = (mine + finished(0, slot)).astype(jnp.bfloat16)
        e_mine[slot] = ((out.astype(jnp.float32) + mine) * skip_scale).astype(jnp.bfloat16)
        e_copy(slot).start()

    def take_entering(j):
        slot = arrival(j)
        e_copy(slot).wait_recv()
        build(xe, slot, e_mine[slot], columns(seg))
        build(xe, slot, e_recv[slot], columns(peer))

    def end_second(rows, with_time):
        def work(j):
            slot = departure(j)
            acc_ref[slot] = second_sum(1, slot, rows, with_time, acc_ref[slot])
            out = (e_mine[slot].astype(jnp.float32) + finished(1, slot)).astype(jnp.bfloat16)
            full = out.reshape(2, slab_rows, side, half)
            for rows_at in range(2):
                o_full[2 * slot + rows_at] = full[rows_at]
            o_copy(slot, peer).start()

            @pl.when(slot != place)
            def _():
                o_copy(slot, seg).start()

            @pl.when(slot == place)
            def _():
                out_ref[place, 0, :, :, columns(seg)] = o_full[2 * slot + seg]

        return work

    for j in range(per_section):
        local_copy(j).start()

    noisy_local().start()
    edge = jnp.zeros((side, lanes), jnp.bfloat16)
    for x in (xe, xa):
        for dx in range(3):

            @pl.loop(0, x.shape[1])
            def _(slot):
                x[dx, slot, 0] = edge
                x[dx, slot, side + 1] = edge

    for slot in (0, slots + 1):
        xa[1, slot, 1 : side + 1] = jnp.zeros((side, side, lanes), jnp.bfloat16)

    pl.semaphore_wait(barrier, len(near))

    for j in range(per_section):
        y_copy(j).start()

    beat = slots
    rounds = (
        (0, round_own),
        (3, round_cross),
        (5, round_line),
        (9, round_rest),
        (11, round_done),
    )

    def ready(g):
        return beat * g + rounds[-1][0]

    every = tuple(range(rows_per_conv))
    plan = (
        (1, 1, 1, send_noisy),
        (9, 1, 1, relay_noisy),
        (14, 1, 1, take_noisy),
        (14, 1, slots, build_noisy),
        (ready(2), 1, slots, first_rows(0)),
        (25, 3, slots, take_active(0)),
        (25, 3, 2, terms(0)),
        (ready(6), 1, slots, end_first),
        (41, 3, slots, take_entering),
        (ready(9), 1, slots, first_rows(1)),
        (52, 3, slots, take_active(1)),
        (52, 3, 2, terms(1)),
        (ready(12), 1, slots, early_rows(1, every[:-1], False)),
        (ready(13), 1, slots, end_second(every[-1:], True)),
    )
    last = max(offset + stride * (count - 1) + 1 for offset, stride, count, _ in plan)

    @pl.loop(0, last)
    def _(step):
        for lag, work in reversed(rounds):
            at = step - lag

            @pl.when((at >= 0) & (lax.rem(at, beat) == 0) & (at < beat * groups))
            def _():
                work(at // beat)

        for offset, stride, count, work in plan:
            at = step - offset

            @pl.when((at >= 0) & (lax.rem(at, stride) == 0) & (at < stride * count))
            def _():
                work(at // stride)

    for i in range(2):
        take(o_full.at[pl.ds(0, 2 * slots - 1)], o_sem.at[i])
    take(n_ref.at[pl.ds(0, 3)], n_sem.at[4])
    take(e_mine, e_sem.at[1, 0])
    take(a_send, a_sem.at[2, 0])
    for way in range(2):

        @pl.when(sends_on[way])
        def _():
            take(t_send.at[way], t_sem.at[way, 2])

    take(w_ref.at[pl.ds(0, taps), pl.ds(0, depth)], y_sem.at[per_section])
    for link, count in enumerate((line - 1, line, 2 * line)):
        take(w_ref.at[:, pl.ds(0, count * depth)], sent_sem.at[link])


def on_device(noisy_clips, conv_first, conv_second, temporal):
    sections = lax.axis_size("segment")
    frames = lax.axis_size("frame")
    clips, frame_local, side, _, lanes = noisy_clips.shape
    half = lanes // 2
    cells = side * side
    if sections != 2 or half % 128 or frames % 8 or frames < 16 or clips != 4 or frame_local != 1 or side % 16:
        return pipelined(noisy_clips, conv_first, conv_second, temporal)
    taps = conv_first.shape[1] + temporal.shape[1] + conv_second.shape[1]
    per_section = taps // temporal.shape[1]
    dma = pltpu.SemaphoreType.DMA
    vmem = pl.BlockSpec(memory_space=pltpu.VMEM)
    kind = jnp.bfloat16
    return pl.pallas_call(
        functools.partial(fused_kernel, frames),
        out_shape=jax.ShapeDtypeStruct((clips, 1, side // 2, side, lanes), kind),
        in_specs=[pl.BlockSpec(memory_space=pl.ANY)] * 4,
        out_specs=vmem,
        scratch_shapes=[
            pltpu.VMEM((2 * taps, lanes, half), kind),
            pltpu.VMEM((clips, side, side, lanes), kind),
            pltpu.VMEM((3, clips, side + 2, side, lanes), kind),
            pltpu.VMEM((3, clips + 2, side + 2, side, lanes), kind),
            pltpu.VMEM((2, clips, cells, half), kind),
            pltpu.VMEM((2, clips, cells, half), kind),
            pltpu.VMEM((2, 2, cells, half), kind),
            pltpu.VMEM((2, 2, cells, half), kind),
            pltpu.VMEM((clips, cells, half), kind),
            pltpu.VMEM((clips, cells, half), kind),
            pltpu.VMEM((clips, cells, half), jnp.float32),
            pltpu.VMEM((2 * clips, side // 2, side, half), kind),
            dma((per_section,)),
            dma((5,)),
            dma((per_section + 1,)),
            dma((4, 2 * per_section)),
            dma((3,)),
            dma((3, clips)),
            dma((2, 3)),
            dma((2, clips)),
            dma((2,)),
        ],
        compiler_params=pltpu.CompilerParams(
            collective_id=0, has_side_effects=True, vmem_limit_bytes=58 * 1024 * 1024
        ),
    )(noisy_clips, conv_first, conv_second, temporal)


def solution(mesh):
    in_specs = (
        P(None, "frame", None, None, None),
        P("segment", None, "frame", None),
        P("segment", None, "frame", None),
        P("segment", None, "frame", None),
    )
    out_specs = P(None, "frame", "segment", None, None)
    return jax.shard_map(
        on_device, mesh=mesh, in_specs=in_specs, out_specs=out_specs, check_vma=False
    )
```

```python
import functools

import jax
import jax.numpy as jnp
from jax import lax
from jax.experimental import pallas as pl
from jax.experimental.pallas import tpu as pltpu
from jax.sharding import PartitionSpec as P

skip_scale = 0.7071067811865476
MESH = pl.DeviceIdType.MESH


def passed_along(shard, axis, by):
    length = lax.axis_size(axis)
    pairs = [(i, i + by) for i in range(length) if 0 <= i + by < length]
    return lax.ppermute(shard, axis, pairs)


def extended_2(cells, sides, width):
    for axis, dim in sides:
        count = lax.axis_size(axis)
        ends = count - 1
        head = lax.slice_in_dim(cells, 0, width, axis=dim)
        tail = lax.slice_in_dim(cells, cells.shape[dim] - width, cells.shape[dim], axis=dim)
        cells = jnp.concatenate(
            [
                lax.ppermute(tail, axis, [(i, (i + 1) % count) for i in range(ends)]),
                cells,
                lax.ppermute(head, axis, [((i + 1) % count, i) for i in range(ends)]),
            ],
            axis=dim,
        )
    return cells


def broadcast(shard, axis, root):
    mine = lax.axis_index(axis) == root
    return lax.psum(jnp.where(mine, shard, jnp.zeros_like(shard)), axis)


def spatial(field_in, kernel):
    extent = field_in.shape[1]
    channels = field_in.shape[3]
    padded = jnp.pad(field_in, ((0, 0), (1, 1), (1, 1), (0, 0)))
    accumulated = jnp.zeros((field_in.shape[0] * extent * extent, channels), jnp.float32)
    for row_shift in range(3):
        for col_shift in range(3):
            window = padded[
                :, row_shift : row_shift + extent, col_shift : col_shift + extent, :
            ].reshape(-1, channels)
            accumulated = accumulated + jnp.dot(
                window, kernel[3 * row_shift + col_shift], preferred_element_type=jnp.float32
            )
    return accumulated.reshape(field_in.shape)


def temporal_mix(extended, kernel, frame_local):
    channels = extended.shape[3]
    out_shape = (frame_local,) + extended.shape[1:]
    accumulated = jnp.zeros(out_shape, jnp.float32)
    for offset in range(3):
        window = extended[offset : offset + frame_local].reshape(-1, channels)
        accumulated = accumulated + jnp.dot(
            window, kernel[offset], preferred_element_type=jnp.float32
        ).reshape(out_shape)
    return accumulated


def pipelined(noisy_clips, conv_first, conv_second, temporal):
    sections = lax.axis_size("segment")
    segment_id = lax.axis_index("segment")
    first_full, second_full, time_full = (
        lax.all_gather(conv_first, "frame", axis=2, tiled=True),
        lax.all_gather(conv_second, "frame", axis=2, tiled=True),
        lax.all_gather(temporal, "frame", axis=2, tiled=True),
    )
    first_kernel = first_full[0]
    second_kernel = second_full[0]
    time_kernel = time_full[0]
    clip_count = noisy_clips.shape[0]
    frame_local = noisy_clips.shape[1]
    side_len = noisy_clips.shape[2]
    block_shape = noisy_clips.shape[1:]
    tick_count = clip_count + sections - 1
    half_sections = sections // 2
    is_up = segment_id >= half_sections
    store_depth = max(half_sections - 1, 1)
    side_store = jnp.zeros((store_depth,) + block_shape, jnp.bfloat16)
    out_store = jnp.zeros(noisy_clips.shape, jnp.bfloat16)
    prev_out = jnp.zeros(block_shape, jnp.bfloat16)

    def tick_step(carry, tick_index):
        prev_out, side_store, out_store = carry
        clip_now = tick_index - segment_id
        active = (clip_now >= 0) & (clip_now < clip_count)
        clip_slot = jnp.clip(clip_now, 0, clip_count - 1)
        own_input = lax.dynamic_index_in_dim(noisy_clips, clip_slot, 0, keepdims=False)
        received, side_store = passed_along((prev_out, side_store), "segment", 1)
        entering = jnp.where(segment_id == 0, own_input, received)
        written = (jnp.arange(store_depth) == segment_id - 1) & (segment_id < half_sections)
        side_store = jnp.where(written[:, None, None, None, None], entering[None], side_store)
        stack_slot = jnp.clip(sections - 2 - segment_id, 0, store_depth - 1)
        stored = lax.dynamic_index_in_dim(side_store, stack_slot, 0, keepdims=False)
        skip_feature = jnp.where(segment_id == sections - 1, own_input, stored)
        joined = (
            (entering.astype(jnp.float32) + skip_feature.astype(jnp.float32)) * skip_scale
        ).astype(jnp.bfloat16)
        section_in = jnp.where(is_up, joined, entering)
        activated = lax.cond(
            active,
            lambda: jax.nn.silu(spatial(section_in, first_kernel)).astype(jnp.bfloat16),
            lambda: jnp.zeros(block_shape, jnp.bfloat16),
        )
        extended = extended_2(activated, (("frame", 0),), 1)

        def second_pass():
            branch_sum = spatial(activated, second_kernel) + temporal_mix(
                extended, time_kernel, frame_local
            )
            return (section_in.astype(jnp.float32) + jax.nn.silu(branch_sum)).astype(jnp.bfloat16)

        section_out = lax.cond(active, second_pass, lambda: jnp.zeros(block_shape, jnp.bfloat16))
        finished = (jnp.arange(clip_count) == clip_slot) & active & (segment_id == sections - 1)
        out_store = jnp.where(finished[:, None, None, None, None], section_out[None], out_store)
        return ((section_out, side_store, out_store), None)

    final_carry, unused = lax.scan(
        tick_step, (prev_out, side_store, out_store), jnp.arange(tick_count, dtype=jnp.int32)
    )
    delivered = broadcast(final_carry[2], "segment", sections - 1)
    slab_rows = side_len // sections
    return lax.dynamic_slice_in_dim(delivered, segment_id * slab_rows, slab_rows, 2)


def fused_kernel(
    frames,
    noisy_ref,
    first_ref,
    second_ref,
    time_ref,
    out_ref,
    w_ref,
    n_ref,
    xe,
    xa,
    a_send,
    a_recv,
    t_send,
    t_recv,
    e_mine,
    e_recv,
    acc_ref,
    o_full,
    local_sem,
    n_sem,
    y_sem,
    got_sem,
    sent_sem,
    a_sem,
    t_sem,
    e_sem,
    o_sem,
):
    clips, side, lanes = noisy_ref.shape[0], noisy_ref.shape[2], noisy_ref.shape[4]
    half = lanes // 2
    cells = side * side
    depth = first_ref.shape[2]
    width = time_ref.shape[1]
    rows_per_conv = first_ref.shape[1] // width
    per_section = 2 * rows_per_conv + 1
    taps = per_section * width
    groups = 2 * per_section
    line = frames // 4
    seg = lax.axis_index("segment")
    me = lax.axis_index("frame")
    slots = frames // line
    core, x_at, z_at, place = lax.rem(me, 2), lax.rem(me // 2, 2), me // slots, lax.rem(me, slots)
    peer = 1 - seg
    other = me + 1 - 2 * core
    slab_rows = side // 2

    def frame_of(x_place, z_place):
        return (z_place * 2 + x_place) * 2 + core

    x_peer = frame_of(1 - x_at, z_at)
    z_pair = z_at + 1 - 2 * lax.rem(z_at, 2)
    z_half = z_at // 2
    inner = lax.rem(z_at, 2) != z_half
    z_near, z_end = 2 - z_half, 3 - 3 * z_half
    far = (z_near, z_end)
    across = (x_peer, x_peer + 1 - 2 * core)

    barrier = pltpu.get_barrier_semaphore()
    near = [(seg, other)] + [(seg, f) for f in across]
    near += [(seg, frame_of(x_at, z)) for z in far + (z_pair,)]
    near += [(peer, f) for f in (me, other) + across]
    for target in near:
        pl.semaphore_signal(barrier, inc=1, device_id=target, device_id_type=MESH)

    def columns(which):
        return pl.ds(pl.multiple_of(which * half, half), half)

    def rows_of(owner):
        return pl.ds(pl.multiple_of(owner * depth, depth), depth)

    crossing = [g % 2 < 1 for g in range(groups)]

    def part(j):
        if j < rows_per_conv:
            return first_ref, j * width
        if j == rows_per_conv:
            return time_ref, 0
        return second_ref, (j - rows_per_conv - 1) * width

    def local_copy(j):
        ref, start = part(j)
        return pltpu.make_async_copy(
            ref.at[0, pl.ds(start, width), :, columns(seg)],
            w_ref.at[pl.ds(seg * taps + j * width, width), rows_of(me)],
            local_sem.at[j],
        )

    def remote(src, dst, send, recv, device):
        return pltpu.make_async_remote_copy(
            src_ref=src,
            dst_ref=dst,
            send_sem=send,
            recv_sem=recv,
            device_id=device,
            device_id_type=MESH,
        )

    def take(ref, sem):
        pltpu.make_async_copy(ref, ref, sem).wait()

    def y_copy(j):
        ref, start = part(j)
        return remote(
            ref.at[0, pl.ds(start, width), :, columns(peer)],
            w_ref.at[pl.ds(seg * taps + j * width, width), rows_of(me)],
            y_sem.at[per_section],
            y_sem.at[j],
            (peer, me),
        )

    def slab(g, owner):
        return w_ref.at[pl.ds(g * width, width), rows_of(owner)]

    def some(g, count):
        return w_ref.at[pl.ds(g * width, width), pl.ds(0, count * depth)]

    own, crossed, lined, paired, rest = range(5)

    def give(g, owner, kind, link, target):
        ref = slab(g, owner)
        remote(ref, ref, sent_sem.at[link], got_sem.at[kind, g], (seg, target)).start()

    def give_core(g, owner):
        give(g, owner, own, 2, other)

    def round_own(g):
        section, j = g // per_section, lax.rem(g, per_section)

        @pl.when(seg == section)
        def _():
            take(slab(g, me), local_sem.at[j])

        @pl.when(seg != section)
        def _():
            take(slab(g, me), y_sem.at[j])

        give(g, me, crossed, 0, x_peer)
        give(g, me, lined, 1, frame_of(x_at, z_near))

        @pl.when(inner)
        def _():
            give(g, me, lined, 1, frame_of(x_at, z_end))

        give(g, me, paired, 1, frame_of(x_at, z_pair))
        give_core(g, me)

    def crosses(g):
        return lax.rem(g, 2) < 1

    def round_cross(g):
        take(some(g, 1), got_sem.at[crossed, g])

        @pl.when(crosses(g))
        def _():
            give(g, x_peer, rest, 1, frame_of(x_at, z_pair))

        give_core(g, x_peer)

    def round_line(g):
        take(some(g, 2), got_sem.at[lined, g])

        @pl.when(inner)
        def _():
            give(g, frame_of(x_at, z_end), lined, 1, frame_of(x_at, z_pair))

        for z in far:
            give(g, frame_of(x_at, z), rest, 0, x_peer)
        for z in far:
            give_core(g, frame_of(x_at, z))

    def round_pair(g):
        take(some(g, 1), got_sem.at[paired, g])

        @pl.when(jnp.logical_not(crosses(g)))
        def _():
            give(g, frame_of(x_at, z_pair), rest, 0, x_peer)

        give_core(g, frame_of(x_at, z_pair))

    def round_rest(g):
        take(some(g, 3), got_sem.at[rest, g])
        for z in far + (z_pair,):
            give_core(g, frame_of(1 - x_at, z))

    def round_done(g):
        take(some(g, 2 * line), got_sem.at[own, g])

    def build(x, clip, value, where):
        width_of = value.shape[1]
        wide = value.astype(jnp.float32)
        place = lax.broadcasted_iota(jnp.int32, (cells, width_of), 0) % side
        shifted = (
            jnp.where(place == 0, 0.0, pltpu.roll(wide, 1, 0)).astype(jnp.bfloat16),
            value,
            jnp.where(place == side - 1, 0.0, pltpu.roll(wide, cells - 1, 0)).astype(jnp.bfloat16),
        )
        for dx in range(3):
            x[dx, clip, 1 : side + 1, :, where] = shifted[dx].reshape(side, side, width_of)

    def row_sum(x, clip, rows, base, total=None):
        for dy in rows:
            for dx in range(3):
                view = x[dx, clip, dy : dy + side].reshape(cells, lanes)
                term = jnp.dot(
                    view, w_ref[base + width * dy + dx], preferred_element_type=jnp.float32
                )
                total = term if total is None else total + term
        return total

    def silu(u):
        return u / (1.0 + jnp.exp(-u))

    def arrival(j):
        return jnp.where(j == 0, 0, jnp.where(j == 1, slots - 1, j - 1))

    def departure(j):
        there = lax.rem(place + slots // 2 * (1 - j // 2), slots)
        return jnp.where(lax.rem(j, 2) == 0, there + 1 - 2 * lax.rem(there, 2), there)

    def noisy_local():
        return pltpu.make_async_copy(noisy_ref.at[place, 0], n_ref.at[place], n_sem.at[0])

    def send_noisy(unused):
        remote(
            noisy_ref.at[lax.rem(other, slots), 0],
            n_ref.at[place],
            n_sem.at[4],
            n_sem.at[1],
            (seg, other),
        ).start()
        for target in across:
            remote(
                noisy_ref.at[lax.rem(target, slots), 0, :, :, columns(seg)],
                n_ref.at[place, :, :, columns(seg)],
                n_sem.at[4],
                n_sem.at[2],
                (seg, target),
            ).start()

    def relay_noisy(unused):
        take(n_ref.at[0], n_sem.at[2])
        for target in across:
            ref = n_ref.at[lax.rem(target, slots), :, :, columns(seg)]
            remote(ref, ref, n_sem.at[4], n_sem.at[3], (peer, me)).start()

    def take_noisy(unused):
        for i in (0, 1, 3):
            take(n_ref.at[0], n_sem.at[i])

    def build_noisy(j):
        slot = arrival(j)
        build(xe, slot, n_ref[slot].reshape(cells, lanes), slice(None))

    def a_copy(s, slot):
        return remote(
            a_send.at[s, slot], a_recv.at[s, slot], a_sem.at[2, 0], a_sem.at[s, slot], (peer, me)
        )

    def e_copy(slot):
        return remote(e_mine.at[slot], e_recv.at[slot], e_sem.at[1, 0], e_sem.at[0, slot], (peer, me))

    sends_on = (z_at < line - 1, z_at > 0)
    takes_on = (z_at > 0, z_at < line - 1)

    def t_copy(s, way):
        target = me + slots if way == 0 else me - slots
        return remote(
            t_send.at[way, s],
            t_recv.at[way, s],
            t_sem.at[way, 2],
            t_sem.at[way, s],
            (seg, lax.rem(target + frames, frames)),
        )

    def o_copy(slot, rows):
        return remote(
            o_full.at[2 * slot + rows],
            out_ref.at[place, 0, :, :, columns(seg)],
            o_sem.at[1],
            o_sem.at[0],
            (rows, z_at * slots + slot),
        )

    def first_rows(s):
        def work(j):
            slot = arrival(j)
            total = row_sum(xe, slot, range(rows_per_conv), s * taps)
            a_send[s, slot] = silu(total).astype(jnp.bfloat16)
            a_copy(s, slot).start()

        return work

    def take_active(s):
        def work(j):
            slot = arrival(j)
            a_copy(s, slot).wait_recv()
            build(xa, slot + 1, a_send[s, slot], columns(seg))
            build(xa, slot + 1, a_recv[s, slot], columns(peer))

        return work

    def mixed(s, slot, k):
        view = xa[1, slot + k, 1 : side + 1].reshape(cells, lanes)
        return jnp.dot(
            view, w_ref[s * taps + rows_per_conv * width + k], preferred_element_type=jnp.float32
        )

    def terms(s):
        def work(j):
            for way, slot in ((1, 0), (0, slots - 1)):

                @pl.when((j == 1 - way) & sends_on[way])
                def _():
                    view = xa[1, slot + 1, 1 : side + 1].reshape(cells, lanes)
                    base = s * taps + rows_per_conv * width
                    t_send[way, s] = jnp.dot(
                        view, w_ref[base + 2 * way], preferred_element_type=jnp.float32
                    ).astype(jnp.bfloat16)
                    t_copy(s, way).start()

        return work

    def second_sum(s, slot, rows, with_time, total=None):
        base = s * taps + (rows_per_conv + 1) * width
        total = row_sum(xa, slot + 1, rows, base, total)
        if with_time:
            for k in range(width):
                total = total + mixed(s, slot, k)
        return total

    def early_rows(s, rows, with_time):
        def work(j):
            slot = arrival(j)
            acc_ref[slot] = second_sum(s, slot, rows, with_time)

        return work

    def finished(s, slot):
        for way, edge_slot in ((0, 0), (1, slots - 1)):

            @pl.when(takes_on[way] & (slot == edge_slot))
            def _():
                t_copy(s, way).wait_recv()
                acc_ref[slot] = acc_ref[slot] + t_recv[way, s].astype(jnp.float32)

        return silu(acc_ref[slot])

    def end_first(j):
        slot = arrival(j)
        acc_ref[slot] = second_sum(0, slot, range(rows_per_conv), True)
        mine = n_ref[slot, :, :, columns(seg)].reshape(cells, half).astype(jnp.float32)
        out = (mine + finished(0, slot)).astype(jnp.bfloat16)
        e_mine[slot] = ((out.astype(jnp.float32) + mine) * skip_scale).astype(jnp.bfloat16)
        e_copy(slot).start()

    def take_entering(j):
        slot = arrival(j)
        e_copy(slot).wait_recv()
        build(xe, slot, e_mine[slot], columns(seg))
        build(xe, slot, e_recv[slot], columns(peer))

    def end_second(rows, with_time):
        def work(j):
            slot = departure(j)
            acc_ref[slot] = second_sum(1, slot, rows, with_time, acc_ref[slot])
            out = (e_mine[slot].astype(jnp.float32) + finished(1, slot)).astype(jnp.bfloat16)
            full = out.reshape(2, slab_rows, side, half)
            for rows_at in range(2):
                o_full[2 * slot + rows_at] = full[rows_at]
            o_copy(slot, peer).start()

            @pl.when(slot != place)
            def _():
                o_copy(slot, seg).start()

            @pl.when(slot == place)
            def _():
                out_ref[place, 0, :, :, columns(seg)] = o_full[2 * slot + seg]

        return work

    for j in range(per_section):
        local_copy(j).start()

    noisy_local().start()
    edge = jnp.zeros((side, lanes), jnp.bfloat16)
    for x in (xe, xa):
        for dx in range(3):

            @pl.loop(0, x.shape[1])
            def _(slot):
                x[dx, slot, 0] = edge
                x[dx, slot, side + 1] = edge

    for slot in (0, slots + 1):
        xa[1, slot, 1 : side + 1] = jnp.zeros((side, side, lanes), jnp.bfloat16)

    pl.semaphore_wait(barrier, len(near))

    for j in range(per_section):
        y_copy(j).start()

    beat = slots
    rounds = (
        (0, round_own),
        (3, round_cross),
        (jnp.where(inner, 5, 9), round_line),
        (6, round_pair),
        (13, round_rest),
        (16, round_done),
    )

    def ready(g):
        return beat * g + rounds[-1][0]

    every = tuple(range(rows_per_conv))
    plan = (
        (1, 1, 1, send_noisy),
        (9, 1, 1, relay_noisy),
        (14, 1, 1, take_noisy),
        (14, 1, slots, build_noisy),
        (ready(2), 1, slots, first_rows(0)),
        (ready(2) + 6, 3, slots, take_active(0)),
        (ready(2) + 6, 3, 2, terms(0)),
        (ready(6) + 0, 1, slots, end_first),
        (ready(6) + 5, 3, slots, take_entering),
        (ready(9) + 0, 1, slots, first_rows(1)),
        (ready(9) + 5, 3, slots, take_active(1)),
        (ready(9) + 5, 3, 2, terms(1)),
        (ready(12) + 0, 1, slots, early_rows(1, every[:-1], False)),
        (ready(13) + 0, 1, slots, end_second(every[-1:], True)),
    )
    last = max(offset + stride * (count - 1) + 1 for offset, stride, count, _ in plan)

    @pl.loop(0, last)
    def _(step):
        for lag, work in reversed(rounds):
            at = step - lag

            @pl.when((at >= 0) & (lax.rem(at, beat) == 0) & (at < beat * groups))
            def _():
                work(at // beat)

        for offset, stride, count, work in plan:
            at = step - offset

            @pl.when((at >= 0) & (lax.rem(at, stride) == 0) & (at < stride * count))
            def _():
                work(at // stride)

    for i in range(2):
        take(o_full.at[pl.ds(0, 2 * slots - 1)], o_sem.at[i])
    take(n_ref.at[pl.ds(0, 3)], n_sem.at[4])
    take(e_mine, e_sem.at[1, 0])
    take(a_send, a_sem.at[2, 0])
    for way in range(2):

        @pl.when(sends_on[way])
        def _():
            take(t_send.at[way], t_sem.at[way, 2])

    take(w_ref.at[pl.ds(0, taps), pl.ds(0, depth)], y_sem.at[per_section])
    def sent(link, count):
        high = max(k for k in range(1, groups + 1) if count % k == 0)
        take(w_ref.at[pl.ds(0, high * width), pl.ds(0, count // high * depth)], sent_sem.at[link])

    crossings = sum(crossing)
    sent(0, 3 * groups + groups - crossings)
    sent(2, 2 * line * groups)

    @pl.when(inner)
    def _():
        sent(1, 4 * groups + crossings)

    @pl.when(jnp.logical_not(inner))
    def _():
        sent(1, 2 * groups + crossings)


def on_device(noisy_clips, conv_first, conv_second, temporal):
    sections = lax.axis_size("segment")
    frames = lax.axis_size("frame")
    clips, frame_local, side, _, lanes = noisy_clips.shape
    half = lanes // 2
    cells = side * side
    if sections != 2 or half % 128 or frames != 16 or clips != 4 or frame_local != 1 or side % 16:
        return pipelined(noisy_clips, conv_first, conv_second, temporal)
    taps = conv_first.shape[1] + temporal.shape[1] + conv_second.shape[1]
    per_section = taps // temporal.shape[1]
    dma = pltpu.SemaphoreType.DMA
    vmem = pl.BlockSpec(memory_space=pltpu.VMEM)
    kind = jnp.bfloat16
    return pl.pallas_call(
        functools.partial(fused_kernel, frames),
        out_shape=jax.ShapeDtypeStruct((clips, 1, side // 2, side, lanes), kind),
        in_specs=[pl.BlockSpec(memory_space=pl.ANY)] * 4,
        out_specs=vmem,
        scratch_shapes=[
            pltpu.VMEM((2 * taps, lanes, half), kind),
            pltpu.VMEM((clips, side, side, lanes), kind),
            pltpu.VMEM((3, clips, side + 2, side, lanes), kind),
            pltpu.VMEM((3, clips + 2, side + 2, side, lanes), kind),
            pltpu.VMEM((2, clips, cells, half), kind),
            pltpu.VMEM((2, clips, cells, half), kind),
            pltpu.VMEM((2, 2, cells, half), kind),
            pltpu.VMEM((2, 2, cells, half), kind),
            pltpu.VMEM((clips, cells, half), kind),
            pltpu.VMEM((clips, cells, half), kind),
            pltpu.VMEM((clips, cells, half), jnp.float32),
            pltpu.VMEM((2 * clips, side // 2, side, half), kind),
            dma((per_section,)),
            dma((5,)),
            dma((per_section + 1,)),
            dma((5, 2 * per_section)),
            dma((3,)),
            dma((3, clips)),
            dma((2, 3)),
            dma((2, clips)),
            dma((2,)),
        ],
        compiler_params=pltpu.CompilerParams(
            collective_id=0, has_side_effects=True, vmem_limit_bytes=58 * 1024 * 1024
        ),
    )(noisy_clips, conv_first, conv_second, temporal)


def solution(mesh):
    in_specs = (
        P(None, "frame", None, None, None),
        P("segment", None, "frame", None),
        P("segment", None, "frame", None),
        P("segment", None, "frame", None),
    )
    out_specs = P(None, "frame", "segment", None, None)
    return jax.shard_map(
        on_device, mesh=mesh, in_specs=in_specs, out_specs=out_specs, check_vma=False
    )
```

```python
import functools

import jax
import jax.numpy as jnp
from jax import lax
from jax.experimental import pallas as pl
from jax.experimental.pallas import tpu as pltpu
from jax.sharding import PartitionSpec as P

skip_scale = 0.7071067811865476
MESH = pl.DeviceIdType.MESH


def passed_along(shard, axis, by):
    length = lax.axis_size(axis)
    pairs = [(i, i + by) for i in range(length) if 0 <= i + by < length]
    return lax.ppermute(shard, axis, pairs)


def extended_2(cells, sides, width):
    for axis, dim in sides:
        count = lax.axis_size(axis)
        ends = count - 1
        head = lax.slice_in_dim(cells, 0, width, axis=dim)
        tail = lax.slice_in_dim(cells, cells.shape[dim] - width, cells.shape[dim], axis=dim)
        cells = jnp.concatenate(
            [
                lax.ppermute(tail, axis, [(i, (i + 1) % count) for i in range(ends)]),
                cells,
                lax.ppermute(head, axis, [((i + 1) % count, i) for i in range(ends)]),
            ],
            axis=dim,
        )
    return cells


def broadcast(shard, axis, root):
    mine = lax.axis_index(axis) == root
    return lax.psum(jnp.where(mine, shard, jnp.zeros_like(shard)), axis)


def spatial(field_in, kernel):
    extent = field_in.shape[1]
    channels = field_in.shape[3]
    padded = jnp.pad(field_in, ((0, 0), (1, 1), (1, 1), (0, 0)))
    accumulated = jnp.zeros((field_in.shape[0] * extent * extent, channels), jnp.float32)
    for row_shift in range(3):
        for col_shift in range(3):
            window = padded[
                :, row_shift : row_shift + extent, col_shift : col_shift + extent, :
            ].reshape(-1, channels)
            accumulated = accumulated + jnp.dot(
                window, kernel[3 * row_shift + col_shift], preferred_element_type=jnp.float32
            )
    return accumulated.reshape(field_in.shape)


def temporal_mix(extended, kernel, frame_local):
    channels = extended.shape[3]
    out_shape = (frame_local,) + extended.shape[1:]
    accumulated = jnp.zeros(out_shape, jnp.float32)
    for offset in range(3):
        window = extended[offset : offset + frame_local].reshape(-1, channels)
        accumulated = accumulated + jnp.dot(
            window, kernel[offset], preferred_element_type=jnp.float32
        ).reshape(out_shape)
    return accumulated


def pipelined(noisy_clips, conv_first, conv_second, temporal):
    sections = lax.axis_size("segment")
    segment_id = lax.axis_index("segment")
    first_full, second_full, time_full = (
        lax.all_gather(conv_first, "frame", axis=2, tiled=True),
        lax.all_gather(conv_second, "frame", axis=2, tiled=True),
        lax.all_gather(temporal, "frame", axis=2, tiled=True),
    )
    first_kernel = first_full[0]
    second_kernel = second_full[0]
    time_kernel = time_full[0]
    clip_count = noisy_clips.shape[0]
    frame_local = noisy_clips.shape[1]
    side_len = noisy_clips.shape[2]
    block_shape = noisy_clips.shape[1:]
    tick_count = clip_count + sections - 1
    half_sections = sections // 2
    is_up = segment_id >= half_sections
    store_depth = max(half_sections - 1, 1)
    side_store = jnp.zeros((store_depth,) + block_shape, jnp.bfloat16)
    out_store = jnp.zeros(noisy_clips.shape, jnp.bfloat16)
    prev_out = jnp.zeros(block_shape, jnp.bfloat16)

    def tick_step(carry, tick_index):
        prev_out, side_store, out_store = carry
        clip_now = tick_index - segment_id
        active = (clip_now >= 0) & (clip_now < clip_count)
        clip_slot = jnp.clip(clip_now, 0, clip_count - 1)
        own_input = lax.dynamic_index_in_dim(noisy_clips, clip_slot, 0, keepdims=False)
        received, side_store = passed_along((prev_out, side_store), "segment", 1)
        entering = jnp.where(segment_id == 0, own_input, received)
        written = (jnp.arange(store_depth) == segment_id - 1) & (segment_id < half_sections)
        side_store = jnp.where(written[:, None, None, None, None], entering[None], side_store)
        stack_slot = jnp.clip(sections - 2 - segment_id, 0, store_depth - 1)
        stored = lax.dynamic_index_in_dim(side_store, stack_slot, 0, keepdims=False)
        skip_feature = jnp.where(segment_id == sections - 1, own_input, stored)
        joined = (
            (entering.astype(jnp.float32) + skip_feature.astype(jnp.float32)) * skip_scale
        ).astype(jnp.bfloat16)
        section_in = jnp.where(is_up, joined, entering)
        activated = lax.cond(
            active,
            lambda: jax.nn.silu(spatial(section_in, first_kernel)).astype(jnp.bfloat16),
            lambda: jnp.zeros(block_shape, jnp.bfloat16),
        )
        extended = extended_2(activated, (("frame", 0),), 1)

        def second_pass():
            branch_sum = spatial(activated, second_kernel) + temporal_mix(
                extended, time_kernel, frame_local
            )
            return (section_in.astype(jnp.float32) + jax.nn.silu(branch_sum)).astype(jnp.bfloat16)

        section_out = lax.cond(active, second_pass, lambda: jnp.zeros(block_shape, jnp.bfloat16))
        finished = (jnp.arange(clip_count) == clip_slot) & active & (segment_id == sections - 1)
        out_store = jnp.where(finished[:, None, None, None, None], section_out[None], out_store)
        return ((section_out, side_store, out_store), None)

    final_carry, unused = lax.scan(
        tick_step, (prev_out, side_store, out_store), jnp.arange(tick_count, dtype=jnp.int32)
    )
    delivered = broadcast(final_carry[2], "segment", sections - 1)
    slab_rows = side_len // sections
    return lax.dynamic_slice_in_dim(delivered, segment_id * slab_rows, slab_rows, 2)


CODE, PACK, EVENTS = 16, 3, 127
ORDERS = (
    (
        131328, 3149920, 1192209, 6357810, 1246240, 7341363, 4203041, 3428372,
        3478790, 475446, 4346147, 8486948, 9458198, 3610513, 4428418, 2462595,
        4458579, 5514761, 11575306, 1590539, 11641173, 3680025, 1745478, 1791545,
        3842856, 12666816, 3916375, 2736968, 839768, 13712397, 1845833, 2856025,
        13800733, 4861078, 4954067, 11838554, 4996443, 11885733, 14757344, 5104294,
        6153127, 15921648, 243,
    ),
    (
        131328, 3149920, 1192209, 6357810, 1246259, 7341344, 1319457, 406592,
        1409408, 8540213, 4273795, 5317383, 2361410, 9458198, 9574289, 4428581,
        596128, 5480759, 3715504, 10638404, 1656102, 697173, 735558, 12589654,
        2670887, 3850779, 3877315, 839751, 5720077, 5782737, 2806345, 1872985,
        2856253, 4888093, 2922451, 11838554, 10825035, 5004213, 14703782, 14868813,
        14919517, 15921648, 243,
    ),
    (
        131328, 1118304, 3146528, 2167393, 2233137, 278578, 348272, 3351302,
        4346177, 1324068, 464210, 3482902, 8491136, 8556867, 4470310, 1544787,
        11575380, 3614595, 4524179, 5616033, 4589880, 2643618, 673593, 1622691,
        12801817, 3869498, 793129, 13769544, 12593752, 2867529, 9853212, 9818442,
        2906684, 9915347, 9722832, 894525, 14834764, 14888359, 11838493, 10833376,
        14769589, 15921648, 243,
    ),
    (
        131328, 1118304, 3153923, 2167393, 2233137, 278578, 348272, 3351302,
        8409409, 8536705, 1324068, 9458307, 2461973, 9573941, 476051, 5449224,
        4497462, 5507504, 3614625, 1525169, 1614421, 4601896, 1641123, 12829270,
        4667689, 13784843, 12651592, 12605466, 13842986, 1772873, 2856537, 9903163,
        9752650, 2906653, 9818428, 4009291, 5023323, 10871388, 5104053, 6153127,
        14726308, 15921648, 243,
    ),
)


def fused_kernel(
    frames,
    noisy_ref,
    first_ref,
    second_ref,
    time_ref,
    out_ref,
    w_ref,
    n_ref,
    xe,
    xa,
    a_send,
    a_recv,
    t_send,
    t_recv,
    e_mine,
    e_recv,
    acc_ref,
    o_full,
    local_sem,
    n_sem,
    y_sem,
    got_sem,
    sent_sem,
    a_sem,
    t_sem,
    e_sem,
    o_sem,
):
    clips, side, lanes = noisy_ref.shape[0], noisy_ref.shape[2], noisy_ref.shape[4]
    half = lanes // 2
    cells = side * side
    depth = first_ref.shape[2]
    width = time_ref.shape[1]
    rows_per_conv = first_ref.shape[1] // width
    per_section = 2 * rows_per_conv + 1
    taps = per_section * width
    groups = 2 * per_section
    line = frames // 4
    seg = lax.axis_index("segment")
    me = lax.axis_index("frame")
    slots = frames // line
    core, x_at, z_at, place = lax.rem(me, 2), lax.rem(me // 2, 2), me // slots, lax.rem(me, slots)
    peer = 1 - seg
    other = me + 1 - 2 * core
    slab_rows = side // 2

    def frame_of(x_place, z_place):
        return (z_place * 2 + x_place) * 2 + core

    x_peer = frame_of(1 - x_at, z_at)
    z_pair = z_at + 1 - 2 * lax.rem(z_at, 2)
    z_half = z_at // 2
    inner = lax.rem(z_at, 2) != z_half
    z_near, z_end = 2 - z_half, 3 - 3 * z_half
    far = (z_near, z_end)
    across = (x_peer, x_peer + 1 - 2 * core)

    barrier = pltpu.get_barrier_semaphore()
    near = [(seg, other)] + [(seg, f) for f in across]
    near += [(seg, frame_of(x_at, z)) for z in far + (z_pair,)]
    near += [(peer, f) for f in (me, other) + across]
    for target in near:
        pl.semaphore_signal(barrier, inc=1, device_id=target, device_id_type=MESH)

    def columns(which):
        return pl.ds(pl.multiple_of(which * half, half), half)

    def rows_of(owner):
        return pl.ds(pl.multiple_of(owner * depth, depth), depth)

    crossing = [g % 2 < 1 for g in range(groups)]
    every = tuple(range(rows_per_conv))

    def part(j):
        if j < rows_per_conv:
            return first_ref, j * width
        if j == rows_per_conv:
            return time_ref, 0
        return second_ref, (j - rows_per_conv - 1) * width

    def local_copy(j):
        ref, start = part(j)
        return pltpu.make_async_copy(
            ref.at[0, pl.ds(start, width), :, columns(seg)],
            w_ref.at[pl.ds(seg * taps + j * width, width), rows_of(me)],
            local_sem.at[j],
        )

    def remote(src, dst, send, recv, device):
        return pltpu.make_async_remote_copy(
            src_ref=src,
            dst_ref=dst,
            send_sem=send,
            recv_sem=recv,
            device_id=device,
            device_id_type=MESH,
        )

    def take(ref, sem):
        pltpu.make_async_copy(ref, ref, sem).wait()

    def y_copy(j):
        ref, start = part(j)
        return remote(
            ref.at[0, pl.ds(start, width), :, columns(peer)],
            w_ref.at[pl.ds(seg * taps + j * width, width), rows_of(me)],
            y_sem.at[per_section],
            y_sem.at[j],
            (peer, me),
        )

    def slab(g, owner):
        return w_ref.at[pl.ds(g * width, width), rows_of(owner)]

    def some(g, count):
        return w_ref.at[pl.ds(g * width, width), pl.ds(0, count * depth)]

    own, crossed, lined, paired, rest = range(5)

    def give(g, owner, kind, link, target):
        ref = slab(g, owner)
        remote(ref, ref, sent_sem.at[link], got_sem.at[kind, g], (seg, target)).start()

    def give_core(g, owner):
        give(g, owner, own, 2, other)

    def round_own(g):
        section, j = g // per_section, lax.rem(g, per_section)

        @pl.when(seg == section)
        def _():
            take(slab(g, me), local_sem.at[j])

        @pl.when(seg != section)
        def _():
            take(slab(g, me), y_sem.at[j])

        give(g, me, crossed, 0, x_peer)
        give(g, me, lined, 1, frame_of(x_at, z_near))

        @pl.when(inner)
        def _():
            give(g, me, lined, 1, frame_of(x_at, z_end))

        give(g, me, paired, 1, frame_of(x_at, z_pair))
        give_core(g, me)

    def crosses(g):
        return lax.rem(g, 2) < 1

    def round_cross(g):
        take(some(g, 1), got_sem.at[crossed, g])

        @pl.when(crosses(g))
        def _():
            give(g, x_peer, rest, 1, frame_of(x_at, z_pair))

        give_core(g, x_peer)

    def round_line(g):
        take(some(g, 2), got_sem.at[lined, g])

        @pl.when(inner)
        def _():
            give(g, frame_of(x_at, z_end), lined, 1, frame_of(x_at, z_pair))

        for z in far:
            give(g, frame_of(x_at, z), rest, 0, x_peer)
        for z in far:
            give_core(g, frame_of(x_at, z))

    def round_pair(g):
        take(some(g, 1), got_sem.at[paired, g])

        @pl.when(jnp.logical_not(crosses(g)))
        def _():
            give(g, frame_of(x_at, z_pair), rest, 0, x_peer)

        give_core(g, frame_of(x_at, z_pair))

    def round_rest(g):
        take(some(g, 3), got_sem.at[rest, g])
        for z in far + (z_pair,):
            give_core(g, frame_of(1 - x_at, z))

    def round_done(g):
        take(some(g, 2 * line), got_sem.at[own, g])

    def build(x, clip, value, where):
        width_of = value.shape[1]
        wide = value.astype(jnp.float32)
        place = lax.broadcasted_iota(jnp.int32, (cells, width_of), 0) % side
        shifted = (
            jnp.where(place == 0, 0.0, pltpu.roll(wide, 1, 0)).astype(jnp.bfloat16),
            value,
            jnp.where(place == side - 1, 0.0, pltpu.roll(wide, cells - 1, 0)).astype(jnp.bfloat16),
        )
        for dx in range(3):
            x[dx, clip, 1 : side + 1, :, where] = shifted[dx].reshape(side, side, width_of)

    def row_sum(x, clip, rows, base, total=None):
        for dy in rows:
            for dx in range(3):
                view = x[dx, clip, dy : dy + side].reshape(cells, lanes)
                term = jnp.dot(
                    view, w_ref[base + width * dy + dx], preferred_element_type=jnp.float32
                )
                total = term if total is None else total + term
        return total

    def silu(u):
        return u / (1.0 + jnp.exp(-u))

    def arrival(j):
        slot = jnp.where(j == 0, 0, jnp.where(j == 1, slots - 1, j - 1))
        return jnp.where(z_half == 0, slot, slots - 1 - slot)

    def departure(j):
        there = lax.rem(place + slots // 2 * (1 - j // 2), slots)
        return jnp.where(lax.rem(j, 2) == 0, there + 1 - 2 * lax.rem(there, 2), there)

    def noisy_local():
        return pltpu.make_async_copy(noisy_ref.at[place, 0], n_ref.at[place], n_sem.at[0])

    def send_noisy(part_at):
        @pl.when(part_at == 0)
        def _():
            remote(
                noisy_ref.at[lax.rem(other, slots), 0],
                n_ref.at[place],
                n_sem.at[4],
                n_sem.at[1],
                (seg, other),
            ).start()

        target = jnp.where(part_at == 0, across[0], across[1])
        remote(
            noisy_ref.at[lax.rem(target, slots), 0, :, :, columns(seg)],
            n_ref.at[place, :, :, columns(seg)],
            n_sem.at[4],
            n_sem.at[2],
            (seg, target),
        ).start()

    def relay_noisy(unused):
        take(n_ref.at[0], n_sem.at[2])
        for target in across:
            ref = n_ref.at[lax.rem(target, slots), :, :, columns(seg)]
            remote(ref, ref, n_sem.at[4], n_sem.at[3], (peer, me)).start()

    def build_noisy(j):
        @pl.when(j == 0)
        def _():
            for i in (0, 1, 3):
                take(n_ref.at[0], n_sem.at[i])

        slot = arrival(j)
        build(xe, slot, n_ref[slot].reshape(cells, lanes), slice(None))

    def a_copy(s, slot):
        return remote(
            a_send.at[s, slot], a_recv.at[s, slot], a_sem.at[2, 0], a_sem.at[s, slot], (peer, me)
        )

    def e_copy(slot):
        return remote(e_mine.at[slot], e_recv.at[slot], e_sem.at[1, 0], e_sem.at[0, slot], (peer, me))

    sends_on = (z_at < line - 1, z_at > 0)
    takes_on = (z_at > 0, z_at < line - 1)

    def t_copy(s, way):
        target = me + slots if way == 0 else me - slots
        return remote(
            t_send.at[way, s],
            t_recv.at[way, s],
            t_sem.at[way, 2],
            t_sem.at[way, s],
            (seg, lax.rem(target + frames, frames)),
        )

    def o_copy(slot, rows):
        return remote(
            o_full.at[2 * slot + rows],
            out_ref.at[place, 0, :, :, columns(seg)],
            o_sem.at[1],
            o_sem.at[0],
            (rows, z_at * slots + slot),
        )

    def first_rows(turn):
        s, slot = lax.div(turn, slots), arrival(lax.rem(turn, slots))
        total = row_sum(xe, slot, every, s * taps)
        a_send[s, slot] = silu(total).astype(jnp.bfloat16)
        a_copy(s, slot).start()

    def take_active(turn):
        s, slot = lax.div(turn, slots), arrival(lax.rem(turn, slots))
        a_copy(s, slot).wait_recv()
        build(xa, slot + 1, a_send[s, slot], columns(seg))
        build(xa, slot + 1, a_recv[s, slot], columns(peer))

    def mixed(s, slot, k):
        view = xa[1, slot + k, 1 : side + 1].reshape(cells, lanes)
        return jnp.dot(
            view, w_ref[s * taps + rows_per_conv * width + k], preferred_element_type=jnp.float32
        )

    def terms(turn):
        s, slot = lax.div(turn, slots), arrival(lax.rem(turn, slots))
        view = xa[1, slot + 1, 1 : side + 1].reshape(cells, lanes)
        base = s * taps + rows_per_conv * width
        for way, edge_slot in ((1, 0), (0, slots - 1)):

            @pl.when((slot == edge_slot) & sends_on[way])
            def _():
                t_send[way, s] = jnp.dot(
                    view, w_ref[base + 2 * way], preferred_element_type=jnp.float32
                ).astype(jnp.bfloat16)
                t_copy(s, way).start()

    def second_sum(s, slot, rows, with_time, total=None):
        base = s * taps + (rows_per_conv + 1) * width
        total = row_sum(xa, slot + 1, rows, base, total)
        if with_time:
            for k in range(width):
                total = total + mixed(s, slot, k)
        return total

    def early_rows(j):
        slot = arrival(j)
        acc_ref[slot] = second_sum(1, slot, every[:-1], False)

    def finished(s, slot):
        for way, edge_slot in ((0, 0), (1, slots - 1)):

            @pl.when(takes_on[way] & (slot == edge_slot))
            def _():
                t_copy(s, way).wait_recv()
                acc_ref[slot] = acc_ref[slot] + t_recv[way, s].astype(jnp.float32)

        return silu(acc_ref[slot])

    def end_first(j):
        slot = arrival(j)
        acc_ref[slot] = second_sum(0, slot, every, True)
        mine = n_ref[slot, :, :, columns(seg)].reshape(cells, half).astype(jnp.float32)
        out = (mine + finished(0, slot)).astype(jnp.bfloat16)
        e_mine[slot] = ((out.astype(jnp.float32) + mine) * skip_scale).astype(jnp.bfloat16)
        e_copy(slot).start()

    def take_entering(j):
        slot = arrival(j)
        e_copy(slot).wait_recv()
        build(xe, slot, e_mine[slot], columns(seg))
        build(xe, slot, e_recv[slot], columns(peer))

    def end_second(j):
        slot = departure(j)
        acc_ref[slot] = second_sum(1, slot, every[-1:], True, acc_ref[slot])
        out = (e_mine[slot].astype(jnp.float32) + finished(1, slot)).astype(jnp.bfloat16)
        full = out.reshape(2, slab_rows, side, half)
        for rows_at in range(2):
            o_full[2 * slot + rows_at] = full[rows_at]
        o_copy(slot, peer).start()

        @pl.when(slot != place)
        def _():
            o_copy(slot, seg).start()

        @pl.when(slot == place)
        def _():
            out_ref[place, 0, :, :, columns(seg)] = o_full[2 * slot + seg]

    works = (
        round_own,
        round_cross,
        round_line,
        round_pair,
        round_rest,
        round_done,
        send_noisy,
        relay_noisy,
        build_noisy,
        first_rows,
        take_active,
        terms,
        end_first,
        take_entering,
        early_rows,
        end_second,
    )

    words = []
    for codes in zip(*ORDERS):
        ends, inners = (jnp.where(seg == 0, codes[n], codes[n + 1]) for n in (0, 2))
        words.append(jnp.where(inner, inners, ends))

    def run(some_works, kind, turn, low=0):
        if len(some_works) == 1:
            some_works[0](turn)
            return
        cut = len(some_works) // 2

        @pl.when(kind < low + cut)
        def _():
            run(some_works[:cut], kind, turn, low)

        @pl.when(kind >= low + cut)
        def _():
            run(some_works[cut:], kind, turn, low + cut)

    for j in range(per_section):
        local_copy(j).start()

    noisy_local().start()
    edge = jnp.zeros((side, lanes), jnp.bfloat16)
    for x in (xe, xa):
        for dx in range(3):

            @pl.loop(0, x.shape[1])
            def _(slot):
                x[dx, slot, 0] = edge
                x[dx, slot, side + 1] = edge

    for slot in (0, slots + 1):
        xa[1, slot, 1 : side + 1] = jnp.zeros((side, side, lanes), jnp.bfloat16)

    pl.semaphore_wait(barrier, len(near))

    for j in range(per_section):
        y_copy(j).start()

    @pl.loop(0, EVENTS)
    def _(i):
        at, level = i // PACK, words
        while len(level) > 1:
            odd = lax.rem(at, 2) == 1
            level = [
                jnp.where(odd, level[n + 1], level[n]) if n + 1 < len(level) else level[n]
                for n in range(0, len(level), 2)
            ]
            at = at // 2
        code = level[0]
        for n in range(1, PACK):
            code = jnp.where(lax.rem(i, PACK) == n, level[0] // (CODE * CODE) ** n, code)
        code = lax.rem(code, CODE * CODE)
        run(works, code // CODE, lax.rem(code, CODE))

    for i in range(2):
        take(o_full.at[pl.ds(0, 2 * slots - 1)], o_sem.at[i])
    take(n_ref.at[pl.ds(0, 3)], n_sem.at[4])
    take(e_mine, e_sem.at[1, 0])
    take(a_send, a_sem.at[2, 0])
    for way in range(2):

        @pl.when(sends_on[way])
        def _():
            take(t_send.at[way], t_sem.at[way, 2])

    take(w_ref.at[pl.ds(0, taps), pl.ds(0, depth)], y_sem.at[per_section])
    def sent(link, count):
        high = max(k for k in range(1, groups + 1) if count % k == 0)
        take(w_ref.at[pl.ds(0, high * width), pl.ds(0, count // high * depth)], sent_sem.at[link])

    crossings = sum(crossing)
    sent(0, 3 * groups + groups - crossings)
    sent(2, 2 * line * groups)

    @pl.when(inner)
    def _():
        sent(1, 4 * groups + crossings)

    @pl.when(jnp.logical_not(inner))
    def _():
        sent(1, 2 * groups + crossings)


def on_device(noisy_clips, conv_first, conv_second, temporal):
    sections = lax.axis_size("segment")
    frames = lax.axis_size("frame")
    clips, frame_local, side, _, lanes = noisy_clips.shape
    half = lanes // 2
    cells = side * side
    if sections != 2 or half % 128 or frames != 16 or clips != 4 or frame_local != 1 or side % 16:
        return pipelined(noisy_clips, conv_first, conv_second, temporal)
    taps = conv_first.shape[1] + temporal.shape[1] + conv_second.shape[1]
    per_section = taps // temporal.shape[1]
    dma = pltpu.SemaphoreType.DMA
    vmem = pl.BlockSpec(memory_space=pltpu.VMEM)
    kind = jnp.bfloat16
    return pl.pallas_call(
        functools.partial(fused_kernel, frames),
        out_shape=jax.ShapeDtypeStruct((clips, 1, side // 2, side, lanes), kind),
        in_specs=[pl.BlockSpec(memory_space=pl.ANY)] * 4,
        out_specs=vmem,
        scratch_shapes=[
            pltpu.VMEM((2 * taps, lanes, half), kind),
            pltpu.VMEM((clips, side, side, lanes), kind),
            pltpu.VMEM((3, clips, side + 2, side, lanes), kind),
            pltpu.VMEM((3, clips + 2, side + 2, side, lanes), kind),
            pltpu.VMEM((2, clips, cells, half), kind),
            pltpu.VMEM((2, clips, cells, half), kind),
            pltpu.VMEM((2, 2, cells, half), kind),
            pltpu.VMEM((2, 2, cells, half), kind),
            pltpu.VMEM((clips, cells, half), kind),
            pltpu.VMEM((clips, cells, half), kind),
            pltpu.VMEM((clips, cells, half), jnp.float32),
            pltpu.VMEM((2 * clips, side // 2, side, half), kind),
            dma((per_section,)),
            dma((5,)),
            dma((per_section + 1,)),
            dma((5, 2 * per_section)),
            dma((3,)),
            dma((3, clips)),
            dma((2, 3)),
            dma((2, clips)),
            dma((2,)),
        ],
        compiler_params=pltpu.CompilerParams(
            collective_id=0, has_side_effects=True, vmem_limit_bytes=58 * 1024 * 1024
        ),
    )(noisy_clips, conv_first, conv_second, temporal)


def solution(mesh):
    in_specs = (
        P(None, "frame", None, None, None),
        P("segment", None, "frame", None),
        P("segment", None, "frame", None),
        P("segment", None, "frame", None),
    )
    out_specs = P(None, "frame", "segment", None, None)
    return jax.shard_map(
        on_device, mesh=mesh, in_specs=in_specs, out_specs=out_specs, check_vma=False
    )
```

```python
import functools

import jax
import jax.numpy as jnp
from jax import lax
from jax.experimental import pallas as pl
from jax.experimental.pallas import tpu as pltpu
from jax.sharding import PartitionSpec as P

skip_scale = 0.7071067811865476
MESH = pl.DeviceIdType.MESH


def passed_along(shard, axis, by):
    length = lax.axis_size(axis)
    pairs = [(i, i + by) for i in range(length) if 0 <= i + by < length]
    return lax.ppermute(shard, axis, pairs)


def extended_2(cells, sides, width):
    for axis, dim in sides:
        count = lax.axis_size(axis)
        ends = count - 1
        head = lax.slice_in_dim(cells, 0, width, axis=dim)
        tail = lax.slice_in_dim(cells, cells.shape[dim] - width, cells.shape[dim], axis=dim)
        cells = jnp.concatenate(
            [
                lax.ppermute(tail, axis, [(i, (i + 1) % count) for i in range(ends)]),
                cells,
                lax.ppermute(head, axis, [((i + 1) % count, i) for i in range(ends)]),
            ],
            axis=dim,
        )
    return cells


def broadcast(shard, axis, root):
    mine = lax.axis_index(axis) == root
    return lax.psum(jnp.where(mine, shard, jnp.zeros_like(shard)), axis)


def spatial(field_in, kernel):
    extent = field_in.shape[1]
    channels = field_in.shape[3]
    padded = jnp.pad(field_in, ((0, 0), (1, 1), (1, 1), (0, 0)))
    accumulated = jnp.zeros((field_in.shape[0] * extent * extent, channels), jnp.float32)
    for row_shift in range(3):
        for col_shift in range(3):
            window = padded[
                :, row_shift : row_shift + extent, col_shift : col_shift + extent, :
            ].reshape(-1, channels)
            accumulated = accumulated + jnp.dot(
                window, kernel[3 * row_shift + col_shift], preferred_element_type=jnp.float32
            )
    return accumulated.reshape(field_in.shape)


def temporal_mix(extended, kernel, frame_local):
    channels = extended.shape[3]
    out_shape = (frame_local,) + extended.shape[1:]
    accumulated = jnp.zeros(out_shape, jnp.float32)
    for offset in range(3):
        window = extended[offset : offset + frame_local].reshape(-1, channels)
        accumulated = accumulated + jnp.dot(
            window, kernel[offset], preferred_element_type=jnp.float32
        ).reshape(out_shape)
    return accumulated


def pipelined(noisy_clips, conv_first, conv_second, temporal):
    sections = lax.axis_size("segment")
    segment_id = lax.axis_index("segment")
    first_full, second_full, time_full = (
        lax.all_gather(conv_first, "frame", axis=2, tiled=True),
        lax.all_gather(conv_second, "frame", axis=2, tiled=True),
        lax.all_gather(temporal, "frame", axis=2, tiled=True),
    )
    first_kernel = first_full[0]
    second_kernel = second_full[0]
    time_kernel = time_full[0]
    clip_count = noisy_clips.shape[0]
    frame_local = noisy_clips.shape[1]
    side_len = noisy_clips.shape[2]
    block_shape = noisy_clips.shape[1:]
    tick_count = clip_count + sections - 1
    half_sections = sections // 2
    is_up = segment_id >= half_sections
    store_depth = max(half_sections - 1, 1)
    side_store = jnp.zeros((store_depth,) + block_shape, jnp.bfloat16)
    out_store = jnp.zeros(noisy_clips.shape, jnp.bfloat16)
    prev_out = jnp.zeros(block_shape, jnp.bfloat16)

    def tick_step(carry, tick_index):
        prev_out, side_store, out_store = carry
        clip_now = tick_index - segment_id
        active = (clip_now >= 0) & (clip_now < clip_count)
        clip_slot = jnp.clip(clip_now, 0, clip_count - 1)
        own_input = lax.dynamic_index_in_dim(noisy_clips, clip_slot, 0, keepdims=False)
        received, side_store = passed_along((prev_out, side_store), "segment", 1)
        entering = jnp.where(segment_id == 0, own_input, received)
        written = (jnp.arange(store_depth) == segment_id - 1) & (segment_id < half_sections)
        side_store = jnp.where(written[:, None, None, None, None], entering[None], side_store)
        stack_slot = jnp.clip(sections - 2 - segment_id, 0, store_depth - 1)
        stored = lax.dynamic_index_in_dim(side_store, stack_slot, 0, keepdims=False)
        skip_feature = jnp.where(segment_id == sections - 1, own_input, stored)
        joined = (
            (entering.astype(jnp.float32) + skip_feature.astype(jnp.float32)) * skip_scale
        ).astype(jnp.bfloat16)
        section_in = jnp.where(is_up, joined, entering)
        activated = lax.cond(
            active,
            lambda: jax.nn.silu(spatial(section_in, first_kernel)).astype(jnp.bfloat16),
            lambda: jnp.zeros(block_shape, jnp.bfloat16),
        )
        extended = extended_2(activated, (("frame", 0),), 1)

        def second_pass():
            branch_sum = spatial(activated, second_kernel) + temporal_mix(
                extended, time_kernel, frame_local
            )
            return (section_in.astype(jnp.float32) + jax.nn.silu(branch_sum)).astype(jnp.bfloat16)

        section_out = lax.cond(active, second_pass, lambda: jnp.zeros(block_shape, jnp.bfloat16))
        finished = (jnp.arange(clip_count) == clip_slot) & active & (segment_id == sections - 1)
        out_store = jnp.where(finished[:, None, None, None, None], section_out[None], out_store)
        return ((section_out, side_store, out_store), None)

    final_carry, unused = lax.scan(
        tick_step, (prev_out, side_store, out_store), jnp.arange(tick_count, dtype=jnp.int32)
    )
    delivered = broadcast(final_carry[2], "segment", sections - 1)
    slab_rows = side_len // sections
    return lax.dynamic_slice_in_dim(delivered, segment_id * slab_rows, slab_rows, 2)


CODE, PACK, EVENTS = 16, 3, 127
ORDERS = (
    (
        6291712, 221442, 1126416, 3277873, 332339, 1253488, 406548, 464161,
        4203061, 544822, 3613462, 8486977, 2392599, 623441, 5380162, 9539640,
        9577795, 5449363, 723524, 2577433, 4536588, 10507578, 2639536, 10573338,
        859057, 5750855, 3908124, 10693057, 12729416, 5817130, 2871325, 9722185,
        9818429, 13773898, 2968470, 13851482, 6048919, 11838541, 10837472, 10936757,
        11002609, 15983602, 240,
    ),
    (
        6291712, 221442, 1126416, 3277873, 332339, 1253488, 3409428, 8486945,
        8618517, 2230069, 3544640, 2295888, 1524023, 2361681, 5380162, 9539640,
        9577795, 5449363, 11575321, 11641156, 742410, 2573730, 3757324, 3842886,
        12604954, 4668353, 3981864, 5712323, 13638683, 13715469, 4794968, 1954365,
        9802841, 9849387, 13851180, 11838615, 10832685, 5004213, 14703782, 14868813,
        15837021, 15983602, 240,
    ),
    (
        6291712, 221442, 2101520, 1180720, 340257, 3285616, 2295315, 4199475,
        4280327, 1389604, 2426961, 8405557, 5379713, 4428176, 8533542, 1528722,
        3642243, 599876, 676888, 4536360, 5615776, 2704907, 11641145, 4656214,
        2767522, 1726233, 3916451, 4768555, 5770523, 13781308, 5844161, 4898966,
        3002652, 5936445, 4954067, 9752605, 6048859, 5104294, 14919517, 15971749,
        11838689, 15786226, 241,
    ),
    (
        6291712, 221442, 2101520, 1180720, 340257, 3285616, 2295315, 8393779,
        8552768, 5244803, 3417153, 545045, 4338981, 9458198, 2507665, 9671222,
        10491731, 2570160, 11641156, 5507352, 2662922, 10700088, 4590421, 5639225,
        4702658, 12632873, 1710423, 866858, 13769544, 2825304, 4838203, 5848108,
        4888470, 5936593, 1916205, 13650854, 5983380, 11904348, 5104353, 6153127,
        11838707, 14742257, 240,
    ),
)
DIRECT, SHARES = 0, ((1, 3), (2, 5))


def fused_kernel(
    frames,
    noisy_ref,
    first_ref,
    second_ref,
    time_ref,
    out_ref,
    w_ref,
    n_ref,
    xe,
    xa,
    a_send,
    a_recv,
    t_send,
    t_recv,
    e_mine,
    e_recv,
    acc_ref,
    o_full,
    local_sem,
    n_sem,
    y_sem,
    got_sem,
    sent_sem,
    a_sem,
    t_sem,
    e_sem,
    o_sem,
):
    clips, side, lanes = noisy_ref.shape[0], noisy_ref.shape[2], noisy_ref.shape[4]
    half = lanes // 2
    cells = side * side
    depth = first_ref.shape[2]
    width = time_ref.shape[1]
    rows_per_conv = first_ref.shape[1] // width
    per_section = 2 * rows_per_conv + 1
    taps = per_section * width
    groups = 2 * per_section
    line = frames // 4
    seg = lax.axis_index("segment")
    me = lax.axis_index("frame")
    slots = frames // line
    core, x_at, z_at, place = lax.rem(me, 2), lax.rem(me // 2, 2), me // slots, lax.rem(me, slots)
    peer = 1 - seg
    other = me + 1 - 2 * core
    slab_rows = side // 2

    def frame_of(x_place, z_place):
        return (z_place * 2 + x_place) * 2 + core

    x_peer = frame_of(1 - x_at, z_at)
    z_pair = z_at + 1 - 2 * lax.rem(z_at, 2)
    z_half = z_at // 2
    inner = lax.rem(z_at, 2) != z_half
    z_near, z_end = 2 - z_half, 3 - 3 * z_half
    far = (z_near, z_end)
    across = (x_peer, x_peer + 1 - 2 * core)

    barrier = pltpu.get_barrier_semaphore()
    near = [(seg, other)] + [(seg, f) for f in across]
    near += [(seg, frame_of(x_at, z)) for z in far + (z_pair,)]
    near += [(peer, f) for f in (me, other) + across]
    for target in near:
        pl.semaphore_signal(barrier, inc=1, device_id=target, device_id_type=MESH)

    def columns(which):
        return pl.ds(pl.multiple_of(which * half, half), half)

    def rows_of(owner):
        return pl.ds(pl.multiple_of(owner * depth, depth), depth)

    every = tuple(range(rows_per_conv))

    def part(j):
        if j < rows_per_conv:
            return first_ref, j * width
        if j == rows_per_conv:
            return time_ref, 0
        return second_ref, (j - rows_per_conv - 1) * width

    def local_copy(j):
        ref, start = part(j)
        return pltpu.make_async_copy(
            ref.at[0, pl.ds(start, width), :, columns(seg)],
            w_ref.at[pl.ds(seg * taps + j * width, width), rows_of(me)],
            local_sem.at[j],
        )

    def remote(src, dst, send, recv, device):
        return pltpu.make_async_remote_copy(
            src_ref=src,
            dst_ref=dst,
            send_sem=send,
            recv_sem=recv,
            device_id=device,
            device_id_type=MESH,
        )

    def take(ref, sem):
        pltpu.make_async_copy(ref, ref, sem).wait()

    def y_copy(j):
        ref, start = part(j)
        return remote(
            ref.at[0, pl.ds(start, width), :, columns(peer)],
            w_ref.at[pl.ds(seg * taps + j * width, width), rows_of(me)],
            y_sem.at[per_section],
            y_sem.at[j],
            (peer, me),
        )

    def slab(g, owner):
        return w_ref.at[pl.ds(g * width, width), rows_of(owner)]

    def some(g, count):
        return w_ref.at[pl.ds(g * width, width), pl.ds(0, count * depth)]

    own, crossed, lined, paired, rest = range(5)

    def give(g, owner, kind, link, target):
        ref = slab(g, owner)
        remote(ref, ref, sent_sem.at[link], got_sem.at[kind, g], (seg, target)).start()

    def give_core(g, owner):
        give(g, owner, own, 2, other)

    def round_own(g):
        section, j = g // per_section, lax.rem(g, per_section)

        @pl.when(seg == section)
        def _():
            take(slab(g, me), local_sem.at[j])

        @pl.when(seg != section)
        def _():
            take(slab(g, me), y_sem.at[j])

        give(g, me, crossed, 0, x_peer)
        give(g, me, lined, 1, frame_of(x_at, z_near))

        @pl.when(inner | (g < DIRECT))
        def _():
            give(g, me, lined, 1, frame_of(x_at, z_end))

        give(g, me, paired, 1, frame_of(x_at, z_pair))
        give_core(g, me)

    def crosses(g, is_inner):
        end, mid = (lax.rem(g, share[1]) < share[0] for share in SHARES)
        return jnp.where(is_inner, mid, end)

    def round_cross(g):
        take(some(g, 1), got_sem.at[crossed, g])

        @pl.when(crosses(g, inner))
        def _():
            give(g, x_peer, rest, 1, frame_of(x_at, z_pair))

        give_core(g, x_peer)

    def round_line(g):
        take(some(g, 2), got_sem.at[lined, g])

        @pl.when(inner & (g >= DIRECT))
        def _():
            give(g, frame_of(x_at, z_end), lined, 1, frame_of(x_at, z_pair))

        for z in far:
            give(g, frame_of(x_at, z), rest, 0, x_peer)
        for z in far:
            give_core(g, frame_of(x_at, z))

    def round_pair(g):
        take(some(g, 1), got_sem.at[paired, g])

        @pl.when(jnp.logical_not(crosses(g, jnp.logical_not(inner))))
        def _():
            give(g, frame_of(x_at, z_pair), rest, 0, x_peer)

        give_core(g, frame_of(x_at, z_pair))

    def round_rest(g):
        take(some(g, 3), got_sem.at[rest, g])
        for z in far + (z_pair,):
            give_core(g, frame_of(1 - x_at, z))

    def round_done(g):
        take(some(g, 2 * line), got_sem.at[own, g])

    def build(x, clip, value, where):
        width_of = value.shape[1]
        wide = value.astype(jnp.float32)
        place = lax.broadcasted_iota(jnp.int32, (cells, width_of), 0) % side
        shifted = (
            jnp.where(place == 0, 0.0, pltpu.roll(wide, 1, 0)).astype(jnp.bfloat16),
            value,
            jnp.where(place == side - 1, 0.0, pltpu.roll(wide, cells - 1, 0)).astype(jnp.bfloat16),
        )
        for dx in range(3):
            x[dx, clip, 1 : side + 1, :, where] = shifted[dx].reshape(side, side, width_of)

    def row_sum(x, clip, rows, base, total=None):
        for dy in rows:
            for dx in range(3):
                view = x[dx, clip, dy : dy + side].reshape(cells, lanes)
                term = jnp.dot(
                    view, w_ref[base + width * dy + dx], preferred_element_type=jnp.float32
                )
                total = term if total is None else total + term
        return total

    def silu(u):
        return u / (1.0 + jnp.exp(-u))

    def arrival(j):
        slot = jnp.where(j == 0, 0, jnp.where(j == 1, slots - 1, j - 1))
        slot = jnp.where(inner, slot, slots - 1 - j)
        return jnp.where(z_half == 0, slot, slots - 1 - slot)

    def noisy_local():
        return pltpu.make_async_copy(noisy_ref.at[place, 0], n_ref.at[place], n_sem.at[0])

    def send_noisy(part_at):
        @pl.when(part_at == 0)
        def _():
            remote(
                noisy_ref.at[lax.rem(other, slots), 0],
                n_ref.at[place],
                n_sem.at[4],
                n_sem.at[1],
                (seg, other),
            ).start()

        target = jnp.where(part_at == 0, across[0], across[1])
        remote(
            noisy_ref.at[lax.rem(target, slots), 0, :, :, columns(seg)],
            n_ref.at[place, :, :, columns(seg)],
            n_sem.at[4],
            n_sem.at[2],
            (seg, target),
        ).start()

    def relay_noisy(unused):
        take(n_ref.at[0], n_sem.at[2])
        for target in across:
            ref = n_ref.at[lax.rem(target, slots), :, :, columns(seg)]
            remote(ref, ref, n_sem.at[4], n_sem.at[3], (peer, me)).start()

    def build_noisy(j):
        @pl.when(j == 0)
        def _():
            for i in (0, 1, 3):
                take(n_ref.at[0], n_sem.at[i])

        slot = arrival(j)
        build(xe, slot, n_ref[slot].reshape(cells, lanes), slice(None))

    def a_copy(s, slot):
        return remote(
            a_send.at[s, slot], a_recv.at[s, slot], a_sem.at[2, 0], a_sem.at[s, slot], (peer, me)
        )

    def e_copy(slot):
        return remote(e_mine.at[slot], e_recv.at[slot], e_sem.at[1, 0], e_sem.at[0, slot], (peer, me))

    sends_on = (z_at < line - 1, z_at > 0)
    takes_on = (z_at > 0, z_at < line - 1)

    def t_copy(s, way):
        target = me + slots if way == 0 else me - slots
        return remote(
            t_send.at[way, s],
            t_recv.at[way, s],
            t_sem.at[way, 2],
            t_sem.at[way, s],
            (seg, lax.rem(target + frames, frames)),
        )

    def o_copy(slot, rows):
        return remote(
            o_full.at[2 * slot + rows],
            out_ref.at[place, 0, :, :, columns(seg)],
            o_sem.at[1],
            o_sem.at[0],
            (rows, z_at * slots + slot),
        )

    def first_rows(turn):
        s, slot = lax.div(turn, slots), arrival(lax.rem(turn, slots))
        total = row_sum(xe, slot, every, s * taps)
        a_send[s, slot] = silu(total).astype(jnp.bfloat16)
        a_copy(s, slot).start()

    def take_active(turn):
        s, slot = lax.div(turn, slots), arrival(lax.rem(turn, slots))
        a_copy(s, slot).wait_recv()
        build(xa, slot + 1, a_send[s, slot], columns(seg))
        build(xa, slot + 1, a_recv[s, slot], columns(peer))

    def mixed(s, slot, k):
        view = xa[1, slot + k, 1 : side + 1].reshape(cells, lanes)
        return jnp.dot(
            view, w_ref[s * taps + rows_per_conv * width + k], preferred_element_type=jnp.float32
        )

    def terms(turn):
        s, slot = lax.div(turn, slots), arrival(lax.rem(turn, slots))
        view = xa[1, slot + 1, 1 : side + 1].reshape(cells, lanes)
        base = s * taps + rows_per_conv * width
        for way, edge_slot in ((1, 0), (0, slots - 1)):

            @pl.when((slot == edge_slot) & sends_on[way])
            def _():
                t_send[way, s] = jnp.dot(
                    view, w_ref[base + 2 * way], preferred_element_type=jnp.float32
                ).astype(jnp.bfloat16)
                t_copy(s, way).start()

    def second_sum(s, slot, rows, with_time, total=None):
        base = s * taps + (rows_per_conv + 1) * width
        total = row_sum(xa, slot + 1, rows, base, total)
        if with_time:
            for k in range(width):
                total = total + mixed(s, slot, k)
        return total

    def early_rows(j):
        slot = arrival(j)
        acc_ref[slot] = second_sum(1, slot, every[:-1], False)

    def finished(s, slot):
        for way, edge_slot in ((0, 0), (1, slots - 1)):

            @pl.when(takes_on[way] & (slot == edge_slot))
            def _():
                t_copy(s, way).wait_recv()
                acc_ref[slot] = acc_ref[slot] + t_recv[way, s].astype(jnp.float32)

        return silu(acc_ref[slot])

    def end_first(j):
        slot = arrival(j)
        acc_ref[slot] = second_sum(0, slot, every, True)
        mine = n_ref[slot, :, :, columns(seg)].reshape(cells, half).astype(jnp.float32)
        out = (mine + finished(0, slot)).astype(jnp.bfloat16)
        e_mine[slot] = ((out.astype(jnp.float32) + mine) * skip_scale).astype(jnp.bfloat16)
        e_copy(slot).start()

    def take_entering(j):
        slot = arrival(j)
        e_copy(slot).wait_recv()
        build(xe, slot, e_mine[slot], columns(seg))
        build(xe, slot, e_recv[slot], columns(peer))

    def end_second(j):
        slot = arrival(j)
        acc_ref[slot] = second_sum(1, slot, every[-1:], True, acc_ref[slot])
        out = (e_mine[slot].astype(jnp.float32) + finished(1, slot)).astype(jnp.bfloat16)
        full = out.reshape(2, slab_rows, side, half)
        for rows_at in range(2):
            o_full[2 * slot + rows_at] = full[rows_at]
        o_copy(slot, peer).start()

        @pl.when(slot != place)
        def _():
            o_copy(slot, seg).start()

        @pl.when(slot == place)
        def _():
            out_ref[place, 0, :, :, columns(seg)] = o_full[2 * slot + seg]

    works = (
        round_own,
        round_cross,
        round_line,
        round_pair,
        round_rest,
        round_done,
        send_noisy,
        relay_noisy,
        build_noisy,
        first_rows,
        take_active,
        terms,
        end_first,
        take_entering,
        early_rows,
        end_second,
    )

    words = []
    for codes in zip(*ORDERS):
        ends, inners = (jnp.where(seg == 0, codes[n], codes[n + 1]) for n in (0, 2))
        words.append(jnp.where(inner, inners, ends))

    def run(some_works, kind, turn, low=0):
        if len(some_works) == 1:
            some_works[0](turn)
            return
        cut = len(some_works) // 2

        @pl.when(kind < low + cut)
        def _():
            run(some_works[:cut], kind, turn, low)

        @pl.when(kind >= low + cut)
        def _():
            run(some_works[cut:], kind, turn, low + cut)

    for j in range(per_section):
        local_copy(j).start()

    noisy_local().start()
    edge = jnp.zeros((side, lanes), jnp.bfloat16)
    for x in (xe, xa):
        for dx in range(3):

            @pl.loop(0, x.shape[1])
            def _(slot):
                x[dx, slot, 0] = edge
                x[dx, slot, side + 1] = edge

    for slot in (0, slots + 1):
        xa[1, slot, 1 : side + 1] = jnp.zeros((side, side, lanes), jnp.bfloat16)

    pl.semaphore_wait(barrier, len(near))

    for j in range(per_section):
        y_copy(j).start()

    @pl.loop(0, EVENTS)
    def _(i):
        at, level = i // PACK, words
        while len(level) > 1:
            odd = lax.rem(at, 2) == 1
            level = [
                jnp.where(odd, level[n + 1], level[n]) if n + 1 < len(level) else level[n]
                for n in range(0, len(level), 2)
            ]
            at = at // 2
        code = level[0]
        for n in range(1, PACK):
            code = jnp.where(lax.rem(i, PACK) == n, level[0] // (CODE * CODE) ** n, code)
        code = lax.rem(code, CODE * CODE)
        run(works, code // CODE, lax.rem(code, CODE))

    for i in range(2):
        take(o_full.at[pl.ds(0, 2 * slots - 1)], o_sem.at[i])
    take(n_ref.at[pl.ds(0, 3)], n_sem.at[4])
    take(e_mine, e_sem.at[1, 0])
    take(a_send, a_sem.at[2, 0])
    for way in range(2):

        @pl.when(sends_on[way])
        def _():
            take(t_send.at[way], t_sem.at[way, 2])

    take(w_ref.at[pl.ds(0, taps), pl.ds(0, depth)], y_sem.at[per_section])
    def sent(link, count):
        rows = count * width * depth
        fits = [k for k in range(1, 2 * taps + 1) if rows % (16 * k) == 0 and rows // k <= lanes]
        take(w_ref.at[pl.ds(0, fits[0]), pl.ds(0, rows // fits[0])], sent_sem.at[link])

    end_count, mid_count = (sum(g % den < num for g in range(groups)) for num, den in SHARES)
    sent(2, 2 * line * groups)

    @pl.when(inner)
    def _():
        sent(0, 4 * groups - end_count)
        sent(1, 4 * groups - DIRECT + mid_count)

    @pl.when(jnp.logical_not(inner))
    def _():
        sent(0, 4 * groups - mid_count)
        sent(1, 2 * groups + DIRECT + end_count)


def on_device(noisy_clips, conv_first, conv_second, temporal):
    sections = lax.axis_size("segment")
    frames = lax.axis_size("frame")
    clips, frame_local, side, _, lanes = noisy_clips.shape
    half = lanes // 2
    cells = side * side
    if sections != 2 or half % 128 or frames != 16 or clips != 4 or frame_local != 1 or side % 16:
        return pipelined(noisy_clips, conv_first, conv_second, temporal)
    taps = conv_first.shape[1] + temporal.shape[1] + conv_second.shape[1]
    per_section = taps // temporal.shape[1]
    dma = pltpu.SemaphoreType.DMA
    vmem = pl.BlockSpec(memory_space=pltpu.VMEM)
    kind = jnp.bfloat16
    return pl.pallas_call(
        functools.partial(fused_kernel, frames),
        out_shape=pltpu.VMEM((clips, 1, side // 2, side, lanes), kind),
        in_specs=[pl.BlockSpec(memory_space=pl.ANY)] * 4,
        out_specs=vmem,
        scratch_shapes=[
            pltpu.VMEM((2 * taps, lanes, half), kind),
            pltpu.VMEM((clips, side, side, lanes), kind),
            pltpu.VMEM((3, clips, side + 2, side, lanes), kind),
            pltpu.VMEM((3, clips + 2, side + 2, side, lanes), kind),
            pltpu.VMEM((2, clips, cells, half), kind),
            pltpu.VMEM((2, clips, cells, half), kind),
            pltpu.VMEM((2, 2, cells, half), kind),
            pltpu.VMEM((2, 2, cells, half), kind),
            pltpu.VMEM((clips, cells, half), kind),
            pltpu.VMEM((clips, cells, half), kind),
            pltpu.VMEM((clips, cells, half), jnp.float32),
            pltpu.VMEM((2 * clips, side // 2, side, half), kind),
            dma((per_section,)),
            dma((5,)),
            dma((per_section + 1,)),
            dma((5, 2 * per_section)),
            dma((3,)),
            dma((3, clips)),
            dma((2, 3)),
            dma((2, clips)),
            dma((2,)),
        ],
        compiler_params=pltpu.CompilerParams(
            collective_id=0, has_side_effects=True, vmem_limit_bytes=58 * 1024 * 1024
        ),
    )(noisy_clips, conv_first, conv_second, temporal)


def solution(mesh):
    in_specs = (
        P(None, "frame", None, None, None),
        P("segment", None, "frame", None),
        P("segment", None, "frame", None),
        P("segment", None, "frame", None),
    )
    out_specs = P(None, "frame", "segment", None, None)
    return jax.shard_map(
        on_device, mesh=mesh, in_specs=in_specs, out_specs=out_specs, check_vma=False
    )
```

```python
import functools

import jax
import jax.numpy as jnp
from jax import lax
from jax.experimental import pallas as pl
from jax.experimental.pallas import tpu as pltpu
from jax.sharding import PartitionSpec as P

skip_scale = 0.7071067811865476
MESH = pl.DeviceIdType.MESH


def passed_along(shard, axis, by):
    length = lax.axis_size(axis)
    pairs = [(i, i + by) for i in range(length) if 0 <= i + by < length]
    return lax.ppermute(shard, axis, pairs)


def extended_2(cells, sides, width):
    for axis, dim in sides:
        count = lax.axis_size(axis)
        ends = count - 1
        head = lax.slice_in_dim(cells, 0, width, axis=dim)
        tail = lax.slice_in_dim(cells, cells.shape[dim] - width, cells.shape[dim], axis=dim)
        cells = jnp.concatenate(
            [
                lax.ppermute(tail, axis, [(i, (i + 1) % count) for i in range(ends)]),
                cells,
                lax.ppermute(head, axis, [((i + 1) % count, i) for i in range(ends)]),
            ],
            axis=dim,
        )
    return cells


def broadcast(shard, axis, root):
    mine = lax.axis_index(axis) == root
    return lax.psum(jnp.where(mine, shard, jnp.zeros_like(shard)), axis)


def spatial(field_in, kernel):
    extent = field_in.shape[1]
    channels = field_in.shape[3]
    padded = jnp.pad(field_in, ((0, 0), (1, 1), (1, 1), (0, 0)))
    accumulated = jnp.zeros((field_in.shape[0] * extent * extent, channels), jnp.float32)
    for row_shift in range(3):
        for col_shift in range(3):
            window = padded[
                :, row_shift : row_shift + extent, col_shift : col_shift + extent, :
            ].reshape(-1, channels)
            accumulated = accumulated + jnp.dot(
                window, kernel[3 * row_shift + col_shift], preferred_element_type=jnp.float32
            )
    return accumulated.reshape(field_in.shape)


def temporal_mix(extended, kernel, frame_local):
    channels = extended.shape[3]
    out_shape = (frame_local,) + extended.shape[1:]
    accumulated = jnp.zeros(out_shape, jnp.float32)
    for offset in range(3):
        window = extended[offset : offset + frame_local].reshape(-1, channels)
        accumulated = accumulated + jnp.dot(
            window, kernel[offset], preferred_element_type=jnp.float32
        ).reshape(out_shape)
    return accumulated


def pipelined(noisy_clips, conv_first, conv_second, temporal):
    sections = lax.axis_size("segment")
    segment_id = lax.axis_index("segment")
    first_full, second_full, time_full = (
        lax.all_gather(conv_first, "frame", axis=2, tiled=True),
        lax.all_gather(conv_second, "frame", axis=2, tiled=True),
        lax.all_gather(temporal, "frame", axis=2, tiled=True),
    )
    first_kernel = first_full[0]
    second_kernel = second_full[0]
    time_kernel = time_full[0]
    clip_count = noisy_clips.shape[0]
    frame_local = noisy_clips.shape[1]
    side_len = noisy_clips.shape[2]
    block_shape = noisy_clips.shape[1:]
    tick_count = clip_count + sections - 1
    half_sections = sections // 2
    is_up = segment_id >= half_sections
    store_depth = max(half_sections - 1, 1)
    side_store = jnp.zeros((store_depth,) + block_shape, jnp.bfloat16)
    out_store = jnp.zeros(noisy_clips.shape, jnp.bfloat16)
    prev_out = jnp.zeros(block_shape, jnp.bfloat16)

    def tick_step(carry, tick_index):
        prev_out, side_store, out_store = carry
        clip_now = tick_index - segment_id
        active = (clip_now >= 0) & (clip_now < clip_count)
        clip_slot = jnp.clip(clip_now, 0, clip_count - 1)
        own_input = lax.dynamic_index_in_dim(noisy_clips, clip_slot, 0, keepdims=False)
        received, side_store = passed_along((prev_out, side_store), "segment", 1)
        entering = jnp.where(segment_id == 0, own_input, received)
        written = (jnp.arange(store_depth) == segment_id - 1) & (segment_id < half_sections)
        side_store = jnp.where(written[:, None, None, None, None], entering[None], side_store)
        stack_slot = jnp.clip(sections - 2 - segment_id, 0, store_depth - 1)
        stored = lax.dynamic_index_in_dim(side_store, stack_slot, 0, keepdims=False)
        skip_feature = jnp.where(segment_id == sections - 1, own_input, stored)
        joined = (
            (entering.astype(jnp.float32) + skip_feature.astype(jnp.float32)) * skip_scale
        ).astype(jnp.bfloat16)
        section_in = jnp.where(is_up, joined, entering)
        activated = lax.cond(
            active,
            lambda: jax.nn.silu(spatial(section_in, first_kernel)).astype(jnp.bfloat16),
            lambda: jnp.zeros(block_shape, jnp.bfloat16),
        )
        extended = extended_2(activated, (("frame", 0),), 1)

        def second_pass():
            branch_sum = spatial(activated, second_kernel) + temporal_mix(
                extended, time_kernel, frame_local
            )
            return (section_in.astype(jnp.float32) + jax.nn.silu(branch_sum)).astype(jnp.bfloat16)

        section_out = lax.cond(active, second_pass, lambda: jnp.zeros(block_shape, jnp.bfloat16))
        finished = (jnp.arange(clip_count) == clip_slot) & active & (segment_id == sections - 1)
        out_store = jnp.where(finished[:, None, None, None, None], section_out[None], out_store)
        return ((section_out, side_store, out_store), None)

    final_carry, unused = lax.scan(
        tick_step, (prev_out, side_store, out_store), jnp.arange(tick_count, dtype=jnp.int32)
    )
    delivered = broadcast(final_carry[2], "segment", sections - 1)
    slab_rows = side_len // sections
    return lax.dynamic_slice_in_dim(delivered, segment_id * slab_rows, slab_rows, 2)


CODE, PACK, EVENTS = 16, 3, 127
ORDERS = (
    (
        131328, 6292483, 3149921, 1192209, 1323539, 3416115, 2236784, 409605,
        8397575, 8552784, 3507009, 541265, 5379364, 3544720, 3610513, 2462610,
        1575235, 4466259, 11575352, 2577418, 4567457, 5576971, 4597922, 1718540,
        3850326, 1784769, 10685767, 5720258, 1850563, 13642072, 4008477, 5851601,
        9776020, 2937418, 13851286, 4926871, 6010020, 11904332, 5103708, 6137569,
        14873072, 14938791, 243,
    ),
    (
        24583, 155905, 1060867, 1126660, 1208370, 1315635, 2176032, 336448,
        3493894, 8552832, 5325187, 541219, 1390390, 2396242, 9508630, 4428344,
        3773193, 10507032, 10560944, 4466353, 2597386, 10703897, 5573445, 2624582,
        12604954, 2736442, 870171, 12721211, 13653820, 2802504, 13712728, 1911625,
        9722322, 9841813, 9950026, 4938285, 11838555, 14703692, 11904333, 15752673,
        14872998, 14938791, 243,
    ),
    (
        131328, 1073504, 2101507, 266800, 7352609, 1258018, 1323811, 3417093,
        8405312, 5276289, 426833, 5375810, 3510309, 1413443, 3548818, 5457043,
        2561544, 1521492, 2666656, 10569016, 4609457, 1587465, 10619478, 4702219,
        836259, 2705466, 1687895, 12802074, 3869994, 13769755, 3943379, 5886025,
        4009108, 9837898, 13720215, 4953389, 5026980, 6071899, 5104352, 6141349,
        15902689, 15986915, 241,
    ),
    (
        24583, 155905, 1114896, 7352352, 2167300, 2233137, 1323525, 8401699,
        4261440, 8618625, 1397072, 4338724, 9458184, 9505091, 1455397, 9671191,
        3548966, 4462647, 11575379, 11641113, 5519400, 5612101, 2704906, 5677881,
        12782530, 12601100, 2802007, 1718797, 4837448, 3877720, 9722139, 9884188,
        13712428, 4857237, 13843757, 4938391, 11838555, 14703692, 5104294, 15902557,
        11904483, 14807283, 241,
    ),
)
DIRECT, SHARES = 0, ((1, 3), (1, 4))


def fused_kernel(
    frames,
    noisy_ref,
    first_ref,
    second_ref,
    time_ref,
    out_ref,
    w_ref,
    n_ref,
    xe,
    xa,
    a_send,
    a_recv,
    t_send,
    t_recv,
    e_mine,
    e_recv,
    acc_ref,
    o_full,
    local_sem,
    n_sem,
    y_sem,
    got_sem,
    sent_sem,
    a_sem,
    t_sem,
    e_sem,
    o_sem,
):
    clips, side, lanes = noisy_ref.shape[0], noisy_ref.shape[2], noisy_ref.shape[4]
    half = lanes // 2
    cells = side * side
    depth = first_ref.shape[2]
    width = time_ref.shape[1]
    rows_per_conv = first_ref.shape[1] // width
    per_section = 2 * rows_per_conv + 1
    taps = per_section * width
    groups = 2 * per_section
    line = frames // 4
    seg = lax.axis_index("segment")
    me = lax.axis_index("frame")
    slots = frames // line
    core, x_at, z_at, place = lax.rem(me, 2), lax.rem(me // 2, 2), me // slots, lax.rem(me, slots)
    peer = 1 - seg
    other = me + 1 - 2 * core
    slab_rows = side // 2

    def frame_of(x_place, z_place):
        return (z_place * 2 + x_place) * 2 + core

    x_peer = frame_of(1 - x_at, z_at)
    z_pair = z_at + 1 - 2 * lax.rem(z_at, 2)
    z_half = z_at // 2
    inner = lax.rem(z_at, 2) != z_half
    z_near, z_end = 2 - z_half, 3 - 3 * z_half
    far = (z_near, z_end)
    across = (x_peer, x_peer + 1 - 2 * core)

    barrier = pltpu.get_barrier_semaphore()
    near = [(seg, other)] + [(seg, f) for f in across]
    near += [(seg, frame_of(x_at, z)) for z in far + (z_pair,)]
    near += [(peer, f) for f in (me, other) + across]
    for target in near:
        pl.semaphore_signal(barrier, inc=1, device_id=target, device_id_type=MESH)

    def columns(which):
        return pl.ds(pl.multiple_of(which * half, half), half)

    def rows_of(owner):
        return pl.ds(pl.multiple_of(owner * depth, depth), depth)

    every = tuple(range(rows_per_conv))

    def part(j):
        if j < rows_per_conv:
            return first_ref, j * width
        if j == rows_per_conv:
            return time_ref, 0
        return second_ref, (j - rows_per_conv - 1) * width

    def local_copy(j):
        ref, start = part(j)
        return pltpu.make_async_copy(
            ref.at[0, pl.ds(start, width), :, columns(seg)],
            w_ref.at[pl.ds(seg * taps + j * width, width), rows_of(me)],
            local_sem.at[j],
        )

    def remote(src, dst, send, recv, device):
        return pltpu.make_async_remote_copy(
            src_ref=src,
            dst_ref=dst,
            send_sem=send,
            recv_sem=recv,
            device_id=device,
            device_id_type=MESH,
        )

    def take(ref, sem):
        pltpu.make_async_copy(ref, ref, sem).wait()

    def y_copy(j):
        ref, start = part(j)
        return remote(
            ref.at[0, pl.ds(start, width), :, columns(peer)],
            w_ref.at[pl.ds(seg * taps + j * width, width), rows_of(me)],
            y_sem.at[per_section],
            y_sem.at[j],
            (peer, me),
        )

    def slab(g, owner):
        return w_ref.at[pl.ds(g * width, width), rows_of(owner)]

    def some(g, count):
        return w_ref.at[pl.ds(g * width, width), pl.ds(0, count * depth)]

    own, crossed, lined, paired, rest = range(5)

    def give(g, owner, kind, link, target):
        ref = slab(g, owner)
        remote(ref, ref, sent_sem.at[link], got_sem.at[kind, g], (seg, target)).start()

    def give_core(g, owner):
        give(g, owner, own, 2, other)

    def round_own(g):
        section, j = g // per_section, lax.rem(g, per_section)

        @pl.when(seg == section)
        def _():
            take(slab(g, me), local_sem.at[j])

        @pl.when(seg != section)
        def _():
            take(slab(g, me), y_sem.at[j])

        give(g, me, crossed, 0, x_peer)
        give(g, me, lined, 1, frame_of(x_at, z_near))

        @pl.when(inner | (g < DIRECT))
        def _():
            give(g, me, lined, 1, frame_of(x_at, z_end))

        give(g, me, paired, 1, frame_of(x_at, z_pair))
        give_core(g, me)

    def crosses(g, is_inner):
        end, mid = (lax.rem(g, share[1]) < share[0] for share in SHARES)
        return jnp.where(is_inner, mid, end)

    def round_cross(g):
        take(some(g, 1), got_sem.at[crossed, g])

        @pl.when(crosses(g, inner))
        def _():
            give(g, x_peer, rest, 3, frame_of(x_at, z_pair))

        give_core(g, x_peer)

    def round_line(g):
        take(some(g, 2), got_sem.at[lined, g])

        @pl.when(inner & (g >= DIRECT))
        def _():
            give(g, frame_of(x_at, z_end), lined, 1, frame_of(x_at, z_pair))

        for z in far:
            give(g, frame_of(x_at, z), rest, 0, x_peer)
        for z in far:
            give_core(g, frame_of(x_at, z))

    def round_pair(g):
        take(some(g, 1), got_sem.at[paired, g])

        @pl.when(jnp.logical_not(crosses(g, jnp.logical_not(inner))))
        def _():
            give(g, frame_of(x_at, z_pair), rest, 4, x_peer)

        give_core(g, frame_of(x_at, z_pair))

    def round_rest(g):
        take(some(g, 3), got_sem.at[rest, g])
        for z in far + (z_pair,):
            give_core(g, frame_of(1 - x_at, z))

    def round_done(g):
        take(some(g, 2 * line), got_sem.at[own, g])

    def build(x, clip, value, where):
        width_of = value.shape[1]
        wide = value.astype(jnp.float32)
        place = lax.broadcasted_iota(jnp.int32, (cells, width_of), 0) % side
        shifted = (
            jnp.where(place == 0, 0.0, pltpu.roll(wide, 1, 0)).astype(jnp.bfloat16),
            value,
            jnp.where(place == side - 1, 0.0, pltpu.roll(wide, cells - 1, 0)).astype(jnp.bfloat16),
        )
        for dx in range(3):
            x[dx, clip, 1 : side + 1, :, where] = shifted[dx].reshape(side, side, width_of)

    def row_sum(x, clip, rows, base, total=None):
        for dy in rows:
            for dx in range(3):
                view = x[dx, clip, dy : dy + side].reshape(cells, lanes)
                term = jnp.dot(
                    view, w_ref[base + width * dy + dx], preferred_element_type=jnp.float32
                )
                total = term if total is None else total + term
        return total

    def silu(u):
        return u / (1.0 + jnp.exp(-u))

    def arrival(j):
        slot = jnp.where(j == 0, 0, jnp.where(j == 1, slots - 1, j - 1))
        slot = jnp.where(inner, slot, slots - 1 - j)
        return jnp.where(z_half == 0, slot, slots - 1 - slot)

    def noisy_local():
        return pltpu.make_async_copy(noisy_ref.at[place, 0], n_ref.at[place], n_sem.at[0])

    def send_noisy(part_at):
        @pl.when(part_at == 0)
        def _():
            remote(
                noisy_ref.at[lax.rem(other, slots), 0],
                n_ref.at[place],
                n_sem.at[4],
                n_sem.at[1],
                (seg, other),
            ).start()

        target = jnp.where(part_at == 0, across[0], across[1])
        remote(
            noisy_ref.at[lax.rem(target, slots), 0, :, :, columns(seg)],
            n_ref.at[place, :, :, columns(seg)],
            n_sem.at[4],
            n_sem.at[2],
            (seg, target),
        ).start()

    def relay_noisy(unused):
        take(n_ref.at[0], n_sem.at[2])
        for target in across:
            ref = n_ref.at[lax.rem(target, slots), :, :, columns(seg)]
            remote(ref, ref, n_sem.at[4], n_sem.at[3], (peer, me)).start()

    def build_noisy(j):
        @pl.when(j == 0)
        def _():
            for i in (0, 1, 3):
                take(n_ref.at[0], n_sem.at[i])

        slot = arrival(j)
        build(xe, slot, n_ref[slot].reshape(cells, lanes), slice(None))

    def a_copy(s, slot):
        return remote(
            a_send.at[s, slot], a_recv.at[s, slot], a_sem.at[2, 0], a_sem.at[s, slot], (peer, me)
        )

    def e_copy(slot):
        return remote(e_mine.at[slot], e_recv.at[slot], e_sem.at[1, 0], e_sem.at[0, slot], (peer, me))

    sends_on = (z_at < line - 1, z_at > 0)
    takes_on = (z_at > 0, z_at < line - 1)

    def t_copy(s, way):
        target = me + slots if way == 0 else me - slots
        return remote(
            t_send.at[way, s],
            t_recv.at[way, s],
            t_sem.at[way, 2],
            t_sem.at[way, s],
            (seg, lax.rem(target + frames, frames)),
        )

    def o_copy(slot, rows):
        return remote(
            o_full.at[2 * slot + rows],
            out_ref.at[place, 0, :, :, columns(seg)],
            o_sem.at[1],
            o_sem.at[0],
            (rows, z_at * slots + slot),
        )

    def first_rows(turn):
        s, slot = lax.div(turn, slots), arrival(lax.rem(turn, slots))
        total = row_sum(xe, slot, every, s * taps)
        a_send[s, slot] = silu(total).astype(jnp.bfloat16)
        a_copy(s, slot).start()

    def take_active(turn):
        s, slot = lax.div(turn, slots), arrival(lax.rem(turn, slots))
        a_copy(s, slot).wait_recv()
        build(xa, slot + 1, a_send[s, slot], columns(seg))
        build(xa, slot + 1, a_recv[s, slot], columns(peer))

    def mixed(s, slot, k):
        view = xa[1, slot + k, 1 : side + 1].reshape(cells, lanes)
        return jnp.dot(
            view, w_ref[s * taps + rows_per_conv * width + k], preferred_element_type=jnp.float32
        )

    def terms(turn):
        s, slot = lax.div(turn, slots), arrival(lax.rem(turn, slots))
        view = xa[1, slot + 1, 1 : side + 1].reshape(cells, lanes)
        base = s * taps + rows_per_conv * width
        for way, edge_slot in ((1, 0), (0, slots - 1)):

            @pl.when((slot == edge_slot) & sends_on[way])
            def _():
                t_send[way, s] = jnp.dot(
                    view, w_ref[base + 2 * way], preferred_element_type=jnp.float32
                ).astype(jnp.bfloat16)
                t_copy(s, way).start()

    def second_sum(s, slot, rows, with_time, total=None):
        base = s * taps + (rows_per_conv + 1) * width
        total = row_sum(xa, slot + 1, rows, base, total)
        if with_time:
            for k in range(width):
                total = total + mixed(s, slot, k)
        return total

    def early_rows(j):
        slot = arrival(j)
        acc_ref[slot] = second_sum(1, slot, every[:-1], False)

    def finished(s, slot):
        for way, edge_slot in ((0, 0), (1, slots - 1)):

            @pl.when(takes_on[way] & (slot == edge_slot))
            def _():
                t_copy(s, way).wait_recv()
                acc_ref[slot] = acc_ref[slot] + t_recv[way, s].astype(jnp.float32)

        return silu(acc_ref[slot])

    def end_first(j):
        slot = arrival(j)
        acc_ref[slot] = second_sum(0, slot, every, True)
        mine = n_ref[slot, :, :, columns(seg)].reshape(cells, half).astype(jnp.float32)
        out = (mine + finished(0, slot)).astype(jnp.bfloat16)
        e_mine[slot] = ((out.astype(jnp.float32) + mine) * skip_scale).astype(jnp.bfloat16)
        e_copy(slot).start()

    def take_entering(j):
        slot = arrival(j)
        e_copy(slot).wait_recv()
        build(xe, slot, e_mine[slot], columns(seg))
        build(xe, slot, e_recv[slot], columns(peer))

    def end_second(j):
        slot = arrival(j)
        acc_ref[slot] = second_sum(1, slot, every[-1:], True, acc_ref[slot])
        out = (e_mine[slot].astype(jnp.float32) + finished(1, slot)).astype(jnp.bfloat16)
        full = out.reshape(2, slab_rows, side, half)
        for rows_at in range(2):
            o_full[2 * slot + rows_at] = full[rows_at]
        o_copy(slot, peer).start()

        @pl.when(slot != place)
        def _():
            o_copy(slot, seg).start()

        @pl.when(slot == place)
        def _():
            out_ref[place, 0, :, :, columns(seg)] = o_full[2 * slot + seg]

    works = (
        round_own,
        round_cross,
        round_line,
        round_pair,
        round_rest,
        round_done,
        send_noisy,
        relay_noisy,
        build_noisy,
        first_rows,
        take_active,
        terms,
        end_first,
        take_entering,
        early_rows,
        end_second,
    )

    words = []
    for codes in zip(*ORDERS):
        ends, inners = (jnp.where(seg == 0, codes[n], codes[n + 1]) for n in (0, 2))
        words.append(jnp.where(inner, inners, ends))

    def run(some_works, kind, turn, low=0):
        if len(some_works) == 1:
            some_works[0](turn)
            return
        cut = len(some_works) // 2

        @pl.when(kind < low + cut)
        def _():
            run(some_works[:cut], kind, turn, low)

        @pl.when(kind >= low + cut)
        def _():
            run(some_works[cut:], kind, turn, low + cut)

    for j in range(per_section):
        local_copy(j).start()

    noisy_local().start()
    edge = jnp.zeros((side, lanes), jnp.bfloat16)
    for x in (xe, xa):
        for dx in range(3):

            @pl.loop(0, x.shape[1])
            def _(slot):
                x[dx, slot, 0] = edge
                x[dx, slot, side + 1] = edge

    for slot in (0, slots + 1):
        xa[1, slot, 1 : side + 1] = jnp.zeros((side, side, lanes), jnp.bfloat16)

    pl.semaphore_wait(barrier, len(near))

    for j in range(per_section):
        y_copy(j).start()

    @pl.loop(0, EVENTS)
    def _(i):
        at, level = i // PACK, words
        while len(level) > 1:
            odd = lax.rem(at, 2) == 1
            level = [
                jnp.where(odd, level[n + 1], level[n]) if n + 1 < len(level) else level[n]
                for n in range(0, len(level), 2)
            ]
            at = at // 2
        code = level[0]
        for n in range(1, PACK):
            code = jnp.where(lax.rem(i, PACK) == n, level[0] // (CODE * CODE) ** n, code)
        code = lax.rem(code, CODE * CODE)
        run(works, code // CODE, lax.rem(code, CODE))

    for i in range(2):
        take(o_full.at[pl.ds(0, 2 * slots - 1)], o_sem.at[i])
    take(n_ref.at[pl.ds(0, 3)], n_sem.at[4])
    take(e_mine, e_sem.at[1, 0])
    take(a_send, a_sem.at[2, 0])
    for way in range(2):

        @pl.when(sends_on[way])
        def _():
            take(t_send.at[way], t_sem.at[way, 2])

    take(w_ref.at[pl.ds(0, taps), pl.ds(0, depth)], y_sem.at[per_section])
    def sent(link, count):
        rows = count * width * depth
        fits = [k for k in range(1, 2 * taps + 1) if rows % (16 * k) == 0 and rows // k <= lanes]
        take(w_ref.at[pl.ds(0, fits[0]), pl.ds(0, rows // fits[0])], sent_sem.at[link])

    end_count, mid_count = (sum(g % den < num for g in range(groups)) for num, den in SHARES)
    sent(0, 3 * groups)
    sent(2, 2 * line * groups)

    @pl.when(inner)
    def _():
        sent(1, 4 * groups - DIRECT)
        sent(3, mid_count)
        sent(4, groups - end_count)

    @pl.when(jnp.logical_not(inner))
    def _():
        sent(1, 2 * groups + DIRECT)
        sent(3, end_count)
        sent(4, groups - mid_count)


def on_device(noisy_clips, conv_first, conv_second, temporal):
    sections = lax.axis_size("segment")
    frames = lax.axis_size("frame")
    clips, frame_local, side, _, lanes = noisy_clips.shape
    half = lanes // 2
    cells = side * side
    if sections != 2 or half % 128 or frames != 16 or clips != 4 or frame_local != 1 or side % 16:
        return pipelined(noisy_clips, conv_first, conv_second, temporal)
    taps = conv_first.shape[1] + temporal.shape[1] + conv_second.shape[1]
    per_section = taps // temporal.shape[1]
    dma = pltpu.SemaphoreType.DMA
    vmem = pl.BlockSpec(memory_space=pltpu.VMEM)
    kind = jnp.bfloat16
    return pl.pallas_call(
        functools.partial(fused_kernel, frames),
        out_shape=pltpu.VMEM((clips, 1, side // 2, side, lanes), kind),
        in_specs=[pl.BlockSpec(memory_space=pl.ANY)] * 4,
        out_specs=vmem,
        scratch_shapes=[
            pltpu.VMEM((2 * taps, lanes, half), kind),
            pltpu.VMEM((clips, side, side, lanes), kind),
            pltpu.VMEM((3, clips, side + 2, side, lanes), kind),
            pltpu.VMEM((3, clips + 2, side + 2, side, lanes), kind),
            pltpu.VMEM((2, clips, cells, half), kind),
            pltpu.VMEM((2, clips, cells, half), kind),
            pltpu.VMEM((2, 2, cells, half), kind),
            pltpu.VMEM((2, 2, cells, half), kind),
            pltpu.VMEM((clips, cells, half), kind),
            pltpu.VMEM((clips, cells, half), kind),
            pltpu.VMEM((clips, cells, half), jnp.float32),
            pltpu.VMEM((2 * clips, side // 2, side, half), kind),
            dma((per_section,)),
            dma((5,)),
            dma((per_section + 1,)),
            dma((5, 2 * per_section)),
            dma((5,)),
            dma((3, clips)),
            dma((2, 3)),
            dma((2, clips)),
            dma((2,)),
        ],
        compiler_params=pltpu.CompilerParams(
            collective_id=0, has_side_effects=True, vmem_limit_bytes=58 * 1024 * 1024
        ),
    )(noisy_clips, conv_first, conv_second, temporal)


def solution(mesh):
    in_specs = (
        P(None, "frame", None, None, None),
        P("segment", None, "frame", None),
        P("segment", None, "frame", None),
        P("segment", None, "frame", None),
    )
    out_specs = P(None, "frame", "segment", None, None)
    return jax.shard_map(
        on_device, mesh=mesh, in_specs=in_specs, out_specs=out_specs, check_vma=False
    )
```

```python
import functools

import jax
import jax.numpy as jnp
from jax import lax
from jax.experimental import pallas as pl
from jax.experimental.pallas import tpu as pltpu
from jax.sharding import PartitionSpec as P

skip_scale = 0.7071067811865476
MESH = pl.DeviceIdType.MESH


def passed_along(shard, axis, by):
    length = lax.axis_size(axis)
    pairs = [(i, i + by) for i in range(length) if 0 <= i + by < length]
    return lax.ppermute(shard, axis, pairs)


def extended_2(cells, sides, width):
    for axis, dim in sides:
        count = lax.axis_size(axis)
        ends = count - 1
        head = lax.slice_in_dim(cells, 0, width, axis=dim)
        tail = lax.slice_in_dim(cells, cells.shape[dim] - width, cells.shape[dim], axis=dim)
        cells = jnp.concatenate(
            [
                lax.ppermute(tail, axis, [(i, (i + 1) % count) for i in range(ends)]),
                cells,
                lax.ppermute(head, axis, [((i + 1) % count, i) for i in range(ends)]),
            ],
            axis=dim,
        )
    return cells


def broadcast(shard, axis, root):
    mine = lax.axis_index(axis) == root
    return lax.psum(jnp.where(mine, shard, jnp.zeros_like(shard)), axis)


def spatial(field_in, kernel):
    extent = field_in.shape[1]
    channels = field_in.shape[3]
    padded = jnp.pad(field_in, ((0, 0), (1, 1), (1, 1), (0, 0)))
    accumulated = jnp.zeros((field_in.shape[0] * extent * extent, channels), jnp.float32)
    for row_shift in range(3):
        for col_shift in range(3):
            window = padded[
                :, row_shift : row_shift + extent, col_shift : col_shift + extent, :
            ].reshape(-1, channels)
            accumulated = accumulated + jnp.dot(
                window, kernel[3 * row_shift + col_shift], preferred_element_type=jnp.float32
            )
    return accumulated.reshape(field_in.shape)


def temporal_mix(extended, kernel, frame_local):
    channels = extended.shape[3]
    out_shape = (frame_local,) + extended.shape[1:]
    accumulated = jnp.zeros(out_shape, jnp.float32)
    for offset in range(3):
        window = extended[offset : offset + frame_local].reshape(-1, channels)
        accumulated = accumulated + jnp.dot(
            window, kernel[offset], preferred_element_type=jnp.float32
        ).reshape(out_shape)
    return accumulated


def pipelined(noisy_clips, conv_first, conv_second, temporal):
    sections = lax.axis_size("segment")
    segment_id = lax.axis_index("segment")
    first_full, second_full, time_full = (
        lax.all_gather(conv_first, "frame", axis=2, tiled=True),
        lax.all_gather(conv_second, "frame", axis=2, tiled=True),
        lax.all_gather(temporal, "frame", axis=2, tiled=True),
    )
    first_kernel = first_full[0]
    second_kernel = second_full[0]
    time_kernel = time_full[0]
    clip_count = noisy_clips.shape[0]
    frame_local = noisy_clips.shape[1]
    side_len = noisy_clips.shape[2]
    block_shape = noisy_clips.shape[1:]
    tick_count = clip_count + sections - 1
    half_sections = sections // 2
    is_up = segment_id >= half_sections
    store_depth = max(half_sections - 1, 1)
    side_store = jnp.zeros((store_depth,) + block_shape, jnp.bfloat16)
    out_store = jnp.zeros(noisy_clips.shape, jnp.bfloat16)
    prev_out = jnp.zeros(block_shape, jnp.bfloat16)

    def tick_step(carry, tick_index):
        prev_out, side_store, out_store = carry
        clip_now = tick_index - segment_id
        active = (clip_now >= 0) & (clip_now < clip_count)
        clip_slot = jnp.clip(clip_now, 0, clip_count - 1)
        own_input = lax.dynamic_index_in_dim(noisy_clips, clip_slot, 0, keepdims=False)
        received, side_store = passed_along((prev_out, side_store), "segment", 1)
        entering = jnp.where(segment_id == 0, own_input, received)
        written = (jnp.arange(store_depth) == segment_id - 1) & (segment_id < half_sections)
        side_store = jnp.where(written[:, None, None, None, None], entering[None], side_store)
        stack_slot = jnp.clip(sections - 2 - segment_id, 0, store_depth - 1)
        stored = lax.dynamic_index_in_dim(side_store, stack_slot, 0, keepdims=False)
        skip_feature = jnp.where(segment_id == sections - 1, own_input, stored)
        joined = (
            (entering.astype(jnp.float32) + skip_feature.astype(jnp.float32)) * skip_scale
        ).astype(jnp.bfloat16)
        section_in = jnp.where(is_up, joined, entering)
        activated = lax.cond(
            active,
            lambda: jax.nn.silu(spatial(section_in, first_kernel)).astype(jnp.bfloat16),
            lambda: jnp.zeros(block_shape, jnp.bfloat16),
        )
        extended = extended_2(activated, (("frame", 0),), 1)

        def second_pass():
            branch_sum = spatial(activated, second_kernel) + temporal_mix(
                extended, time_kernel, frame_local
            )
            return (section_in.astype(jnp.float32) + jax.nn.silu(branch_sum)).astype(jnp.bfloat16)

        section_out = lax.cond(active, second_pass, lambda: jnp.zeros(block_shape, jnp.bfloat16))
        finished = (jnp.arange(clip_count) == clip_slot) & active & (segment_id == sections - 1)
        out_store = jnp.where(finished[:, None, None, None, None], section_out[None], out_store)
        return ((section_out, side_store, out_store), None)

    final_carry, unused = lax.scan(
        tick_step, (prev_out, side_store, out_store), jnp.arange(tick_count, dtype=jnp.int32)
    )
    delivered = broadcast(final_carry[2], "segment", sections - 1)
    slab_rows = side_len // sections
    return lax.dynamic_slice_in_dim(delivered, segment_id * slab_rows, slab_rows, 2)


CODE, PACK, EVENTS = 16, 3, 127
ORDERS = (
    (
        131328, 6292483, 3149921, 1192209, 1323539, 3416115, 2236784, 409605,
        8402183, 4292944, 8594306, 541265, 5379364, 3544720, 3610513, 2462610,
        1575235, 4466259, 10500106, 3757232, 11641127, 1641285, 4629077, 2628108,
        12697686, 870185, 1784483, 1850306, 3982167, 5777992, 13647177, 9722141,
        9818411, 13781548, 5909910, 9950027, 10767451, 5070004, 10837472, 10936757,
        15786737, 14938791, 243,
    ),
    (
        24583, 155905, 266243, 3215664, 1208370, 1315635, 2176032, 336448,
        3493894, 8552832, 5325187, 541219, 1390390, 2396242, 9508630, 4428344,
        9648393, 10507032, 10596389, 4466353, 2597386, 10703897, 5573445, 2624582,
        3823130, 4663744, 3870145, 5708827, 13647042, 2802504, 13719613, 13773641,
        9722141, 2922133, 9950026, 10770989, 5983156, 5027237, 5103708, 14853857,
        11006301, 15983602, 240,
    ),
    (
        131328, 1073504, 2101507, 266800, 7352609, 1258018, 3351301, 3417108,
        8405312, 5276289, 8586833, 1378114, 3482962, 4428176, 3548818, 541843,
        595539, 1521447, 11575380, 4536360, 11641173, 2693190, 1653078, 723618,
        4694842, 5704898, 4729537, 5770688, 3877827, 1788186, 5886930, 3943574,
        13670172, 2987082, 5905725, 4953553, 5004198, 10871388, 5104053, 14726308,
        15902557, 15790563, 243,
    ),
    (
        24583, 155905, 1114896, 7352352, 2167300, 2233137, 1323525, 8401699,
        4261440, 8618625, 1397072, 4338724, 9458184, 9505091, 1455397, 9671191,
        3548966, 4462647, 11575379, 10572825, 3680433, 5612101, 2704906, 5677881,
        12782530, 12601100, 2802007, 1718797, 5785928, 3877842, 9853211, 9818396,
        1915948, 9752650, 5913901, 9915347, 10898523, 5104220, 6153127, 15905956,
        10875104, 14807989, 241,
    ),
)
DIRECT, SHARES = 0, ((1, 3), (1, 4))


def fused_kernel(
    frames,
    noisy_ref,
    first_ref,
    second_ref,
    time_ref,
    out_ref,
    w_ref,
    n_ref,
    xe,
    xa,
    a_send,
    a_recv,
    t_send,
    t_recv,
    e_mine,
    e_recv,
    acc_ref,
    o_full,
    local_sem,
    n_sem,
    y_sem,
    got_sem,
    sent_sem,
    a_sem,
    t_sem,
    e_sem,
    o_sem,
):
    clips, side, lanes = noisy_ref.shape[0], noisy_ref.shape[2], noisy_ref.shape[4]
    half = lanes // 2
    cells = side * side
    depth = first_ref.shape[2]
    width = time_ref.shape[1]
    rows_per_conv = first_ref.shape[1] // width
    per_section = 2 * rows_per_conv + 1
    taps = per_section * width
    groups = 2 * per_section
    line = frames // 4
    seg = lax.axis_index("segment")
    me = lax.axis_index("frame")
    slots = frames // line
    core, x_at, z_at, place = lax.rem(me, 2), lax.rem(me // 2, 2), me // slots, lax.rem(me, slots)
    peer = 1 - seg
    other = me + 1 - 2 * core
    slab_rows = side // 2

    def frame_of(x_place, z_place):
        return (z_place * 2 + x_place) * 2 + core

    x_peer = frame_of(1 - x_at, z_at)
    z_pair = z_at + 1 - 2 * lax.rem(z_at, 2)
    z_half = z_at // 2
    inner = lax.rem(z_at, 2) != z_half
    z_near, z_end = 2 - z_half, 3 - 3 * z_half
    far = (z_near, z_end)
    across = (x_peer, x_peer + 1 - 2 * core)

    barrier = pltpu.get_barrier_semaphore()
    near = [(seg, other)] + [(seg, f) for f in across]
    near += [(seg, frame_of(x_at, z)) for z in far + (z_pair,)]
    near += [(peer, f) for f in (me, other) + across]
    for target in near:
        pl.semaphore_signal(barrier, inc=1, device_id=target, device_id_type=MESH)

    def columns(which):
        return pl.ds(pl.multiple_of(which * half, half), half)

    def rows_of(owner):
        return pl.ds(pl.multiple_of(owner * depth, depth), depth)

    every = tuple(range(rows_per_conv))

    def part(j):
        if j < rows_per_conv:
            return first_ref, j * width
        if j == rows_per_conv:
            return time_ref, 0
        return second_ref, (j - rows_per_conv - 1) * width

    def local_copy(j):
        ref, start = part(j)
        return pltpu.make_async_copy(
            ref.at[0, pl.ds(start, width), :, columns(seg)],
            w_ref.at[pl.ds(seg * taps + j * width, width), rows_of(me)],
            local_sem.at[j],
        )

    def remote(src, dst, send, recv, device):
        return pltpu.make_async_remote_copy(
            src_ref=src,
            dst_ref=dst,
            send_sem=send,
            recv_sem=recv,
            device_id=device,
            device_id_type=MESH,
        )

    def take(ref, sem):
        pltpu.make_async_copy(ref, ref, sem).wait()

    def y_copy(j):
        ref, start = part(j)
        return remote(
            ref.at[0, pl.ds(start, width), :, columns(peer)],
            w_ref.at[pl.ds(seg * taps + j * width, width), rows_of(me)],
            y_sem.at[per_section],
            y_sem.at[j],
            (peer, me),
        )

    def slab(g, owner):
        return w_ref.at[pl.ds(g * width, width), rows_of(owner)]

    def some(g, count):
        return w_ref.at[pl.ds(g * width, width), pl.ds(0, count * depth)]

    own, crossed, lined, paired, rest = range(5)

    def give(g, owner, kind, link, target):
        ref = slab(g, owner)
        remote(ref, ref, sent_sem.at[link], got_sem.at[kind, g], (seg, target)).start()

    def give_core(g, owner):
        give(g, owner, own, 2, other)

    def round_own(g):
        section, j = g // per_section, lax.rem(g, per_section)

        @pl.when(seg == section)
        def _():
            take(slab(g, me), local_sem.at[j])

        @pl.when(seg != section)
        def _():
            take(slab(g, me), y_sem.at[j])

        give(g, me, crossed, 0, x_peer)
        give(g, me, lined, 1, frame_of(x_at, z_near))

        @pl.when(inner | (g < DIRECT))
        def _():
            give(g, me, lined, 1, frame_of(x_at, z_end))

        give(g, me, paired, 1, frame_of(x_at, z_pair))
        give_core(g, me)

    def crosses(g, is_inner):
        end, mid = (lax.rem(g, share[1]) < share[0] for share in SHARES)
        return jnp.where(is_inner, mid, end)

    def round_cross(g):
        take(some(g, 1), got_sem.at[crossed, g])

        @pl.when(crosses(g, inner))
        def _():
            give(g, x_peer, rest, 3, frame_of(x_at, z_pair))

        give_core(g, x_peer)

    def round_line(g):
        take(some(g, 2), got_sem.at[lined, g])

        @pl.when(inner & (g >= DIRECT))
        def _():
            give(g, frame_of(x_at, z_end), lined, 1, frame_of(x_at, z_pair))

        for z in far:
            give(g, frame_of(x_at, z), rest, 0, x_peer)
        for z in far:
            give_core(g, frame_of(x_at, z))

    def round_pair(g):
        take(some(g, 1), got_sem.at[paired, g])

        @pl.when(jnp.logical_not(crosses(g, jnp.logical_not(inner))))
        def _():
            give(g, frame_of(x_at, z_pair), rest, 4, x_peer)

        give_core(g, frame_of(x_at, z_pair))

    def round_rest(g):
        take(some(g, 3), got_sem.at[rest, g])
        for z in far + (z_pair,):
            give_core(g, frame_of(1 - x_at, z))

    def round_done(g):
        take(some(g, 2 * line), got_sem.at[own, g])

    def build(x, clip, value, where):
        width_of = value.shape[1]
        wide = value.astype(jnp.float32)
        place = lax.broadcasted_iota(jnp.int32, (cells, width_of), 0) % side
        shifted = (
            jnp.where(place == 0, 0.0, pltpu.roll(wide, 1, 0)).astype(jnp.bfloat16),
            value,
            jnp.where(place == side - 1, 0.0, pltpu.roll(wide, cells - 1, 0)).astype(jnp.bfloat16),
        )
        for dx in range(3):
            x[dx, clip, 1 : side + 1, :, where] = shifted[dx].reshape(side, side, width_of)

    def row_sum(x, clip, rows, base, total=None):
        for dy in rows:
            for dx in range(3):
                view = x[dx, clip, dy : dy + side].reshape(cells, lanes)
                term = jnp.dot(
                    view, w_ref[base + width * dy + dx], preferred_element_type=jnp.float32
                )
                total = term if total is None else total + term
        return total

    def silu(u):
        return u / (1.0 + jnp.exp(-u))

    def arrival(j):
        slot = jnp.where(j == 0, 0, jnp.where(j == 1, slots - 1, j - 1))
        slot = jnp.where(inner, slot, slots - 1 - j)
        return jnp.where(z_half == 0, slot, slots - 1 - slot)

    def noisy_local():
        return pltpu.make_async_copy(noisy_ref.at[place, 0], n_ref.at[place], n_sem.at[0])

    def send_noisy(part_at):
        @pl.when(part_at == 0)
        def _():
            remote(
                noisy_ref.at[lax.rem(other, slots), 0],
                n_ref.at[place],
                n_sem.at[4],
                n_sem.at[1],
                (seg, other),
            ).start()

        target = jnp.where(part_at == 0, across[0], across[1])
        remote(
            noisy_ref.at[lax.rem(target, slots), 0, :, :, columns(seg)],
            n_ref.at[place, :, :, columns(seg)],
            n_sem.at[4],
            n_sem.at[2],
            (seg, target),
        ).start()

    def relay_noisy(unused):
        take(n_ref.at[0], n_sem.at[2])
        for target in across:
            ref = n_ref.at[lax.rem(target, slots), :, :, columns(seg)]
            remote(ref, ref, n_sem.at[4], n_sem.at[3], (peer, me)).start()

    def build_noisy(j):
        @pl.when(j == 0)
        def _():
            for i in (0, 1, 3):
                take(n_ref.at[0], n_sem.at[i])

        slot = arrival(j)
        build(xe, slot, n_ref[slot].reshape(cells, lanes), slice(None))

    def a_copy(s, slot):
        return remote(
            a_send.at[s, slot], a_recv.at[s, slot], a_sem.at[2, 0], a_sem.at[s, slot], (peer, me)
        )

    def e_copy(slot):
        return remote(e_mine.at[slot], e_recv.at[slot], e_sem.at[1, 0], e_sem.at[0, slot], (peer, me))

    sends_on = (z_at < line - 1, z_at > 0)
    takes_on = (z_at > 0, z_at < line - 1)

    def t_copy(s, way):
        target = me + slots if way == 0 else me - slots
        return remote(
            t_send.at[way, s],
            t_recv.at[way, s],
            t_sem.at[way, 2],
            t_sem.at[way, s],
            (seg, lax.rem(target + frames, frames)),
        )

    def o_copy(slot, rows):
        return remote(
            o_full.at[2 * slot + rows],
            out_ref.at[place, 0, :, :, columns(seg)],
            o_sem.at[1],
            o_sem.at[0],
            (rows, z_at * slots + slot),
        )

    def first_rows(turn):
        s, slot = lax.div(turn, slots), arrival(lax.rem(turn, slots))
        total = row_sum(xe, slot, every, s * taps)
        a_send[s, slot] = silu(total).astype(jnp.bfloat16)
        a_copy(s, slot).start()

    def take_active(turn):
        s, slot = lax.div(turn, slots), arrival(lax.rem(turn, slots))
        a_copy(s, slot).wait_recv()
        build(xa, slot + 1, a_send[s, slot], columns(seg))
        build(xa, slot + 1, a_recv[s, slot], columns(peer))

    def mixed(s, slot, k):
        view = xa[1, slot + k, 1 : side + 1].reshape(cells, lanes)
        return jnp.dot(
            view, w_ref[s * taps + rows_per_conv * width + k], preferred_element_type=jnp.float32
        )

    def terms(turn):
        s, slot = lax.div(turn, slots), arrival(lax.rem(turn, slots))
        view = xa[1, slot + 1, 1 : side + 1].reshape(cells, lanes)
        base = s * taps + rows_per_conv * width
        for way, edge_slot in ((1, 0), (0, slots - 1)):

            @pl.when((slot == edge_slot) & sends_on[way])
            def _():
                t_send[way, s] = jnp.dot(
                    view, w_ref[base + 2 * way], preferred_element_type=jnp.float32
                ).astype(jnp.bfloat16)
                t_copy(s, way).start()

    def second_sum(s, slot, rows, with_time, total=None):
        base = s * taps + (rows_per_conv + 1) * width
        total = row_sum(xa, slot + 1, rows, base, total)
        if with_time:
            for k in range(width):
                total = total + mixed(s, slot, k)
        return total

    def early_rows(j):
        slot = arrival(j)
        acc_ref[slot] = second_sum(1, slot, every[:-1], False)

    def finished(s, slot):
        for way, edge_slot in ((0, 0), (1, slots - 1)):

            @pl.when(takes_on[way] & (slot == edge_slot))
            def _():
                t_copy(s, way).wait_recv()
                acc_ref[slot] = acc_ref[slot] + t_recv[way, s].astype(jnp.float32)

        return silu(acc_ref[slot])

    def end_first(j):
        slot = arrival(j)
        acc_ref[slot] = second_sum(0, slot, every, True)
        mine = n_ref[slot, :, :, columns(seg)].reshape(cells, half).astype(jnp.float32)
        out = (mine + finished(0, slot)).astype(jnp.bfloat16)
        e_mine[slot] = ((out.astype(jnp.float32) + mine) * skip_scale).astype(jnp.bfloat16)
        e_copy(slot).start()

    def take_entering(j):
        slot = arrival(j)
        e_copy(slot).wait_recv()
        build(xe, slot, e_mine[slot], columns(seg))
        build(xe, slot, e_recv[slot], columns(peer))

    def end_second(j):
        slot = arrival(j)
        acc_ref[slot] = second_sum(1, slot, every[-1:], True, acc_ref[slot])
        out = (e_mine[slot].astype(jnp.float32) + finished(1, slot)).astype(jnp.bfloat16)
        full = out.reshape(2, slab_rows, side, half)
        for rows_at in range(2):
            o_full[2 * slot + rows_at] = full[rows_at]
        o_copy(slot, peer).start()

        @pl.when(slot != place)
        def _():
            o_copy(slot, seg).start()

        @pl.when(slot == place)
        def _():
            out_ref[place, 0, :, :, columns(seg)] = o_full[2 * slot + seg]

    works = (
        round_own,
        round_cross,
        round_line,
        round_pair,
        round_rest,
        round_done,
        send_noisy,
        relay_noisy,
        build_noisy,
        first_rows,
        take_active,
        terms,
        end_first,
        take_entering,
        early_rows,
        end_second,
    )

    words = []
    for codes in zip(*ORDERS):
        ends, inners = (jnp.where(seg == 0, codes[n], codes[n + 1]) for n in (0, 2))
        words.append(jnp.where(inner, inners, ends))

    def run(some_works, kind, turn, low=0):
        if len(some_works) == 1:
            some_works[0](turn)
            return
        cut = len(some_works) // 2

        @pl.when(kind < low + cut)
        def _():
            run(some_works[:cut], kind, turn, low)

        @pl.when(kind >= low + cut)
        def _():
            run(some_works[cut:], kind, turn, low + cut)

    for j in range(per_section):
        local_copy(j).start()

    noisy_local().start()
    edge = jnp.zeros((side, lanes), jnp.bfloat16)
    for x in (xe, xa):
        for dx in range(3):

            @pl.loop(0, x.shape[1])
            def _(slot):
                x[dx, slot, 0] = edge
                x[dx, slot, side + 1] = edge

    for slot in (0, slots + 1):
        xa[1, slot, 1 : side + 1] = jnp.zeros((side, side, lanes), jnp.bfloat16)

    pl.semaphore_wait(barrier, len(near))

    for j in range(per_section):
        y_copy(j).start()

    @pl.loop(0, EVENTS)
    def _(i):
        at, level = i // PACK, words
        while len(level) > 1:
            odd = lax.rem(at, 2) == 1
            level = [
                jnp.where(odd, level[n + 1], level[n]) if n + 1 < len(level) else level[n]
                for n in range(0, len(level), 2)
            ]
            at = at // 2
        code = level[0]
        for n in range(1, PACK):
            code = jnp.where(lax.rem(i, PACK) == n, level[0] // (CODE * CODE) ** n, code)
        code = lax.rem(code, CODE * CODE)
        run(works, code // CODE, lax.rem(code, CODE))

    for i in range(2):
        take(o_full.at[pl.ds(0, 2 * slots - 1)], o_sem.at[i])
    take(n_ref.at[pl.ds(0, 3)], n_sem.at[4])
    take(e_mine, e_sem.at[1, 0])
    take(a_send, a_sem.at[2, 0])
    for way in range(2):

        @pl.when(sends_on[way])
        def _():
            take(t_send.at[way], t_sem.at[way, 2])

    take(w_ref.at[pl.ds(0, taps), pl.ds(0, depth)], y_sem.at[per_section])
    def sent(link, count):
        rows = count * width * depth
        fits = [k for k in range(1, 2 * taps + 1) if rows % (16 * k) == 0 and rows // k <= lanes]
        take(w_ref.at[pl.ds(0, fits[0]), pl.ds(0, rows // fits[0])], sent_sem.at[link])

    end_count, mid_count = (sum(g % den < num for g in range(groups)) for num, den in SHARES)
    sent(0, 3 * groups)
    sent(2, 2 * line * groups)

    @pl.when(inner)
    def _():
        sent(1, 4 * groups - DIRECT)
        sent(3, mid_count)
        sent(4, groups - end_count)

    @pl.when(jnp.logical_not(inner))
    def _():
        sent(1, 2 * groups + DIRECT)
        sent(3, end_count)
        sent(4, groups - mid_count)


def on_device(noisy_clips, conv_first, conv_second, temporal):
    sections = lax.axis_size("segment")
    frames = lax.axis_size("frame")
    clips, frame_local, side, _, lanes = noisy_clips.shape
    half = lanes // 2
    cells = side * side
    if sections != 2 or half % 128 or frames != 16 or clips != 4 or frame_local != 1 or side % 16:
        return pipelined(noisy_clips, conv_first, conv_second, temporal)
    taps = conv_first.shape[1] + temporal.shape[1] + conv_second.shape[1]
    per_section = taps // temporal.shape[1]
    dma = pltpu.SemaphoreType.DMA
    vmem = pl.BlockSpec(memory_space=pltpu.VMEM)
    kind = jnp.bfloat16
    return pl.pallas_call(
        functools.partial(fused_kernel, frames),
        out_shape=pltpu.VMEM((clips, 1, side // 2, side, lanes), kind),
        in_specs=[pl.BlockSpec(memory_space=pl.ANY)] * 4,
        out_specs=vmem,
        scratch_shapes=[
            pltpu.VMEM((2 * taps, lanes, half), kind),
            pltpu.VMEM((clips, side, side, lanes), kind),
            pltpu.VMEM((3, clips, side + 2, side, lanes), kind),
            pltpu.VMEM((3, clips + 2, side + 2, side, lanes), kind),
            pltpu.VMEM((2, clips, cells, half), kind),
            pltpu.VMEM((2, clips, cells, half), kind),
            pltpu.VMEM((2, 2, cells, half), kind),
            pltpu.VMEM((2, 2, cells, half), kind),
            pltpu.VMEM((clips, cells, half), kind),
            pltpu.VMEM((clips, cells, half), kind),
            pltpu.VMEM((clips, cells, half), jnp.float32),
            pltpu.VMEM((2 * clips, side // 2, side, half), kind),
            dma((per_section,)),
            dma((5,)),
            dma((per_section + 1,)),
            dma((5, 2 * per_section)),
            dma((5,)),
            dma((3, clips)),
            dma((2, 3)),
            dma((2, clips)),
            dma((2,)),
        ],
        compiler_params=pltpu.CompilerParams(
            collective_id=0, has_side_effects=True, vmem_limit_bytes=58 * 1024 * 1024
        ),
    )(noisy_clips, conv_first, conv_second, temporal)


def solution(mesh):
    in_specs = (
        P(None, "frame", None, None, None),
        P("segment", None, "frame", None),
        P("segment", None, "frame", None),
        P("segment", None, "frame", None),
    )
    out_specs = P(None, "frame", "segment", None, None)
    return jax.shard_map(
        on_device, mesh=mesh, in_specs=in_specs, out_specs=out_specs, check_vma=False
    )
```

```python
import functools

import jax
import jax.numpy as jnp
from jax import lax
from jax.experimental import pallas as pl
from jax.experimental.pallas import tpu as pltpu
from jax.sharding import PartitionSpec as P

skip_scale = 0.7071067811865476
MESH = pl.DeviceIdType.MESH


def passed_along(shard, axis, by):
    length = lax.axis_size(axis)
    pairs = [(i, i + by) for i in range(length) if 0 <= i + by < length]
    return lax.ppermute(shard, axis, pairs)


def extended_2(cells, sides, width):
    for axis, dim in sides:
        count = lax.axis_size(axis)
        ends = count - 1
        head = lax.slice_in_dim(cells, 0, width, axis=dim)
        tail = lax.slice_in_dim(cells, cells.shape[dim] - width, cells.shape[dim], axis=dim)
        cells = jnp.concatenate(
            [
                lax.ppermute(tail, axis, [(i, (i + 1) % count) for i in range(ends)]),
                cells,
                lax.ppermute(head, axis, [((i + 1) % count, i) for i in range(ends)]),
            ],
            axis=dim,
        )
    return cells


def broadcast(shard, axis, root):
    mine = lax.axis_index(axis) == root
    return lax.psum(jnp.where(mine, shard, jnp.zeros_like(shard)), axis)


def spatial(field_in, kernel):
    extent = field_in.shape[1]
    channels = field_in.shape[3]
    padded = jnp.pad(field_in, ((0, 0), (1, 1), (1, 1), (0, 0)))
    accumulated = jnp.zeros((field_in.shape[0] * extent * extent, channels), jnp.float32)
    for row_shift in range(3):
        for col_shift in range(3):
            window = padded[
                :, row_shift : row_shift + extent, col_shift : col_shift + extent, :
            ].reshape(-1, channels)
            accumulated = accumulated + jnp.dot(
                window, kernel[3 * row_shift + col_shift], preferred_element_type=jnp.float32
            )
    return accumulated.reshape(field_in.shape)


def temporal_mix(extended, kernel, frame_local):
    channels = extended.shape[3]
    out_shape = (frame_local,) + extended.shape[1:]
    accumulated = jnp.zeros(out_shape, jnp.float32)
    for offset in range(3):
        window = extended[offset : offset + frame_local].reshape(-1, channels)
        accumulated = accumulated + jnp.dot(
            window, kernel[offset], preferred_element_type=jnp.float32
        ).reshape(out_shape)
    return accumulated


def pipelined(noisy_clips, conv_first, conv_second, temporal):
    sections = lax.axis_size("segment")
    segment_id = lax.axis_index("segment")
    first_full, second_full, time_full = (
        lax.all_gather(conv_first, "frame", axis=2, tiled=True),
        lax.all_gather(conv_second, "frame", axis=2, tiled=True),
        lax.all_gather(temporal, "frame", axis=2, tiled=True),
    )
    first_kernel = first_full[0]
    second_kernel = second_full[0]
    time_kernel = time_full[0]
    clip_count = noisy_clips.shape[0]
    frame_local = noisy_clips.shape[1]
    side_len = noisy_clips.shape[2]
    block_shape = noisy_clips.shape[1:]
    tick_count = clip_count + sections - 1
    half_sections = sections // 2
    is_up = segment_id >= half_sections
    store_depth = max(half_sections - 1, 1)
    side_store = jnp.zeros((store_depth,) + block_shape, jnp.bfloat16)
    out_store = jnp.zeros(noisy_clips.shape, jnp.bfloat16)
    prev_out = jnp.zeros(block_shape, jnp.bfloat16)

    def tick_step(carry, tick_index):
        prev_out, side_store, out_store = carry
        clip_now = tick_index - segment_id
        active = (clip_now >= 0) & (clip_now < clip_count)
        clip_slot = jnp.clip(clip_now, 0, clip_count - 1)
        own_input = lax.dynamic_index_in_dim(noisy_clips, clip_slot, 0, keepdims=False)
        received, side_store = passed_along((prev_out, side_store), "segment", 1)
        entering = jnp.where(segment_id == 0, own_input, received)
        written = (jnp.arange(store_depth) == segment_id - 1) & (segment_id < half_sections)
        side_store = jnp.where(written[:, None, None, None, None], entering[None], side_store)
        stack_slot = jnp.clip(sections - 2 - segment_id, 0, store_depth - 1)
        stored = lax.dynamic_index_in_dim(side_store, stack_slot, 0, keepdims=False)
        skip_feature = jnp.where(segment_id == sections - 1, own_input, stored)
        joined = (
            (entering.astype(jnp.float32) + skip_feature.astype(jnp.float32)) * skip_scale
        ).astype(jnp.bfloat16)
        section_in = jnp.where(is_up, joined, entering)
        activated = lax.cond(
            active,
            lambda: jax.nn.silu(spatial(section_in, first_kernel)).astype(jnp.bfloat16),
            lambda: jnp.zeros(block_shape, jnp.bfloat16),
        )
        extended = extended_2(activated, (("frame", 0),), 1)

        def second_pass():
            branch_sum = spatial(activated, second_kernel) + temporal_mix(
                extended, time_kernel, frame_local
            )
            return (section_in.astype(jnp.float32) + jax.nn.silu(branch_sum)).astype(jnp.bfloat16)

        section_out = lax.cond(active, second_pass, lambda: jnp.zeros(block_shape, jnp.bfloat16))
        finished = (jnp.arange(clip_count) == clip_slot) & active & (segment_id == sections - 1)
        out_store = jnp.where(finished[:, None, None, None, None], section_out[None], out_store)
        return ((section_out, side_store, out_store), None)

    final_carry, unused = lax.scan(
        tick_step, (prev_out, side_store, out_store), jnp.arange(tick_count, dtype=jnp.int32)
    )
    delivered = broadcast(final_carry[2], "segment", sections - 1)
    slab_rows = side_len // sections
    return lax.dynamic_slice_in_dim(delivered, segment_id * slab_rows, slab_rows, 2)


CODE, PACK, EVENTS = 16, 3, 127
ORDERS = (
    (
        131328, 6292483, 3149921, 1192209, 1323539, 3416115, 2236784, 409605,
        8402183, 4292944, 8594306, 541265, 5379364, 3544720, 3610513, 2462610,
        1575235, 4466259, 10500106, 3757232, 11641127, 1641285, 4629077, 2628108,
        12697686, 870185, 1784483, 1850306, 3982167, 5777992, 13647177, 9722141,
        9818411, 13781548, 5909910, 9950027, 10767451, 5070004, 10837472, 10936757,
        15786737, 14938791, 243,
    ),
    (
        24583, 155905, 266243, 3215664, 1208370, 1315635, 2176032, 336448,
        3493894, 8552832, 5325187, 541219, 1390390, 2396242, 9508630, 4428344,
        9648393, 10507032, 10596389, 4466353, 2597386, 10703897, 5573445, 2624582,
        3823130, 4663744, 3870145, 5708827, 13647042, 2802504, 13719613, 13773641,
        9722141, 2922133, 9950026, 10770989, 5983156, 5027237, 5103708, 14853857,
        11006301, 15983602, 240,
    ),
    (
        131328, 1073504, 2101507, 266800, 7352609, 1258018, 3351301, 3417108,
        8405312, 5276289, 8586833, 1378114, 3482962, 4428176, 3548818, 541843,
        595539, 1521447, 11575380, 4536360, 11641173, 2693190, 1653078, 723618,
        4694842, 5704898, 4729537, 5770688, 3877827, 1788186, 5886930, 3943574,
        13670172, 2987082, 5905725, 4953553, 5004198, 10871388, 5104053, 14726308,
        15902557, 15790563, 243,
    ),
    (
        24583, 155905, 1114896, 7352352, 2167300, 2233137, 1323525, 8401699,
        4261440, 8618625, 1397072, 4338724, 9458184, 9505091, 1455397, 9671191,
        3548966, 4462647, 11575379, 10572825, 3680433, 5612101, 2704906, 5677881,
        12782530, 12601100, 2802007, 1718797, 5785928, 3877842, 9853211, 9818396,
        1915948, 9752650, 5913901, 9915347, 10898523, 5104220, 6153127, 15905956,
        10875104, 14807989, 241,
    ),
)
DIRECT, SHARES = 0, ((1, 3), (1, 4))


def fused_kernel(
    frames,
    noisy_ref,
    first_ref,
    second_ref,
    time_ref,
    out_ref,
    w_ref,
    n_ref,
    xe,
    xa,
    a_send,
    a_recv,
    t_send,
    t_recv,
    e_mine,
    e_recv,
    acc_ref,
    o_full,
    local_sem,
    n_sem,
    y_sem,
    got_sem,
    sent_sem,
    a_sem,
    t_sem,
    e_sem,
    o_sem,
):
    clips, side, lanes = noisy_ref.shape[0], noisy_ref.shape[2], noisy_ref.shape[4]
    half = lanes // 2
    cells = side * side
    depth = first_ref.shape[2]
    width = time_ref.shape[1]
    rows_per_conv = first_ref.shape[1] // width
    per_section = 2 * rows_per_conv + 1
    taps = per_section * width
    groups = 2 * per_section
    line = frames // 4
    seg = lax.axis_index("segment")
    me = lax.axis_index("frame")
    slots = frames // line
    core, x_at, z_at, place = lax.rem(me, 2), lax.rem(me // 2, 2), me // slots, lax.rem(me, slots)
    peer = 1 - seg
    other = me + 1 - 2 * core
    slab_rows = side // 2

    def frame_of(x_place, z_place):
        return (z_place * 2 + x_place) * 2 + core

    x_peer = frame_of(1 - x_at, z_at)
    z_pair = z_at + 1 - 2 * lax.rem(z_at, 2)
    z_half = z_at // 2
    inner = lax.rem(z_at, 2) != z_half
    z_near, z_end = 2 - z_half, 3 - 3 * z_half
    far = (z_near, z_end)
    across = (x_peer, x_peer + 1 - 2 * core)

    barrier = pltpu.get_barrier_semaphore()
    near = [(seg, other)] + [(seg, f) for f in across]
    near += [(seg, frame_of(x_at, z)) for z in far + (z_pair,)]
    near += [(peer, f) for f in (me, other) + across]
    for target in near:
        pl.semaphore_signal(barrier, inc=1, device_id=target, device_id_type=MESH)

    def columns(which):
        return pl.ds(pl.multiple_of(which * half, half), half)

    def rows_of(owner):
        return pl.ds(pl.multiple_of(owner * depth, depth), depth)

    every = tuple(range(rows_per_conv))

    def part(j):
        if j < rows_per_conv:
            return first_ref, j * width
        if j == rows_per_conv:
            return time_ref, 0
        return second_ref, (j - rows_per_conv - 1) * width

    def local_copy(j):
        ref, start = part(j)
        return pltpu.make_async_copy(
            ref.at[0, pl.ds(start, width), :, columns(seg)],
            w_ref.at[pl.ds(seg * taps + j * width, width), rows_of(me)],
            local_sem.at[j],
        )

    def remote(src, dst, send, recv, device):
        return pltpu.make_async_remote_copy(
            src_ref=src,
            dst_ref=dst,
            send_sem=send,
            recv_sem=recv,
            device_id=device,
            device_id_type=MESH,
        )

    def take(ref, sem):
        pltpu.make_async_copy(ref, ref, sem).wait()

    def y_copy(j):
        ref, start = part(j)
        return remote(
            ref.at[0, pl.ds(start, width), :, columns(peer)],
            w_ref.at[pl.ds(seg * taps + j * width, width), rows_of(me)],
            y_sem.at[per_section],
            y_sem.at[j],
            (peer, me),
        )

    def slab(g, owner):
        return w_ref.at[pl.ds(g * width, width), rows_of(owner)]

    def some(g, count):
        return w_ref.at[pl.ds(g * width, width), pl.ds(0, count * depth)]

    own, crossed, lined, paired, rest = range(5)

    def give(g, owner, kind, link, target):
        ref = slab(g, owner)
        remote(ref, ref, sent_sem.at[link], got_sem.at[kind, g], (seg, target)).start()

    def give_core(g, owner):
        give(g, owner, own, 2, other)

    def round_own(g):
        section, j = g // per_section, lax.rem(g, per_section)

        @pl.when(seg == section)
        def _():
            take(slab(g, me), local_sem.at[j])

        @pl.when(seg != section)
        def _():
            take(slab(g, me), y_sem.at[j])

        give(g, me, crossed, 0, x_peer)
        give(g, me, lined, 1, frame_of(x_at, z_near))

        @pl.when(inner | (g < DIRECT))
        def _():
            give(g, me, lined, 1, frame_of(x_at, z_end))

        give(g, me, paired, 1, frame_of(x_at, z_pair))
        give_core(g, me)

    def crosses(g, is_inner):
        end, mid = (lax.rem(g, share[1]) < share[0] for share in SHARES)
        return jnp.where(is_inner, mid, end)

    def round_cross(g):
        take(some(g, 1), got_sem.at[crossed, g])

        @pl.when(crosses(g, inner))
        def _():
            give(g, x_peer, rest, 3, frame_of(x_at, z_pair))

        give_core(g, x_peer)

    def round_line(g):
        take(some(g, 2), got_sem.at[lined, g])

        @pl.when(inner & (g >= DIRECT))
        def _():
            give(g, frame_of(x_at, z_end), lined, 1, frame_of(x_at, z_pair))

        for z in far:
            give(g, frame_of(x_at, z), rest, 0, x_peer)
        for z in far:
            give_core(g, frame_of(x_at, z))

    def round_pair(g):
        take(some(g, 1), got_sem.at[paired, g])

        @pl.when(jnp.logical_not(crosses(g, jnp.logical_not(inner))))
        def _():
            give(g, frame_of(x_at, z_pair), rest, 4, x_peer)

        give_core(g, frame_of(x_at, z_pair))

    def round_rest(g):
        take(some(g, 3), got_sem.at[rest, g])
        for z in far + (z_pair,):
            give_core(g, frame_of(1 - x_at, z))

    def round_done(g):
        take(some(g, 2 * line), got_sem.at[own, g])

    def build(x, clip, value, where):
        width_of = value.shape[1]
        wide = value.astype(jnp.float32)
        place = lax.broadcasted_iota(jnp.int32, (cells, width_of), 0) % side
        shifted = (
            jnp.where(place == 0, 0.0, pltpu.roll(wide, 1, 0)).astype(jnp.bfloat16),
            value,
            jnp.where(place == side - 1, 0.0, pltpu.roll(wide, cells - 1, 0)).astype(jnp.bfloat16),
        )
        for dx in range(3):
            x[dx, clip, 1 : side + 1, :, where] = shifted[dx].reshape(side, side, width_of)

    def row_sum(x, clip, rows, base, total=None):
        for dy in rows:
            for dx in range(3):
                view = x[dx, clip, dy : dy + side].reshape(cells, lanes)
                term = jnp.dot(
                    view, w_ref[base + width * dy + dx], preferred_element_type=jnp.float32
                )
                total = term if total is None else total + term
        return total

    def silu(u):
        return u / (1.0 + jnp.exp(-u))

    def arrival(j):
        slot = jnp.where(j == 0, 0, jnp.where(j == 1, slots - 1, j - 1))
        slot = jnp.where(inner, slot, slots - 1 - j)
        return jnp.where(z_half == 0, slot, slots - 1 - slot)

    def noisy_local():
        return pltpu.make_async_copy(noisy_ref.at[place, 0], n_ref.at[place], n_sem.at[0])

    def send_noisy(part_at):
        @pl.when(part_at == 0)
        def _():
            remote(
                noisy_ref.at[lax.rem(other, slots), 0],
                n_ref.at[place],
                n_sem.at[4],
                n_sem.at[1],
                (seg, other),
            ).start()

        target = jnp.where(part_at == 0, across[0], across[1])
        remote(
            noisy_ref.at[lax.rem(target, slots), 0, :, :, columns(seg)],
            n_ref.at[place, :, :, columns(seg)],
            n_sem.at[4],
            n_sem.at[2],
            (seg, target),
        ).start()

    def relay_noisy(unused):
        take(n_ref.at[0], n_sem.at[2])
        for target in across:
            ref = n_ref.at[lax.rem(target, slots), :, :, columns(seg)]
            remote(ref, ref, n_sem.at[4], n_sem.at[3], (peer, me)).start()

    def build_noisy(j):
        @pl.when(j == 0)
        def _():
            for i in (0, 1, 3):
                take(n_ref.at[0], n_sem.at[i])

        slot = arrival(j)
        build(xe, slot, n_ref[slot].reshape(cells, lanes), slice(None))

    def a_copy(s, slot):
        return remote(
            a_send.at[s, slot], a_recv.at[s, slot], a_sem.at[2, 0], a_sem.at[s, slot], (peer, me)
        )

    def e_copy(slot):
        return remote(e_mine.at[slot], e_recv.at[slot], e_sem.at[1, 0], e_sem.at[0, slot], (peer, me))

    sends_on = (z_at < line - 1, z_at > 0)
    takes_on = (z_at > 0, z_at < line - 1)

    def t_copy(s, way):
        target = me + slots if way == 0 else me - slots
        return remote(
            t_send.at[way, s],
            t_recv.at[way, s],
            t_sem.at[way, 2],
            t_sem.at[way, s],
            (seg, lax.rem(target + frames, frames)),
        )

    def o_copy(slot, rows):
        return remote(
            o_full.at[2 * slot + rows],
            out_ref.at[place, 0, :, :, columns(seg)],
            o_sem.at[1],
            o_sem.at[0],
            (rows, z_at * slots + slot),
        )

    def first_rows(turn):
        s, slot = lax.div(turn, slots), arrival(lax.rem(turn, slots))
        total = row_sum(xe, slot, every, s * taps)
        a_send[s, slot] = silu(total).astype(jnp.bfloat16)
        a_copy(s, slot).start()

    def take_active(turn):
        s, slot = lax.div(turn, slots), arrival(lax.rem(turn, slots))
        a_copy(s, slot).wait_recv()
        build(xa, slot + 1, a_send[s, slot], columns(seg))
        build(xa, slot + 1, a_recv[s, slot], columns(peer))

    def mixed(s, slot, k):
        view = xa[1, slot + k, 1 : side + 1].reshape(cells, lanes)
        return jnp.dot(
            view, w_ref[s * taps + rows_per_conv * width + k], preferred_element_type=jnp.float32
        )

    def terms(turn):
        s, slot = lax.div(turn, slots), arrival(lax.rem(turn, slots))
        view = xa[1, slot + 1, 1 : side + 1].reshape(cells, lanes)
        base = s * taps + rows_per_conv * width
        for way, edge_slot in ((1, 0), (0, slots - 1)):

            @pl.when((slot == edge_slot) & sends_on[way])
            def _():
                t_send[way, s] = jnp.dot(
                    view, w_ref[base + 2 * way], preferred_element_type=jnp.float32
                ).astype(jnp.bfloat16)
                t_copy(s, way).start()

    def second_sum(s, slot, rows, with_time, total=None):
        base = s * taps + (rows_per_conv + 1) * width
        total = row_sum(xa, slot + 1, rows, base, total)
        if with_time:
            for k in range(width):
                total = total + mixed(s, slot, k)
        return total

    def early_rows(j):
        slot = arrival(j)
        acc_ref[slot] = second_sum(1, slot, every[:-1], False)

    def finished(s, slot):
        for way, edge_slot in ((0, 0), (1, slots - 1)):

            @pl.when(takes_on[way] & (slot == edge_slot))
            def _():
                t_copy(s, way).wait_recv()
                acc_ref[slot] = acc_ref[slot] + t_recv[way, s].astype(jnp.float32)

        return silu(acc_ref[slot])

    def end_first(j):
        slot = arrival(j)
        acc_ref[slot] = second_sum(0, slot, every, True)
        mine = n_ref[slot, :, :, columns(seg)].reshape(cells, half).astype(jnp.float32)
        out = (mine + finished(0, slot)).astype(jnp.bfloat16)
        e_mine[slot] = ((out.astype(jnp.float32) + mine) * skip_scale).astype(jnp.bfloat16)
        e_copy(slot).start()

    def take_entering(j):
        slot = arrival(j)
        e_copy(slot).wait_recv()
        build(xe, slot, e_mine[slot], columns(seg))
        build(xe, slot, e_recv[slot], columns(peer))

    def end_second(j):
        slot = arrival(j)
        acc_ref[slot] = second_sum(1, slot, every[-1:], True, acc_ref[slot])
        out = (e_mine[slot].astype(jnp.float32) + finished(1, slot)).astype(jnp.bfloat16)
        full = out.reshape(2, slab_rows, side, half)
        o_full[2 * slot + peer] = jnp.where(peer == 0, full[0], full[1])
        o_copy(slot, peer).start()
        o_full[2 * slot + seg] = jnp.where(seg == 0, full[0], full[1])

        @pl.when(slot != place)
        def _():
            o_copy(slot, seg).start()

        @pl.when(slot == place)
        def _():
            out_ref[place, 0, :, :, columns(seg)] = o_full[2 * slot + seg]

    works = (
        round_own,
        round_cross,
        round_line,
        round_pair,
        round_rest,
        round_done,
        send_noisy,
        relay_noisy,
        build_noisy,
        first_rows,
        take_active,
        terms,
        end_first,
        take_entering,
        early_rows,
        end_second,
    )

    words = []
    for codes in zip(*ORDERS):
        ends, inners = (jnp.where(seg == 0, codes[n], codes[n + 1]) for n in (0, 2))
        words.append(jnp.where(inner, inners, ends))

    def run(some_works, kind, turn, low=0):
        if len(some_works) == 1:
            some_works[0](turn)
            return
        cut = len(some_works) // 2

        @pl.when(kind < low + cut)
        def _():
            run(some_works[:cut], kind, turn, low)

        @pl.when(kind >= low + cut)
        def _():
            run(some_works[cut:], kind, turn, low + cut)

    for j in range(per_section):
        local_copy(j).start()

    noisy_local().start()
    edge = jnp.zeros((side, lanes), jnp.bfloat16)
    for x in (xe, xa):
        for dx in range(3):

            @pl.loop(0, x.shape[1])
            def _(slot):
                x[dx, slot, 0] = edge
                x[dx, slot, side + 1] = edge

    for slot in (0, slots + 1):
        xa[1, slot, 1 : side + 1] = jnp.zeros((side, side, lanes), jnp.bfloat16)

    pl.semaphore_wait(barrier, len(near))

    for j in range(per_section):
        y_copy(j).start()

    @pl.loop(0, EVENTS)
    def _(i):
        at, level = i // PACK, words
        while len(level) > 1:
            odd = lax.rem(at, 2) == 1
            level = [
                jnp.where(odd, level[n + 1], level[n]) if n + 1 < len(level) else level[n]
                for n in range(0, len(level), 2)
            ]
            at = at // 2
        code = level[0]
        for n in range(1, PACK):
            code = jnp.where(lax.rem(i, PACK) == n, level[0] // (CODE * CODE) ** n, code)
        code = lax.rem(code, CODE * CODE)
        run(works, code // CODE, lax.rem(code, CODE))

    for i in range(2):
        take(o_full.at[pl.ds(0, 2 * slots - 1)], o_sem.at[i])
    take(n_ref.at[pl.ds(0, 3)], n_sem.at[4])
    take(e_mine, e_sem.at[1, 0])
    take(a_send, a_sem.at[2, 0])
    for way in range(2):

        @pl.when(sends_on[way])
        def _():
            take(t_send.at[way], t_sem.at[way, 2])

    take(w_ref.at[pl.ds(0, taps), pl.ds(0, depth)], y_sem.at[per_section])
    def sent(link, count):
        rows = count * width * depth
        fits = [k for k in range(1, 2 * taps + 1) if rows % (16 * k) == 0 and rows // k <= lanes]
        take(w_ref.at[pl.ds(0, fits[0]), pl.ds(0, rows // fits[0])], sent_sem.at[link])

    end_count, mid_count = (sum(g % den < num for g in range(groups)) for num, den in SHARES)
    sent(0, 3 * groups)
    sent(2, 2 * line * groups)

    @pl.when(inner)
    def _():
        sent(1, 4 * groups - DIRECT)
        sent(3, mid_count)
        sent(4, groups - end_count)

    @pl.when(jnp.logical_not(inner))
    def _():
        sent(1, 2 * groups + DIRECT)
        sent(3, end_count)
        sent(4, groups - mid_count)


def on_device(noisy_clips, conv_first, conv_second, temporal):
    sections = lax.axis_size("segment")
    frames = lax.axis_size("frame")
    clips, frame_local, side, _, lanes = noisy_clips.shape
    half = lanes // 2
    cells = side * side
    if sections != 2 or half % 128 or frames != 16 or clips != 4 or frame_local != 1 or side % 16:
        return pipelined(noisy_clips, conv_first, conv_second, temporal)
    taps = conv_first.shape[1] + temporal.shape[1] + conv_second.shape[1]
    per_section = taps // temporal.shape[1]
    dma = pltpu.SemaphoreType.DMA
    vmem = pl.BlockSpec(memory_space=pltpu.VMEM)
    kind = jnp.bfloat16
    return pl.pallas_call(
        functools.partial(fused_kernel, frames),
        out_shape=pltpu.VMEM((clips, 1, side // 2, side, lanes), kind),
        in_specs=[pl.BlockSpec(memory_space=pl.ANY)] * 4,
        out_specs=vmem,
        scratch_shapes=[
            pltpu.VMEM((2 * taps, lanes, half), kind),
            pltpu.VMEM((clips, side, side, lanes), kind),
            pltpu.VMEM((3, clips, side + 2, side, lanes), kind),
            pltpu.VMEM((3, clips + 2, side + 2, side, lanes), kind),
            pltpu.VMEM((2, clips, cells, half), kind),
            pltpu.VMEM((2, clips, cells, half), kind),
            pltpu.VMEM((2, 2, cells, half), kind),
            pltpu.VMEM((2, 2, cells, half), kind),
            pltpu.VMEM((clips, cells, half), kind),
            pltpu.VMEM((clips, cells, half), kind),
            pltpu.VMEM((clips, cells, half), jnp.float32),
            pltpu.VMEM((2 * clips, side // 2, side, half), kind),
            dma((per_section,)),
            dma((5,)),
            dma((per_section + 1,)),
            dma((5, 2 * per_section)),
            dma((5,)),
            dma((3, clips)),
            dma((2, 3)),
            dma((2, clips)),
            dma((2,)),
        ],
        compiler_params=pltpu.CompilerParams(
            collective_id=0, has_side_effects=True, vmem_limit_bytes=58 * 1024 * 1024
        ),
    )(noisy_clips, conv_first, conv_second, temporal)


def solution(mesh):
    in_specs = (
        P(None, "frame", None, None, None),
        P("segment", None, "frame", None),
        P("segment", None, "frame", None),
        P("segment", None, "frame", None),
    )
    out_specs = P(None, "frame", "segment", None, None)
    return jax.shard_map(
        on_device, mesh=mesh, in_specs=in_specs, out_specs=out_specs, check_vma=False
    )
```
